32 devices in a mesh: ctx: 16 (over z, y, core), fsdp: 2 (over x).
Axes of the slice: x: 2, y: 2, z: 4, core: 2. Of those that a mesh axis runs over, the one named last changes fastest.
Arguments:
- tokens: bfloat16 [2, 2, 8192, 768], P(None, 'fsdp', 'ctx'), may hold values from -6 to 6
- cotangent: bfloat16 [2, 2, 8192, 768], P(None, 'fsdp', 'ctx'), may hold values from -6 to 6
- doc_lengths: int32 [2, 2, 8], P(None, 'fsdp'), may hold values from 1 to 4096, 8192 in all within a row
- gain_attn: bfloat16 [768], P('fsdp'), may hold values from 0.25 to 1.75
- w_query: bfloat16 [768, 768], P('fsdp'), may hold values from -0.21875 to 0.21875
- w_key: bfloat16 [768, 768], P('fsdp'), may hold values from -0.21875 to 0.21875
- w_value: bfloat16 [768, 768], P('fsdp'), may hold values from -0.21875 to 0.21875
- w_out: bfloat16 [768, 768], P('fsdp'), may hold values from -2.5 to 2.5
- gain_mlp: bfloat16 [768], P('fsdp'), may hold values from 0.25 to 1.75
- w_gate: bfloat16 [768, 2048], P('fsdp'), may hold values from -0.21875 to 0.21875
- w_up: bfloat16 [768, 2048], P('fsdp'), may hold values from -0.21875 to 0.21875
- w_down: bfloat16 [2048, 768], P('fsdp'), may hold values from -0.125 to 0.125
Outputs:
- output: bfloat16 [2, 2, 8192, 768], P(None, 'fsdp', 'ctx')
- grad_tokens: bfloat16 [2, 2, 8192, 768], P(None, 'fsdp', 'ctx')
- grad_gain_attn: float32 [768], P('fsdp')
- grad_w_query: float32 [768, 768], P('fsdp')
- grad_w_key: float32 [768, 768], P('fsdp')
- grad_w_value: float32 [768, 768], P('fsdp')
- grad_w_out: float32 [768, 768], P('fsdp')
- grad_gain_mlp: float32 [768], P('fsdp')
- grad_w_gate: float32 [768, 2048], P('fsdp')
- grad_w_up: float32 [768, 2048], P('fsdp')
- grad_w_down: float32 [2048, 768], P('fsdp')
The draws below stay inside these ranges and needn't reach their ends.
Inputs may be any that keep to these rules, and one draw needn't show every extreme that they name: `doc_lengths`: each row holds the lengths of the 8 documents of one stream, summing to 8192; the longest is exactly 4096.
All inputs are finite; a program needn't handle non-finite values.
Results may differ from the reference program's by a relative error of at most 0.024.
Values may be sent and summed in bfloat16 or wider, within the bound.
A program may use at most 88 MiB of HBM per device.

```python
import math
import jax
import jax.numpy as jnp
import numpy as np
from jax import lax

D = 768
HEAD_DIM = 64
FF = 2048
MICRO = 2
DOC_MAX = 4096
SEG = 8192
STREAMS = 2
NDOC = 8


def shard_levels(rng, shape, cuts, low, high):
    factor_of = 1.0
    for position, shards_of in cuts:
        heights = jax.random.uniform(jax.random.fold_in(jax.random.fold_in(rng, 6), position), (shards_of,), jnp.float32, low / len(cuts), high / len(cuts))
        factor_of = factor_of * jnp.repeat(jnp.exp(heights), shape[position] // shards_of).reshape((-1,) + (1,) * (len(shape) - 1 - position))
    return factor_of


def profile(count, total, most, slope):
    loads = [(1 << 20) // math.isqrt(rank ** slope) + 1 for rank in range(2, count + 1)]
    spare, holding = total - most - (count - 1), [1] * (count - 1)
    while spare > 0:
        free = [i for i in range(count - 1) if holding[i] < most]
        whole, remaining = sum([loads[i] for i in free]), spare
        for i in free:
            addition = min(most - holding[i], max(1, remaining * loads[i] // whole), spare)
            holding[i] = holding[i] + addition
            spare = spare - addition
    return np.array([most] + holding)


def uneven_parts(own_key, number_of, total, limit, skew):
    if number_of == 2:
        one = jax.random.randint(own_key, (), max(1, total - limit), min(limit, total - 1) + 1)
        return jnp.stack([one, total - one])
    tallies = jnp.asarray(profile(number_of, total, limit, skew), jnp.int32)
    couples = (number_of - 1) // 2
    giver, receiver = tallies[1:1 + 2 * couples:2], tallies[2:2 + 2 * couples:2]
    margin = jnp.minimum(giver - 1, limit - receiver)
    moved = jax.random.randint(jax.random.fold_in(own_key, 1), (couples,), 0, 1 << 20) % (margin + 1)
    tallies = tallies.at[1:1 + 2 * couples:2].set(giver - moved).at[2:2 + 2 * couples:2].set(receiver + moved)
    return tallies[jax.random.permutation(jax.random.fold_in(own_key, 2), number_of)]


def bell_draw(own_key, dims, scale, reach, pieces=(), kind=jnp.bfloat16):
    values = jax.random.normal(own_key, dims, jnp.float32) * scale
    if len(pieces) > 0:
        values = shard_levels(own_key, dims, pieces, -0.22, 0.18) * values
    return jnp.clip(values, min=-reach, max=reach).astype(kind)


def setup_inputs(seed: int = 0) -> dict:
    splits = jax.random.split(jax.random.key(seed), 13)
    tokens = bell_draw(splits[0], (MICRO, STREAMS, SEG, D), 1.0, 6.0, ((1, 2), (2, 16)))
    cotangent = bell_draw(splits[1], (MICRO, STREAMS, SEG, D), 1.0, 6.0, ((1, 2), (2, 16)))
    doc_lengths = jax.vmap(lambda own: uneven_parts(own, NDOC, SEG, DOC_MAX, 2))(jax.random.split(splits[2], MICRO * STREAMS)).reshape((MICRO, STREAMS, NDOC)).astype(jnp.int32)
    gain_attn = jnp.clip(1.0 + 0.15 * jax.random.normal(splits[3], (D,), jnp.float32), 0.25, 1.75).astype(jnp.bfloat16)
    w_query = bell_draw(splits[4], (D, D), D ** -0.5, 0.21875, ((0, 2),))
    w_key = bell_draw(splits[5], (D, D), D ** -0.5, 0.21875, ((0, 2),))
    w_value = bell_draw(splits[6], (D, D), D ** -0.5, 0.21875, ((0, 2),))
    w_out = bell_draw(splits[7], (D, D), (max(D // 128, 1)) ** -0.5, 2.5, ((0, 2),))
    gain_mlp = jnp.clip(1.0 + 0.15 * jax.random.normal(splits[8], (D,), jnp.float32), 0.25, 1.75).astype(jnp.bfloat16)
    w_gate = bell_draw(splits[9], (D, FF), D ** -0.5, 0.21875, ((0, 2),))
    w_up = bell_draw(splits[10], (D, FF), D ** -0.5, 0.21875, ((0, 2),))
    w_down = bell_draw(splits[11], (FF, D), FF ** -0.5, 0.125, ((0, 2),))
    return {"tokens": tokens, "cotangent": cotangent, "doc_lengths": doc_lengths, "gain_attn": gain_attn, "w_query": w_query, "w_key": w_key, "w_value": w_value, "w_out": w_out, "gain_mlp": gain_mlp, "w_gate": w_gate, "w_up": w_up, "w_down": w_down}


EPS = 1e-05
NEG = -1e+30

@jax.custom_vjp
def low(v):
    return lax.optimization_barrier(v.astype(jnp.bfloat16)).astype(jnp.float32)

@jax.custom_vjp
def low_back(v):
    return v

def low_keep(v):
    return (low(v), None)

def low_pass(kept, grad):
    return (grad,)

def back_keep(v):
    return (v, None)

def back_low(kept, grad):
    return (low(grad),)
low.defvjp(low_keep, low_pass)
low_back.defvjp(back_keep, back_low)

def highest(left, right):
    return jnp.dot(left, right, precision=lax.Precision.HIGHEST, preferred_element_type=jnp.float32)

def norm_rows(values, gain):
    return values * lax.rsqrt(lax.optimization_barrier(jnp.mean(values * values, -1, keepdims=True)) + EPS) * gain

def rotary_tables(offsets):
    half_dim = HEAD_DIM // 2
    inverse = jnp.power(10000.0, -jnp.arange(half_dim, dtype=jnp.float32) / half_dim)
    angles = offsets.astype(jnp.float32)[:, None] * inverse[None, :]
    cos_table = jnp.cos(angles)
    sine_table = jnp.sin(angles)
    return (jnp.concatenate([cos_table, cos_table], -1)[:, None, :], jnp.concatenate([sine_table, sine_table], -1)[:, None, :])

def rotate(values, cos_table, sine_table):
    half_dim = values.shape[-1] // 2
    turned = jnp.concatenate([-values[..., half_dim:], values[..., :half_dim]], -1)
    return values * cos_table + turned * sine_table

def stream_forward(tokens, begins, gain_attn, w_query, w_key, w_value, w_out, gain_mlp, w_gate, w_up, w_down):
    seg_len = tokens.shape[0]
    head_count = D // HEAD_DIM
    positions = jnp.arange(seg_len, dtype=jnp.int32)
    cos_table, sine_table = rotary_tables(positions - begins)
    normed = low(norm_rows(tokens, gain_attn))

    def project(weight):
        return highest(normed, weight).reshape(seg_len, head_count, HEAD_DIM)
    queries = low(rotate(low_back(project(w_query)), cos_table, sine_table))
    key_vecs = low(rotate(low_back(project(w_key)), cos_table, sine_table))
    values = low(low_back(project(w_value)))
    block_rows = math.gcd(seg_len, 512)
    window = block_rows + DOC_MAX
    padding = jnp.zeros((DOC_MAX, head_count, HEAD_DIM), jnp.float32)
    key_padded = jnp.concatenate([padding, key_vecs], 0)
    value_padded = jnp.concatenate([padding, values], 0)
    score_scale = HEAD_DIM ** (-0.5)

    def attend(block_index):
        first_row = (block_index * block_rows).astype(jnp.int32)
        query_block = lax.dynamic_slice_in_dim(queries, first_row, block_rows, 0)
        key_window = lax.dynamic_slice_in_dim(key_padded, first_row, window, 0)
        value_window = lax.dynamic_slice_in_dim(value_padded, first_row, window, 0)
        query_pos = first_row + jnp.arange(block_rows, dtype=jnp.int32)
        query_begin = lax.dynamic_slice_in_dim(begins, first_row, block_rows, 0)
        key_pos = first_row - DOC_MAX + jnp.arange(window, dtype=jnp.int32)
        raw_scores = jnp.einsum('qhd,khd->hqk', query_block, key_window, precision=lax.Precision.HIGHEST, preferred_element_type=jnp.float32) * score_scale
        scores = low_back(raw_scores)
        key_valid = (key_pos[None, :] >= query_begin[:, None]) & (key_pos[None, :] <= query_pos[:, None])
        scores = jnp.where(key_valid[None], scores, NEG)
        peak = lax.optimization_barrier(jnp.max(scores, -1, keepdims=True))
        log_totals = peak + jnp.log(lax.optimization_barrier(jnp.sum(jnp.exp(scores - peak), -1, keepdims=True)))
        weights_soft = low(jnp.exp(scores - log_totals))
        return jnp.einsum('hqk,khd->qhd', weights_soft, value_window, precision=lax.Precision.HIGHEST, preferred_element_type=jnp.float32)
    attended = lax.map(jax.checkpoint(attend), jnp.arange(seg_len // block_rows, dtype=jnp.int32))
    attended = low(low_back(attended.reshape(seg_len, D)))
    middle = tokens + low_back(highest(attended, w_out))
    normed_mlp = low(norm_rows(middle, gain_mlp))
    gate_pre = low_back(highest(normed_mlp, w_gate))
    up_pre = low_back(highest(normed_mlp, w_up))
    hidden = low(jax.nn.silu(gate_pre) * up_pre)
    return middle + low_back(highest(hidden, w_down))

def reference(tokens, cotangent, doc_lengths, gain_attn, w_query, w_key, w_value, w_out, gain_mlp, w_gate, w_up, w_down):
    weights = tuple((weight.astype(jnp.float32) for weight in (gain_attn, w_query, w_key, w_value, w_out, gain_mlp, w_gate, w_up, w_down)))
    seg_len = tokens.shape[2]
    flat_tokens = tokens.reshape(-1, seg_len, D).astype(jnp.float32)
    flat_cot = cotangent.reshape(-1, seg_len, D).astype(jnp.float32)
    flat_lengths = doc_lengths.reshape(-1, doc_lengths.shape[-1]).astype(jnp.int32)
    positions = jnp.arange(seg_len, dtype=jnp.int32)

    def one_stream(grad_sums, stream_data):
        stream_tokens, stream_cot, lengths = stream_data
        doc_ends = jnp.cumsum(lengths).astype(jnp.int32)
        doc_begins = doc_ends - lengths
        inside = (positions[:, None] >= doc_begins[None, :]) & (positions[:, None] < doc_ends[None, :])
        begins = lax.optimization_barrier(jnp.sum(jnp.where(inside, doc_begins[None, :], 0), -1)).astype(jnp.int32)

        def forward(stream_in, *weight_list):
            return stream_forward(stream_in, begins, *weight_list)
        result, pullback = jax.vjp(forward, stream_tokens, *weights)
        grads = pullback(stream_cot)
        new_sums = tuple((total + grad for total, grad in zip(grad_sums, grads[1:])))
        return (new_sums, (result, grads[0]))
    start_sums = tuple((jnp.zeros_like(weight) for weight in weights))
    grad_sums, (results, grad_inputs) = lax.scan(one_stream, start_sums, (flat_tokens, flat_cot, flat_lengths))
    return (results.reshape(tokens.shape).astype(jnp.bfloat16), grad_inputs.reshape(tokens.shape).astype(jnp.bfloat16), grad_sums[0], grad_sums[1], grad_sums[2], grad_sums[3], grad_sums[4], grad_sums[5], grad_sums[6], grad_sums[7], grad_sums[8])
```

```python
import functools
import math

import jax
import jax.numpy as jnp
from jax import lax
from jax.experimental import pallas as pl
from jax.experimental.pallas import tpu as pltpu
from jax.sharding import PartitionSpec as P

HEAD_DIM = 64
LANES = 128
EPS = 1e-05
NEG = -1e30
LOG2E = math.log2(math.e)
LN2 = math.log(2.0)
F32 = jnp.float32
BF16 = jnp.bfloat16


def dot_nt(left, right):
    return lax.dot_general(left, right, (((1,), (1,)), ((), ())), preferred_element_type=F32)


def dot_nn(left, right):
    return lax.dot_general(left, right, (((1,), (0,)), ((), ())), preferred_element_type=F32)


def dot_tn(left, right):
    return lax.dot_general(left, right, (((0,), (0,)), ((), ())), preferred_element_type=F32)


def lane_index(rows):
    return lax.broadcasted_iota(jnp.int32, (rows, LANES), 1)


def flip(tile):
    return pltpu.roll(tile, HEAD_DIM, 1)


def params(count):
    return pltpu.CompilerParams(
        dimension_semantics=("arbitrary",) * count, vmem_limit_bytes=60 * 1024 * 1024
    )


def full_block(shape):
    zeros = (0,) * len(shape)
    return pl.BlockSpec(shape, lambda *_: zeros)


def pack_pair(tile):
    count = tile.shape[0] // 2
    low = lane_index(count) < HEAD_DIM
    top, bottom = tile[:count], tile[count:]
    return (jnp.where(low, top, flip(bottom)), jnp.where(low, flip(top), bottom))


def unpack_pair(first, second):
    low = lane_index(first.shape[0]) < HEAD_DIM
    top = jnp.where(low, first, flip(second))
    bottom = jnp.where(low, flip(first), second)
    return jnp.concatenate([top, bottom], 0)


def turn(tile):
    near = (lane_index(tile.shape[0]) % HEAD_DIM) < HEAD_DIM // 2
    return jnp.where(
        near, pltpu.roll(tile, LANES - HEAD_DIM // 2, 1), pltpu.roll(tile, HEAD_DIM // 2, 1)
    )


def project_kernel(pieces, x_ref, g_ref, c_ref, s_ref, wq_ref, wk_ref, wv_ref, n_ref, *outs):
    x = x_ref[...].astype(F32)
    recip = lax.rsqrt(jnp.mean(x * x, -1, keepdims=True) + EPS)
    normed = (x * recip * g_ref[...].astype(F32)).astype(BF16)
    n_ref[...] = normed
    queries = dot_nn(normed, wq_ref[...])
    key_vecs = dot_nn(normed, wk_ref[...])
    values = dot_nn(normed, wv_ref[...])
    cos_table, sine_table = c_ref[...], s_ref[...]
    rows = x.shape[0]
    low = lane_index(rows) < HEAD_DIM
    place = {}
    for out_index, (first, count) in enumerate(pieces):
        for unit in range(first, first + count):
            place[unit] = (out_index, unit - first)
    for pair in range(x.shape[1] // LANES):
        cut = slice(pair * LANES, (pair + 1) * LANES)
        q2, k2, v2 = queries[:, cut], key_vecs[:, cut], values[:, cut]
        q2 = (q2 * cos_table + turn(q2) * sine_table) * (LOG2E * HEAD_DIM**-0.5)
        k2 = k2 * cos_table + turn(k2) * sine_table
        packed = pack_pair(q2)
        kv = (jnp.where(low, k2, flip(v2)), jnp.where(low, flip(k2), v2))
        for side in range(2):
            out_index, spot = place[2 * pair + side]
            outs[out_index][spot, 0, :rows, :] = kv[side].astype(BF16)
            outs[out_index][spot, 0, rows:, :] = packed[side].astype(BF16)


def project(pieces, tokens, gain, cos_table, sine_table, w_query, w_key, w_value):
    rows, width = tokens.shape
    half = rows // 2
    depth = half + half // 2
    return pl.pallas_call(
        functools.partial(project_kernel, pieces),
        grid=(2,),
        in_specs=[
            pl.BlockSpec((half, width), lambda i: (i, 0)),
            full_block((1, width)),
            pl.BlockSpec((half, LANES), lambda i: (i, 0)),
            pl.BlockSpec((half, LANES), lambda i: (i, 0)),
            full_block((width, width)),
            full_block((width, width)),
            full_block((width, width)),
        ],
        out_specs=[pl.BlockSpec((half, width), lambda i: (i, 0))]
        + [pl.BlockSpec((count, 1, depth, LANES), lambda i: (0, i, 0, 0)) for _, count in pieces],
        out_shape=[jax.ShapeDtypeStruct((rows, width), BF16)]
        + [jax.ShapeDtypeStruct((count, 2, depth, LANES), BF16) for _, count in pieces],
        compiler_params=params(1),
        cost_estimate=pl.CostEstimate(
            flops=6 * rows * width * width, bytes_accessed=12 * width * width, transcendentals=0
        ),
        name="project",
    )(tokens, gain, cos_table, sine_table, w_query, w_key, w_value)


def row_begins(starts_ref, positions):
    begins = jnp.zeros_like(positions)
    for index in range(starts_ref.shape[0]):
        start = starts_ref[index]
        begins = jnp.maximum(begins, jnp.where(positions >= start, start, 0))
    return begins


def unpack_one(packed, lanes_low):
    wide = packed.astype(F32)
    low = lane_index(wide.shape[0]) < HEAD_DIM
    keep = low if lanes_low else jnp.logical_not(low)
    turned = flip(wide)
    first, second = (wide, turned) if lanes_low else (turned, wide)
    return jnp.concatenate(
        [jnp.where(keep, first, 0.0), jnp.where(keep, second, 0.0)], 0
    ).astype(BF16)


def attend_kernel(info, starts, mine, other, o_ref, lse_ref):
    block = pl.program_id(0)
    core = info[0]
    lowest, inner = info[1 + 2 * block], info[2 + 2 * block]
    rows = mine.shape[1] * 2 // 3
    low = lane_index(rows) < HEAD_DIM
    queries = unpack_one(mine[block, rows:, :], True)
    row_pos = (2 * block + core) * rows + lax.broadcasted_iota(jnp.int32, (rows, 1), 0)
    begins = row_begins(starts, row_pos)
    lane_low = lane_index(2 * rows) < HEAD_DIM
    column = lax.broadcasted_iota(jnp.int32, (1, 2 * rows), 1)
    offsets = jnp.where(column < rows, column + core * rows, column - core * rows)

    def step(masked, index, carry):
        peak, acc = carry
        kv = jnp.concatenate([mine[index, :rows, :], other[index, :rows, :]], 0)
        ones_v = jnp.where(lane_low, jnp.ones_like(kv), kv)
        scores = dot_nt(queries, kv)
        if masked:
            key_pos = offsets + index * (2 * rows)
            scores = jnp.where((key_pos >= begins) & (key_pos <= row_pos), scores, NEG)
        new_peak = jnp.maximum(peak, jnp.max(scores, -1, keepdims=True))
        weights = jnp.exp2(scores - new_peak)
        acc = acc * jnp.exp2(peak - new_peak) + dot_nn(weights.astype(BF16), ones_v)
        return (new_peak, acc)

    carry = step(True, block, (jnp.full((rows, 1), NEG, F32), jnp.zeros((rows, LANES), F32)))
    carry = lax.fori_loop(lowest, inner, functools.partial(step, True), carry)
    peak, acc = lax.fori_loop(inner, block, functools.partial(step, False), carry)
    result = acc / flip(acc)
    count = rows // 2
    small_low = lane_index(count) < HEAD_DIM
    o_ref[0] = jnp.where(small_low, flip(result[:count]), result[count:]).astype(BF16)
    lse = jnp.where(low, peak + jnp.log2(acc), 0.0)
    lse_ref[0] = jnp.transpose(lse)[0:1, :]


def attend(info, starts, mine, other):
    blocks, depth, _ = mine.shape
    rows = depth * 2 // 3
    return pl.pallas_call(
        attend_kernel,
        grid_spec=pltpu.PrefetchScalarGridSpec(
            num_scalar_prefetch=2,
            grid=(blocks,),
            in_specs=[
                pl.BlockSpec(mine.shape, lambda i, *_: (0, 0, 0)),
                pl.BlockSpec(other.shape, lambda i, *_: (0, 0, 0)),
            ],
            out_specs=[
                pl.BlockSpec((1, rows // 2, LANES), lambda i, *_: (i, 0, 0)),
                pl.BlockSpec((1, 1, rows), lambda i, *_: (i, 0, 0)),
            ],
        ),
        out_shape=[
            jax.ShapeDtypeStruct((blocks, rows // 2, LANES), BF16),
            jax.ShapeDtypeStruct((blocks, 1, rows), F32),
        ],
        compiler_params=params(1),
        cost_estimate=pl.CostEstimate(
            flops=16 * 10**9, bytes_accessed=10**7, transcendentals=10**7
        ),
        name="attend",
    )(info, starts, mine, other)


def attend_grad_kernel(
    info, starts, mine, other, do_ref, o_ref, lse_ref, dm_ref, dp_ref, acc_mine, acc_other
):
    block = pl.program_id(0)
    core = info[0]
    lowest, inner = info[1 + 2 * block], info[2 + 2 * block]
    rows = mine.shape[1] * 2 // 3
    count = rows // 2

    @pl.when(block == 0)
    def _():
        acc_mine[...] = jnp.zeros_like(acc_mine)
        acc_other[...] = jnp.zeros_like(acc_other)

    queries = unpack_one(mine[block, rows:, :], True)
    grad_out = unpack_one(do_ref[0], False)
    both = jnp.concatenate([queries, grad_out], 0)
    product = jnp.transpose(do_ref[0].astype(F32) * o_ref[0].astype(F32))
    delta = jnp.concatenate(
        [
            jnp.sum(product[:HEAD_DIM], 0, keepdims=True),
            jnp.sum(product[HEAD_DIM:], 0, keepdims=True),
        ],
        1,
    )
    lse = lse_ref[0]
    row_pos = (2 * block + core) * rows + lax.broadcasted_iota(jnp.int32, (1, rows), 1)
    begins = row_begins(starts, row_pos)
    line = lax.broadcasted_iota(jnp.int32, (2 * rows, 1), 0)
    offsets = jnp.where(line < rows, line + core * rows, line - core * rows)

    def step(masked, index, grad_q):
        kv = jnp.concatenate([mine[index, :rows, :], other[index, :rows, :]], 0)
        scores = dot_nt(kv, queries)
        weights = jnp.exp2(scores - lse)
        if masked:
            key_pos = offsets + index * (2 * rows)
            weights = jnp.where((key_pos >= begins) & (key_pos <= row_pos), weights, 0.0)
        grad_weights = dot_nt(kv, grad_out)
        grad_scores = (weights * (grad_weights - delta)).astype(BF16)
        grad_kv = dot_nn(jnp.concatenate([grad_scores, weights.astype(BF16)], 1), both)
        acc_mine[index] += grad_kv[:rows]
        acc_other[index] += grad_kv[rows:]
        return grad_q + dot_tn(grad_scores, kv)

    grad_q = step(True, block, jnp.zeros((rows, LANES), F32))
    grad_q = lax.fori_loop(lowest, inner, functools.partial(step, True), grad_q)
    grad_q = lax.fori_loop(inner, block, functools.partial(step, False), grad_q)
    grad_q = grad_q * HEAD_DIM**-0.5
    small_low = lane_index(count) < HEAD_DIM
    dm_ref[block, rows:, :] = jnp.where(small_low, grad_q[:count], flip(grad_q[count:])).astype(
        BF16
    )

    @pl.when(block == pl.num_programs(0) - 1)
    def _():
        scale = jnp.where(lane_index(rows) < HEAD_DIM, LN2, 1.0)

        def flush(index, _):
            dm_ref[index, :rows, :] = (acc_mine[index] * scale).astype(BF16)
            dp_ref[index] = (acc_other[index] * scale).astype(BF16)
            return 0

        lax.fori_loop(0, mine.shape[0], flush, 0)


def attend_grad(info, starts, mine, other, grad_out, out, lse):
    blocks, depth, _ = mine.shape
    rows = depth * 2 // 3
    whole = pl.BlockSpec(mine.shape, lambda i, *_: (0, 0, 0))
    small = pl.BlockSpec((1, rows // 2, LANES), lambda i, *_: (i, 0, 0))
    return pl.pallas_call(
        attend_grad_kernel,
        grid_spec=pltpu.PrefetchScalarGridSpec(
            num_scalar_prefetch=2,
            grid=(blocks,),
            in_specs=[
                whole,
                whole,
                small,
                small,
                pl.BlockSpec((1, 1, rows), lambda i, *_: (i, 0, 0)),
            ],
            out_specs=[whole, pl.BlockSpec((blocks, rows, LANES), lambda i, *_: (0, 0, 0))],
            scratch_shapes=[
                pltpu.VMEM((blocks, rows, LANES), F32),
                pltpu.VMEM((blocks, rows, LANES), F32),
            ],
        ),
        out_shape=[
            jax.ShapeDtypeStruct(mine.shape, BF16),
            jax.ShapeDtypeStruct((blocks, rows, LANES), BF16),
        ],
        compiler_params=params(1),
        cost_estimate=pl.CostEstimate(
            flops=32 * 10**9, bytes_accessed=10**7, transcendentals=10**7
        ),
        name="attend_grad",
    )(info, starts, mine, other, grad_out, out, lse)


def collect_kernel(spots, *refs):
    ins, out = refs[:-1], refs[-1]
    for pair in range(len(spots) // 2):
        tiles = []
        for side in range(2):
            array, spot = spots[2 * pair + side]
            tiles.append(ins[array][spot, 0].astype(F32))
        out[:, pair * LANES : (pair + 1) * LANES] = unpack_pair(*tiles).astype(BF16)


def collect(spots, arrays):
    units, _, count, _ = arrays[0].shape
    width = len(spots) * HEAD_DIM
    return pl.pallas_call(
        functools.partial(collect_kernel, spots),
        grid=(2,),
        in_specs=[
            pl.BlockSpec((units, 1, count, LANES), lambda i: (0, i, 0, 0)) for _ in arrays
        ],
        out_specs=pl.BlockSpec((2 * count, width), lambda i: (i, 0)),
        out_shape=jax.ShapeDtypeStruct((4 * count, width), BF16),
        compiler_params=params(1),
        cost_estimate=pl.CostEstimate(flops=0, bytes_accessed=2 * 10**6, transcendentals=0),
        name="collect",
    )(*arrays)


def spread_kernel(pieces, x_ref, *outs):
    place = {}
    for out_index, (first, count) in enumerate(pieces):
        for unit in range(first, first + count):
            place[unit] = (out_index, unit - first)
    for pair in range(x_ref.shape[1] // LANES):
        tile = x_ref[:, pair * LANES : (pair + 1) * LANES].astype(F32)
        packed = pack_pair(tile)
        for side in range(2):
            out_index, spot = place[2 * pair + side]
            outs[out_index][spot, 0] = packed[side].astype(BF16)


def spread(pieces, rows_array):
    rows, width = rows_array.shape
    half = rows // 2
    count = half // 2
    return pl.pallas_call(
        functools.partial(spread_kernel, pieces),
        grid=(2,),
        in_specs=[pl.BlockSpec((half, width), lambda i: (i, 0))],
        out_specs=[
            pl.BlockSpec((units, 1, count, LANES), lambda i: (0, i, 0, 0)) for _, units in pieces
        ],
        out_shape=[jax.ShapeDtypeStruct((units, 2, count, LANES), BF16) for _, units in pieces],
        compiler_params=params(1),
        cost_estimate=pl.CostEstimate(flops=0, bytes_accessed=2 * 10**6, transcendentals=0),
        name="spread",
    )(rows_array)


def turn_back(tile, cos_table, sine_table):
    near = (lane_index(tile.shape[0]) % HEAD_DIM) < HEAD_DIM // 2
    scaled = tile * sine_table
    moved = jnp.where(
        near,
        pltpu.roll(scaled, LANES - HEAD_DIM // 2, 1),
        pltpu.roll(scaled, HEAD_DIM // 2, 1),
    )
    return tile * cos_table + moved


def collect_grad_kernel(spots, c_ref, s_ref, *refs):
    ins, (q_out, k_out, v_out) = refs[:-3], refs[-3:]
    cos_table, sine_table = c_ref[...], s_ref[...]
    rows = cos_table.shape[0]
    low = lane_index(rows) < HEAD_DIM
    for pair in range(len(spots) // 2):
        cut = slice(pair * LANES, (pair + 1) * LANES)
        kvs, packed = [], []
        for side in range(2):
            array, spot = spots[2 * pair + side]
            kvs.append(ins[array][spot, 0, :rows, :].astype(F32))
            packed.append(ins[array][spot, 0, rows:, :].astype(F32))
        grad_k = jnp.where(low, kvs[0], flip(kvs[1]))
        grad_v = jnp.where(low, flip(kvs[0]), kvs[1])
        q_out[:, cut] = turn_back(unpack_pair(*packed), cos_table, sine_table).astype(BF16)
        k_out[:, cut] = turn_back(grad_k, cos_table, sine_table).astype(BF16)
        v_out[:, cut] = grad_v.astype(BF16)


def collect_grad(spots, arrays, cos_table, sine_table):
    units, _, depth, _ = arrays[0].shape
    half = depth * 2 // 3
    width = len(spots) * HEAD_DIM
    row_block = pl.BlockSpec((half, width), lambda i: (i, 0))
    table = pl.BlockSpec((half, LANES), lambda i: (i, 0))
    shape = jax.ShapeDtypeStruct((2 * half, width), BF16)
    return pl.pallas_call(
        functools.partial(collect_grad_kernel, spots),
        grid=(2,),
        in_specs=[table, table]
        + [pl.BlockSpec((units, 1, depth, LANES), lambda i: (0, i, 0, 0)) for _ in arrays],
        out_specs=[row_block] * 3,
        out_shape=[shape] * 3,
        compiler_params=params(1),
        cost_estimate=pl.CostEstimate(flops=0, bytes_accessed=6 * 10**6, transcendentals=0),
        name="collect_grad",
    )(cos_table, sine_table, *arrays)


def matmul(left, right):
    return jnp.dot(left, right, preferred_element_type=F32)


def norm_backward(grad_out, values, recip_rows, gain):
    scaled = grad_out * gain
    grad_in = recip_rows * scaled - values * (recip_rows * recip_rows * recip_rows) * jnp.mean(
        scaled * values, -1, keepdims=True
    )
    return (grad_in, jnp.sum(grad_out * values * recip_rows, 0))


def feed_forward(tokens, cotangent, attended, w_out, gain_mlp, w_gate, w_up, w_down):
    inputs = tokens.astype(F32)
    gain = gain_mlp.astype(F32)
    middle = inputs + matmul(attended, w_out)
    recip = lax.rsqrt(jnp.mean(middle * middle, -1, keepdims=True) + EPS)
    mlp_low = (middle * recip * gain).astype(BF16)
    gate_pre = matmul(mlp_low, w_gate)
    up_pre = matmul(mlp_low, w_up)
    gate_sigmoid = jax.nn.sigmoid(gate_pre)
    silu_value = gate_pre * gate_sigmoid
    hidden_low = (silu_value * up_pre).astype(BF16)
    result = (middle + matmul(hidden_low, w_down)).astype(BF16)
    grad_hidden = jnp.einsum("td,fd->tf", cotangent, w_down, preferred_element_type=F32)
    grad_gate = (
        grad_hidden * up_pre * gate_sigmoid * (1.0 + gate_pre * (1.0 - gate_sigmoid))
    ).astype(BF16)
    grad_up = (grad_hidden * silu_value).astype(BF16)
    grad_normed = jnp.einsum(
        "tf,df->td", grad_gate, w_gate, preferred_element_type=F32
    ) + jnp.einsum("tf,df->td", grad_up, w_up, preferred_element_type=F32)
    grad_mid, grad_gain = norm_backward(grad_normed, middle, recip, gain)
    grad_middle = cotangent.astype(F32) + grad_mid
    grad_branch = grad_middle.astype(BF16)
    grad_att = jnp.einsum("te,de->td", grad_branch, w_out, preferred_element_type=F32).astype(BF16)
    return result, grad_middle, grad_att, grad_gain, (
        (attended, grad_branch),
        (mlp_low, grad_gate),
        (mlp_low, grad_up),
        (hidden_low, cotangent),
    )


def outer_sum(pairs):
    total = None
    for left, right in pairs:
        part = jnp.einsum("td,te->de", left, right, preferred_element_type=F32)
        total = part if total is None else total + part
    return total


def body(
    tokens, cotangent, doc_lengths, gain_attn, w_query, w_key, w_value, w_out, gain_mlp, w_gate, w_up, w_down
):
    micros, _, rows, width = tokens.shape
    heads = width // HEAD_DIM
    devices = lax.axis_size("ctx")
    place = lax.axis_index("ctx")
    chips = devices // 2
    core = place % 2
    half = rows // 2
    units = micros * heads
    rounds = -(-units // chips)
    swap = [(i, i ^ 1) for i in range(devices)]

    def gathered(shard):
        return lax.all_gather(shard, "fsdp", axis=0, tiled=True)

    gain_attn, w_query, w_key, w_value, w_out, gain_mlp, w_gate, w_up, w_down = (
        gathered(shard)
        for shard in (gain_attn, w_query, w_key, w_value, w_out, gain_mlp, w_gate, w_up, w_down)
    )
    lengths = doc_lengths[:, 0]
    doc_ends = jnp.cumsum(lengths, -1)
    starts = (doc_ends - lengths).astype(jnp.int32)

    def begins_of(micro_starts, positions):
        reached = positions[:, None] >= micro_starts[None, :]
        return jnp.max(jnp.where(reached, micro_starts[None, :], 0), -1)

    lane = jnp.arange(LANES)
    inverse = jnp.power(10000.0, -(lane % (HEAD_DIM // 2)).astype(F32) / (HEAD_DIM // 2))
    sign = jnp.where((lane % HEAD_DIM) < HEAD_DIM // 2, -1.0, 1.0)
    positions = place * rows + jnp.arange(rows, dtype=jnp.int32)
    tables = []
    for micro in range(micros):
        offsets = (positions - begins_of(starts[micro], positions)).astype(F32)
        angles = offsets[:, None] * inverse[None, :]
        tables.append((jnp.cos(angles), jnp.sin(angles) * sign))

    def parts_of(micro):
        parts = []
        for turn_index in range(rounds):
            first = max(turn_index * chips, micro * heads)
            last = min((turn_index + 1) * chips, (micro + 1) * heads)
            if last > first:
                parts.append((turn_index, first - micro * heads, last - first))
        return parts

    def assemble(per_micro, tail):
        buffers = []
        for turn_index in range(rounds):
            found = [piece for piece, (index, _, _) in per_micro if index == turn_index]
            held = sum(piece.shape[0] for piece in found)
            if held < chips:
                found.append(jnp.zeros((chips - held, 2) + tail, BF16))
            whole = found[0] if len(found) == 1 else jnp.concatenate(found, 0)
            buffers.append(whole.reshape((devices,) + tail))
        return buffers

    def spots_of(micro):
        used = [index for index, _, _ in parts_of(micro)]
        spots = []
        for head in range(heads):
            unit = micro * heads + head
            spots.append((used.index(unit // chips), unit % chips))
        return used, tuple(spots)

    def exchange(buffer):
        return lax.all_to_all(buffer, "ctx", split_axis=0, concat_axis=0, tiled=True)

    normed, sends = [], []
    for micro in range(micros):
        parts = parts_of(micro)
        outs = project(
            tuple((first, count) for _, first, count in parts),
            tokens[micro, 0],
            gain_attn[None, :],
            *tables[micro],
            w_query,
            w_key,
            w_value,
        )
        normed.append(outs[0])
        sends += list(zip(outs[1:], parts))
    depth = half + half // 2
    received = [exchange(buffer) for buffer in assemble(sends, (depth, LANES))]

    block_first = jnp.arange(devices, dtype=jnp.int32) * rows + core * half
    infos, unit_starts, others, attended_back, kept = [], [], [], [], []
    for turn_index in range(rounds):
        unit = turn_index * chips + place // 2
        chosen = lax.dynamic_index_in_dim(
            starts, jnp.minimum(unit // heads, micros - 1), 0, keepdims=False
        )
        lowest = begins_of(chosen, block_first) // rows
        inner = -(-begins_of(chosen, block_first + half - 1) // rows)
        block = jnp.arange(devices, dtype=jnp.int32)
        live = unit < units
        lowest = jnp.where(live, lowest, block)
        inner = jnp.where(live, jnp.minimum(inner, block), block)
        info = jnp.concatenate([core[None], jnp.stack([lowest, inner], 1).reshape(-1)])
        infos.append(info.astype(jnp.int32))
        unit_starts.append(chosen)
        other = lax.ppermute(received[turn_index], "ctx", swap)
        others.append(other)
        out, lse = attend(infos[-1], chosen, received[turn_index], other)
        kept.append((out, lse))
        attended_back.append(exchange(out).reshape(chips, 2, half // 2, LANES))

    results, grad_middles, mid_pairs, grad_gain_mlp, grad_sends = [], [], [], 0.0, []
    for micro in range(micros):
        used, spots = spots_of(micro)
        attended = collect(spots, [attended_back[index] for index in used])
        result, grad_middle, grad_att, grad_gain, pairs = feed_forward(
            tokens[micro, 0], cotangent[micro, 0], attended, w_out, gain_mlp, w_gate, w_up, w_down
        )
        results.append(result)
        grad_middles.append(grad_middle)
        mid_pairs.append(pairs)
        grad_gain_mlp = grad_gain_mlp + grad_gain
        parts = parts_of(micro)
        outs = spread(tuple((first, count) for _, first, count in parts), grad_att)
        grad_sends += list(zip(outs, parts))
    grads_in = [exchange(buffer) for buffer in assemble(grad_sends, (half // 2, LANES))]

    def reduced(full):
        part = lax.psum_scatter(full.astype(BF16), "fsdp", scatter_dimension=0, tiled=True)
        return part

    grad_w_out, grad_w_gate, grad_w_up, grad_w_down = (
        reduced(outer_sum([pairs[index] for pairs in mid_pairs])) for index in range(4)
    )

    grad_back = []
    for turn_index in range(rounds):
        own, away = attend_grad(
            infos[turn_index],
            unit_starts[turn_index],
            received[turn_index],
            others[turn_index],
            grads_in[turn_index],
            *kept[turn_index],
        )
        back = lax.ppermute(away, "ctx", swap)
        own_kv = (own[:, :half].astype(F32) + back.astype(F32)).astype(BF16)
        buffer = jnp.concatenate([own_kv, own[:, half:]], 1)
        grad_back.append(exchange(buffer).reshape(chips, 2, depth, LANES))

    grad_inputs, grad_pairs, grad_gain_attn = [], [], 0.0
    for micro in range(micros):
        used, spots = spots_of(micro)
        grad_q, grad_k, grad_v = collect_grad(
            spots, [grad_back[index] for index in used], *tables[micro]
        )
        grad_normed = (
            jnp.einsum("te,de->td", grad_q, w_query, preferred_element_type=F32)
            + jnp.einsum("te,de->td", grad_k, w_key, preferred_element_type=F32)
            + jnp.einsum("te,de->td", grad_v, w_value, preferred_element_type=F32)
        )
        inputs = tokens[micro, 0].astype(F32)
        recip = lax.rsqrt(jnp.mean(inputs * inputs, -1, keepdims=True) + EPS)
        grad_in, grad_gain = norm_backward(grad_normed, inputs, recip, gain_attn.astype(F32))
        grad_inputs.append((grad_middles[micro] + grad_in).astype(BF16))
        grad_gain_attn = grad_gain_attn + grad_gain
        grad_pairs.append(
            ((normed[micro], grad_q), (normed[micro], grad_k), (normed[micro], grad_v))
        )
    grad_w_query, grad_w_key, grad_w_value = (
        reduced(outer_sum([pairs[index] for pairs in grad_pairs])) for index in range(3)
    )
    grads = (
        reduced(grad_gain_attn),
        grad_w_query,
        grad_w_key,
        grad_w_value,
        grad_w_out,
        reduced(grad_gain_mlp),
        grad_w_gate,
        grad_w_up,
        grad_w_down,
    )
    totals = [lax.psum(part, "ctx").astype(F32) for part in grads]
    return (jnp.stack(results)[:, None], jnp.stack(grad_inputs)[:, None], *totals)


def solution(mesh):
    weight, gain = P("fsdp", None), P("fsdp")
    rows = P(None, "fsdp", "ctx", None)
    weights = (gain, weight, weight, weight, weight, gain, weight, weight, weight)
    return jax.shard_map(
        body,
        mesh=mesh,
        in_specs=(rows, rows, P(None, "fsdp", None)) + weights,
        out_specs=(rows, rows) + weights,
        check_vma=False,
    )
```

```python
import functools
import math

import jax
import jax.numpy as jnp
from jax import lax
from jax.experimental import pallas as pl
from jax.experimental.pallas import tpu as pltpu
from jax.sharding import PartitionSpec as P

HEAD_DIM = 64
LANES = 128
EPS = 1e-05
NEG = -1e30
LOG2E = math.log2(math.e)
LN2 = math.log(2.0)
F32 = jnp.float32
BF16 = jnp.bfloat16


def dot_nt(left, right):
    return lax.dot_general(left, right, (((1,), (1,)), ((), ())), preferred_element_type=F32)


def dot_nn(left, right):
    return lax.dot_general(left, right, (((1,), (0,)), ((), ())), preferred_element_type=F32)


def dot_tn(left, right):
    return lax.dot_general(left, right, (((0,), (0,)), ((), ())), preferred_element_type=F32)


def lane_index(rows):
    return lax.broadcasted_iota(jnp.int32, (rows, LANES), 1)


def flip(tile):
    return pltpu.roll(tile, HEAD_DIM, 1)


def params(count):
    return pltpu.CompilerParams(
        dimension_semantics=("arbitrary",) * count, vmem_limit_bytes=60 * 1024 * 1024
    )


def full_block(shape):
    zeros = (0,) * len(shape)
    return pl.BlockSpec(shape, lambda *_: zeros)


def pack_pair(tile):
    count = tile.shape[0] // 2
    low = lane_index(count) < HEAD_DIM
    top, bottom = tile[:count], tile[count:]
    return (jnp.where(low, top, flip(bottom)), jnp.where(low, flip(top), bottom))


def unpack_pair(first, second):
    low = lane_index(first.shape[0]) < HEAD_DIM
    top = jnp.where(low, first, flip(second))
    bottom = jnp.where(low, flip(first), second)
    return jnp.concatenate([top, bottom], 0)


def turn(tile):
    near = (lane_index(tile.shape[0]) % HEAD_DIM) < HEAD_DIM // 2
    return jnp.where(
        near, pltpu.roll(tile, LANES - HEAD_DIM // 2, 1), pltpu.roll(tile, HEAD_DIM // 2, 1)
    )


def project_kernel(count, n_ref, c_ref, s_ref, w_ref, out):
    joined = dot_nn(n_ref[...], w_ref[...])
    cos_table, sine_table = c_ref[...], s_ref[...]
    rows = n_ref.shape[0]
    span = count * HEAD_DIM
    low = lane_index(rows) < HEAD_DIM
    for pair in range(count // 2):
        first = pair * LANES
        q2, k2, v2 = (joined[:, part * span + first : part * span + first + LANES] for part in range(3))
        q2 = (q2 * cos_table + turn(q2) * sine_table) * (LOG2E * HEAD_DIM**-0.5)
        k2 = k2 * cos_table + turn(k2) * sine_table
        packed = pack_pair(q2)
        kv = (jnp.where(low, k2, flip(v2)), jnp.where(low, flip(k2), v2))
        for side in range(2):
            out[2 * pair + side, 0, :rows, :] = kv[side].astype(BF16)
            out[2 * pair + side, 0, rows:, :] = packed[side].astype(BF16)
    if count < out.shape[0]:
        out[count:] = jnp.zeros((out.shape[0] - count,) + out.shape[1:], BF16)


def project(span, count, micros, normed, cos_table, sine_table, weight):
    rows, width = normed.shape
    half = rows // (2 * micros)
    depth = half + half // 2
    return pl.pallas_call(
        functools.partial(project_kernel, count),
        grid=(micros, 2),
        in_specs=[
            pl.BlockSpec((half, width), lambda m, i: (2 * m + i, 0)),
            pl.BlockSpec((half, LANES), lambda m, i: (2 * m + i, 0)),
            pl.BlockSpec((half, LANES), lambda m, i: (2 * m + i, 0)),
            full_block(weight.shape),
        ],
        out_specs=pl.BlockSpec((span, 1, depth, LANES), lambda m, i: (m, i, 0, 0)),
        out_shape=jax.ShapeDtypeStruct((micros * span, 2, depth, LANES), BF16),
        compiler_params=params(2),
        cost_estimate=pl.CostEstimate(
            flops=2 * rows * width * weight.shape[1], bytes_accessed=4 * rows * width, transcendentals=0
        ),
        name="project",
    )(normed, cos_table, sine_table, weight)


def row_begins(starts_ref, positions):
    begins = jnp.zeros_like(positions)
    for index in range(starts_ref.shape[0]):
        start = starts_ref[index]
        begins = jnp.maximum(begins, jnp.where(positions >= start, start, 0))
    return begins


def unpack_one(packed, lanes_low):
    wide = packed.astype(F32)
    low = lane_index(wide.shape[0]) < HEAD_DIM
    keep = low if lanes_low else jnp.logical_not(low)
    turned = flip(wide)
    first, second = (wide, turned) if lanes_low else (turned, wide)
    return jnp.concatenate(
        [jnp.where(keep, first, 0.0), jnp.where(keep, second, 0.0)], 0
    ).astype(BF16)


def attend_kernel(info, starts, mine, other, o_ref, lse_ref):
    block = pl.program_id(0)
    core = info[0]
    lowest, inner = info[1 + 2 * block], info[2 + 2 * block]
    rows = mine.shape[1] * 2 // 3
    low = lane_index(rows) < HEAD_DIM
    queries = unpack_one(mine[block, rows:, :], True)
    row_pos = (2 * block + core) * rows + lax.broadcasted_iota(jnp.int32, (rows, 1), 0)
    begins = row_begins(starts, row_pos)
    lane_low = lane_index(2 * rows) < HEAD_DIM
    column = lax.broadcasted_iota(jnp.int32, (1, 2 * rows), 1)
    offsets = jnp.where(column < rows, column + core * rows, column - core * rows)

    def step(masked, index, carry):
        peak, acc = carry
        kv = jnp.concatenate([mine[index, :rows, :], other[index, :rows, :]], 0)
        ones_v = jnp.where(lane_low, jnp.ones_like(kv), kv)
        scores = dot_nt(queries, kv)
        if masked:
            key_pos = offsets + index * (2 * rows)
            scores = jnp.where((key_pos >= begins) & (key_pos <= row_pos), scores, NEG)
        new_peak = jnp.maximum(peak, jnp.max(scores, -1, keepdims=True))
        weights = jnp.exp2(scores - new_peak)
        acc = acc * jnp.exp2(peak - new_peak) + dot_nn(weights.astype(BF16), ones_v)
        return (new_peak, acc)

    carry = step(True, block, (jnp.full((rows, 1), NEG, F32), jnp.zeros((rows, LANES), F32)))
    carry = lax.fori_loop(lowest, inner, functools.partial(step, True), carry)
    peak, acc = lax.fori_loop(inner, block, functools.partial(step, False), carry)
    result = acc / flip(acc)
    count = rows // 2
    small_low = lane_index(count) < HEAD_DIM
    o_ref[0] = jnp.where(small_low, flip(result[:count]), result[count:]).astype(BF16)
    lse = jnp.where(low, peak + jnp.log2(acc), 0.0)
    lse_ref[0] = jnp.transpose(lse)[0:1, :]


def attend(info, starts, mine, other):
    blocks, depth, _ = mine.shape
    rows = depth * 2 // 3
    return pl.pallas_call(
        attend_kernel,
        grid_spec=pltpu.PrefetchScalarGridSpec(
            num_scalar_prefetch=2,
            grid=(blocks,),
            in_specs=[
                pl.BlockSpec(mine.shape, lambda i, *_: (0, 0, 0)),
                pl.BlockSpec(other.shape, lambda i, *_: (0, 0, 0)),
            ],
            out_specs=[
                pl.BlockSpec((1, rows // 2, LANES), lambda i, *_: (i, 0, 0)),
                pl.BlockSpec((1, 1, rows), lambda i, *_: (i, 0, 0)),
            ],
        ),
        out_shape=[
            jax.ShapeDtypeStruct((blocks, rows // 2, LANES), BF16),
            jax.ShapeDtypeStruct((blocks, 1, rows), F32),
        ],
        compiler_params=params(1),
        cost_estimate=pl.CostEstimate(
            flops=16 * 10**9, bytes_accessed=10**7, transcendentals=10**7
        ),
        name="attend",
    )(info, starts, mine, other)


def attend_grad_kernel(
    info, starts, mine, other, do_ref, o_ref, lse_ref, dm_ref, dp_ref, acc_mine, acc_other
):
    block = pl.program_id(0)
    core = info[0]
    lowest, inner = info[1 + 2 * block], info[2 + 2 * block]
    rows = mine.shape[1] * 2 // 3
    count = rows // 2

    @pl.when(block == 0)
    def _():
        acc_mine[...] = jnp.zeros_like(acc_mine)
        acc_other[...] = jnp.zeros_like(acc_other)

    queries = unpack_one(mine[block, rows:, :], True)
    grad_out = unpack_one(do_ref[0], False)
    both = jnp.concatenate([queries, grad_out], 0)
    product = jnp.transpose(do_ref[0].astype(F32) * o_ref[0].astype(F32))
    delta = jnp.concatenate(
        [
            jnp.sum(product[:HEAD_DIM], 0, keepdims=True),
            jnp.sum(product[HEAD_DIM:], 0, keepdims=True),
        ],
        1,
    )
    lse = lse_ref[0]
    row_pos = (2 * block + core) * rows + lax.broadcasted_iota(jnp.int32, (1, rows), 1)
    begins = row_begins(starts, row_pos)
    line = lax.broadcasted_iota(jnp.int32, (2 * rows, 1), 0)
    offsets = jnp.where(line < rows, line + core * rows, line - core * rows)

    def step(masked, index, grad_q):
        kv = jnp.concatenate([mine[index, :rows, :], other[index, :rows, :]], 0)
        scores = dot_nt(kv, queries)
        weights = jnp.exp2(scores - lse)
        if masked:
            key_pos = offsets + index * (2 * rows)
            weights = jnp.where((key_pos >= begins) & (key_pos <= row_pos), weights, 0.0)
        grad_weights = dot_nt(kv, grad_out)
        grad_scores = (weights * (grad_weights - delta)).astype(BF16)
        grad_kv = dot_nn(jnp.concatenate([grad_scores, weights.astype(BF16)], 1), both)
        acc_mine[index] += grad_kv[:rows]
        acc_other[index] += grad_kv[rows:]
        return grad_q + dot_tn(grad_scores, kv)

    grad_q = step(True, block, jnp.zeros((rows, LANES), F32))
    grad_q = lax.fori_loop(lowest, inner, functools.partial(step, True), grad_q)
    grad_q = lax.fori_loop(inner, block, functools.partial(step, False), grad_q)
    grad_q = grad_q * HEAD_DIM**-0.5
    small_low = lane_index(count) < HEAD_DIM
    dm_ref[block, rows:, :] = jnp.where(small_low, grad_q[:count], flip(grad_q[count:])).astype(
        BF16
    )

    @pl.when(block == pl.num_programs(0) - 1)
    def _():
        scale = jnp.where(lane_index(rows) < HEAD_DIM, LN2, 1.0)

        def flush(index, _):
            dm_ref[index, :rows, :] = (acc_mine[index] * scale).astype(BF16)
            dp_ref[index] = (acc_other[index] * scale).astype(BF16)
            return 0

        lax.fori_loop(0, mine.shape[0], flush, 0)


def attend_grad(info, starts, mine, other, grad_out, spot, out, lse):
    blocks, depth, _ = mine.shape
    rows = depth * 2 // 3
    whole = pl.BlockSpec(mine.shape, lambda i, *_: (0, 0, 0))
    small = pl.BlockSpec((1, rows // 2, LANES), lambda i, *_: (i, 0, 0))
    return pl.pallas_call(
        attend_grad_kernel,
        grid_spec=pltpu.PrefetchScalarGridSpec(
            num_scalar_prefetch=2,
            grid=(blocks,),
            in_specs=[
                whole,
                whole,
                pl.BlockSpec((1, rows // 2, LANES), lambda i, *_: (i, spot, 0)),
                small,
                pl.BlockSpec((1, 1, rows), lambda i, *_: (i, 0, 0)),
            ],
            out_specs=[whole, pl.BlockSpec((blocks, rows, LANES), lambda i, *_: (0, 0, 0))],
            scratch_shapes=[
                pltpu.VMEM((blocks, rows, LANES), F32),
                pltpu.VMEM((blocks, rows, LANES), F32),
            ],
        ),
        out_shape=[
            jax.ShapeDtypeStruct(mine.shape, BF16),
            jax.ShapeDtypeStruct((blocks, rows, LANES), BF16),
        ],
        compiler_params=params(1),
        cost_estimate=pl.CostEstimate(
            flops=32 * 10**9, bytes_accessed=10**7, transcendentals=10**7
        ),
        name="attend_grad",
    )(info, starts, mine, other, grad_out, out, lse)


def collect_kernel(counts, *refs):
    ins, out = refs[:-1], refs[-1]
    length = out.shape[0] // 2
    pieces = [(array, first) for array in ins for first in range(0, array.shape[2], length)]
    pair = 0
    for (array, first), count in zip(pieces, counts):
        cut = slice(first, first + length)
        for spot in range(0, count, 2):
            tiles = [array[spot + side, 0, cut, :].astype(F32) for side in range(2)]
            out[:, pair * LANES : (pair + 1) * LANES] = unpack_pair(*tiles).astype(BF16)
            pair += 1


def collect(counts, micros, arrays):
    units = arrays[0].shape[0]
    length = sum(array.shape[2] for array in arrays) // len(counts)
    width = sum(counts) * HEAD_DIM
    return pl.pallas_call(
        functools.partial(collect_kernel, counts),
        grid=(micros, 2),
        in_specs=[
            pl.BlockSpec((units // micros, 1, array.shape[2], LANES), lambda m, i: (m, i, 0, 0))
            for array in arrays
        ],
        out_specs=pl.BlockSpec((2 * length, width), lambda m, i: (2 * m + i, 0)),
        out_shape=jax.ShapeDtypeStruct((micros * 4 * length, width), BF16),
        compiler_params=params(2),
        cost_estimate=pl.CostEstimate(flops=0, bytes_accessed=4 * 10**6, transcendentals=0),
        name="collect",
    )(*arrays)


def spread_kernel(counts, x_ref, *outs):
    length = x_ref.shape[0] // 2
    pieces = [(out, first) for out in outs for first in range(0, out.shape[2], length)]
    pair = 0
    for (out, first), count in zip(pieces, counts):
        cut = slice(first, first + length)
        for spot in range(0, count, 2):
            tile = x_ref[:, pair * LANES : (pair + 1) * LANES].astype(F32)
            packed = pack_pair(tile)
            for side in range(2):
                out[spot + side, 0, cut, :] = packed[side].astype(BF16)
            pair += 1
        for spot in range(count, out.shape[0]):
            out[spot, 0, cut, :] = jnp.zeros((length, LANES), BF16)


def spread(span, counts, micros, rows_array):
    rows, width = rows_array.shape
    half = rows // (2 * micros)
    lengths = [half // 2] + ([half // 2 * (len(counts) - 1)] if len(counts) > 1 else [])
    return pl.pallas_call(
        functools.partial(spread_kernel, counts),
        grid=(micros, 2),
        in_specs=[pl.BlockSpec((half, width), lambda m, i: (2 * m + i, 0))],
        out_specs=[
            pl.BlockSpec((span, 1, length, LANES), lambda m, i: (m, i, 0, 0)) for length in lengths
        ],
        out_shape=[
            jax.ShapeDtypeStruct((micros * span, 2, length, LANES), BF16) for length in lengths
        ],
        compiler_params=params(2),
        cost_estimate=pl.CostEstimate(flops=0, bytes_accessed=4 * 10**6, transcendentals=0),
        name="spread",
    )(rows_array)


def turn_back(tile, cos_table, sine_table):
    near = (lane_index(tile.shape[0]) % HEAD_DIM) < HEAD_DIM // 2
    scaled = tile * sine_table
    moved = jnp.where(
        near,
        pltpu.roll(scaled, LANES - HEAD_DIM // 2, 1),
        pltpu.roll(scaled, HEAD_DIM // 2, 1),
    )
    return tile * cos_table + moved


def collect_grad_kernel(count, c_ref, s_ref, in_ref, out):
    cos_table, sine_table = c_ref[...], s_ref[...]
    rows = cos_table.shape[0]
    span = count * HEAD_DIM
    low = lane_index(rows) < HEAD_DIM
    for pair in range(count // 2):
        kvs = [in_ref[2 * pair + side, 0, :rows, :].astype(F32) for side in range(2)]
        packed = [in_ref[2 * pair + side, 0, rows:, :].astype(F32) for side in range(2)]
        grad_k = jnp.where(low, kvs[0], flip(kvs[1]))
        grad_v = jnp.where(low, flip(kvs[0]), kvs[1])
        grad_q = turn_back(unpack_pair(*packed), cos_table, sine_table)
        grad_k = turn_back(grad_k, cos_table, sine_table)
        for part, value in enumerate((grad_q, grad_k, grad_v)):
            first = part * span + pair * LANES
            out[:, first : first + LANES] = value.astype(BF16)


def collect_grad(count, micros, array, cos_table, sine_table):
    units, _, depth, _ = array.shape
    half = depth * 2 // 3
    width = 3 * count * HEAD_DIM
    table = pl.BlockSpec((half, LANES), lambda m, i: (2 * m + i, 0))
    return pl.pallas_call(
        functools.partial(collect_grad_kernel, count),
        grid=(micros, 2),
        in_specs=[
            table,
            table,
            pl.BlockSpec((units // micros, 1, depth, LANES), lambda m, i: (m, i, 0, 0)),
        ],
        out_specs=pl.BlockSpec((half, width), lambda m, i: (2 * m + i, 0)),
        out_shape=jax.ShapeDtypeStruct((micros * 2 * half, width), BF16),
        compiler_params=params(2),
        cost_estimate=pl.CostEstimate(flops=0, bytes_accessed=6 * 10**6, transcendentals=0),
        name="collect_grad",
    )(cos_table, sine_table, array)


def matmul(left, right):
    return jnp.dot(left, right, preferred_element_type=F32)


def norm_backward(grad_out, values, recip_rows, gain):
    scaled = grad_out * gain
    grad_in = recip_rows * scaled - values * (recip_rows * recip_rows * recip_rows) * jnp.mean(
        scaled * values, -1, keepdims=True
    )
    return (grad_in, jnp.sum(grad_out * values * recip_rows, 0))


def feed_forward(tokens, cotangent, attended, w_out, gain_mlp, w_gate, w_up, w_down):
    inputs = tokens.astype(F32)
    gain = gain_mlp.astype(F32)
    middle = inputs + matmul(attended, w_out)
    recip = lax.rsqrt(jnp.mean(middle * middle, -1, keepdims=True) + EPS)
    mlp_low = (middle * recip * gain).astype(BF16)
    gate_pre = matmul(mlp_low, w_gate)
    up_pre = matmul(mlp_low, w_up)
    gate_sigmoid = jax.nn.sigmoid(gate_pre)
    silu_value = gate_pre * gate_sigmoid
    hidden_low = (silu_value * up_pre).astype(BF16)
    result = (middle + matmul(hidden_low, w_down)).astype(BF16)
    grad_hidden = jnp.einsum("td,fd->tf", cotangent, w_down, preferred_element_type=F32)
    grad_gate = (
        grad_hidden * up_pre * gate_sigmoid * (1.0 + gate_pre * (1.0 - gate_sigmoid))
    ).astype(BF16)
    grad_up = (grad_hidden * silu_value).astype(BF16)
    grad_normed = jnp.einsum(
        "tf,df->td", grad_gate, w_gate, preferred_element_type=F32
    ) + jnp.einsum("tf,df->td", grad_up, w_up, preferred_element_type=F32)
    grad_mid, grad_gain = norm_backward(grad_normed, middle, recip, gain)
    grad_middle = cotangent.astype(F32) + grad_mid
    grad_branch = grad_middle.astype(BF16)
    grad_att = jnp.einsum("te,de->td", grad_branch, w_out, preferred_element_type=F32).astype(BF16)
    return result, grad_middle, grad_att, grad_gain, (
        (attended, grad_branch),
        (mlp_low, grad_gate),
        (mlp_low, grad_up),
        (hidden_low, cotangent),
    )


def outer(left, right):
    return jnp.einsum("td,te->de", left, right, preferred_element_type=F32).astype(BF16)


def after(value, *others):
    return lax.optimization_barrier((value,) + others)[0]


def body(
    tokens, cotangent, doc_lengths, gain_attn, w_query, w_key, w_value, w_out, gain_mlp, w_gate, w_up, w_down
):
    micros, _, rows, width = tokens.shape
    heads = width // HEAD_DIM
    devices = lax.axis_size("ctx")
    shards = lax.axis_size("fsdp")
    place = lax.axis_index("ctx")
    side = lax.axis_index("fsdp")
    chips = devices // 2
    core = place % 2
    half = rows // 2
    depth = half + half // 2
    span = chips // micros
    rounds = -(-heads // span)
    counts = tuple(min(span, heads - index * span) for index in range(rounds))
    swap = [(i, i ^ 1) for i in range(devices)]
    cross = [(0, 1), (1, 0)]

    def pick(array, index, axis):
        return lax.dynamic_index_in_dim(array, index, axis, keepdims=False)

    def gathered(shard):
        return lax.all_gather(shard, "fsdp", axis=0, tiled=True)

    def fetched(shard):
        if shards != 2:
            return gathered(shard)
        depth_two = shard.reshape((2, shard.shape[0] // 2) + shard.shape[1:])
        near = lax.ppermute(pick(depth_two, core, 0), "fsdp", cross)
        far = lax.ppermute(near, "ctx", swap)
        away = jnp.where(core == 0, jnp.stack([near, far]), jnp.stack([far, near]))
        away = away.reshape(shard.shape)
        return jnp.where(
            side == 0, jnp.concatenate([shard, away]), jnp.concatenate([away, shard])
        )

    def fetched_line(line):
        if shards != 2:
            return gathered(line)
        away = lax.ppermute(line, "fsdp", cross)
        return jnp.where(side == 0, jnp.concatenate([line, away]), jnp.concatenate([away, line]))

    def columns(index):
        cut = slice(index * span * HEAD_DIM, (index * span + counts[index]) * HEAD_DIM)
        return jnp.concatenate([w_query[:, cut], w_key[:, cut], w_value[:, cut]], 1)

    gain_attn, gain_mlp = fetched_line(gain_attn), fetched_line(gain_mlp)
    in_weights = [fetched(columns(index)) for index in range(rounds)]
    w_out, w_gate, w_up, w_down = (gathered(shard) for shard in (w_out, w_gate, w_up, w_down))
    lengths = doc_lengths[:, 0]
    doc_ends = jnp.cumsum(lengths, -1)
    starts = (doc_ends - lengths).astype(jnp.int32)

    def begins_of(micro_starts, positions):
        reached = positions[:, None] >= micro_starts[None, :]
        return jnp.max(jnp.where(reached, micro_starts[None, :], 0), -1)

    lane = jnp.arange(LANES)
    inverse = jnp.power(10000.0, -(lane % (HEAD_DIM // 2)).astype(F32) / (HEAD_DIM // 2))
    sign = jnp.where((lane % HEAD_DIM) < HEAD_DIM // 2, -1.0, 1.0)
    positions = place * rows + jnp.arange(rows, dtype=jnp.int32)
    offsets = jnp.concatenate(
        [positions - begins_of(starts[micro], positions) for micro in range(micros)]
    ).astype(F32)
    angles = offsets[:, None] * inverse[None, :]
    cos_table, sine_table = jnp.cos(angles), jnp.sin(angles) * sign

    def exchange(buffer):
        return lax.all_to_all(buffer, "ctx", split_axis=0, concat_axis=0, tiled=True)

    tokens = tokens.reshape(micros * rows, width)
    cotangent = cotangent.reshape(micros * rows, width)
    inputs = tokens.astype(F32)
    recip = lax.rsqrt(jnp.mean(inputs * inputs, -1, keepdims=True) + EPS)
    normed = (inputs * recip * gain_attn.astype(F32)).astype(BF16)

    block = jnp.arange(devices, dtype=jnp.int32)
    block_first = block * rows + core * half
    chosen = pick(starts, place // 2 // span, 0)
    lowest = begins_of(chosen, block_first) // rows
    inner = jnp.minimum(-(-begins_of(chosen, block_first + half - 1) // rows), block)

    received, infos, others, attended_back, kept = [], [], [], [], []
    for index in range(rounds):
        live = index * span + place // 2 % span < heads
        bounds = jnp.stack([jnp.where(live, lowest, block), jnp.where(live, inner, block)], 1)
        infos.append(jnp.concatenate([core[None], bounds.reshape(-1)]).astype(jnp.int32))
        buffer = project(
            span, counts[index], micros, normed, cos_table, sine_table, in_weights[index]
        ).reshape(devices, depth, LANES)
        if index >= 2:
            buffer = after(buffer, kept[index - 2][1])
        received.append(exchange(buffer))
        whole = received[index]
        if index:
            whole = after(whole, kept[index - 1][1])
        others.append(lax.ppermute(whole, "ctx", swap))
        out, lse = attend(infos[index], chosen, received[index], others[index])
        kept.append((out, lse))
    def came_back(pieces):
        joined = pieces[0] if len(pieces) == 1 else jnp.concatenate(pieces, 1)
        joined = exchange(joined)
        return joined.reshape((chips, 2) + joined.shape[1:])

    early = [after(out, received[-1]) for out, _ in kept[:-1]]
    attended_back = ([came_back(early)] if early else []) + [came_back([kept[-1][0]])]

    attended = collect(counts, micros, attended_back)
    result, grad_middle, grad_att, grad_gain_mlp, pairs = feed_forward(
        tokens, cotangent, attended, w_out, gain_mlp, w_gate, w_up, w_down
    )
    grads_in = [
        exchange(buffer.reshape((devices,) + buffer.shape[2:]))
        for buffer in spread(span, counts, micros, grad_att)
    ]

    def paired(stay, leave, axis, routes):
        return (stay.astype(F32) + lax.ppermute(leave, axis, routes).astype(F32)).astype(BF16)

    def chip_summed(full, gain=None):
        count, wide = full.shape[0] // (2 * shards), full.shape[1]
        parts = full.reshape(shards, 2, count, wide)
        if gain is not None:
            line = gain.astype(BF16).reshape(shards, 2, 1, -1)
            line = jnp.pad(line, ((0, 0), (0, 0), (0, 15), (0, wide - line.shape[-1])))
            parts = jnp.concatenate([parts, line], 2)
        return paired(pick(parts, core, 1), pick(parts, 1 - core, 1), "ctx", swap)

    def owned(parts):
        if shards == 2:
            return paired(pick(parts, side, 0), pick(parts, 1 - side, 0), "fsdp", cross)
        return lax.psum_scatter(parts, "fsdp", scatter_dimension=0, tiled=False)

    alike = [list(range(first, devices, 2)) for first in range(2)]

    def totals_of(parts):
        totals = lax.psum(tuple(parts), "ctx", axis_index_groups=alike)
        found = []
        for total in totals:
            twin = lax.ppermute(total, "ctx", swap)
            found.append(jnp.where(core == 0, jnp.stack([total, twin]), jnp.stack([twin, total])))
        return found

    def opened(total, has_gain):
        wide = total.shape[-1]
        count = total.shape[1] - (16 if has_gain else 0)
        rows_part = total[:, :count].reshape(2 * count, wide).astype(F32)
        if not has_gain:
            return rows_part
        return rows_part, total[:, count, : width // (2 * shards)].reshape(-1).astype(F32)

    pair_out, pair_gate, pair_up, pair_down = pairs
    chip_down = chip_summed(outer(*pair_down))
    chip_gate = chip_summed(outer(*pair_gate))
    chip_up = chip_summed(outer(*pair_up))
    chip_out = chip_summed(outer(*pair_out), grad_gain_mlp)
    first_parts = [owned(chip_out), owned(chip_down)]
    second_parts = [owned(chip_gate), owned(chip_up)]
    first_totals = totals_of(first_parts)
    second_totals = totals_of([after(part, *first_totals) for part in second_parts])
    grad_w_out, grad_gain_mlp = opened(first_totals[0], True)
    grad_w_down = opened(first_totals[1], False)
    grad_w_gate, grad_w_up = (opened(total, False) for total in second_totals)

    grad_back = []
    waits = {0: (chip_out, chip_down, chip_gate, chip_up), 1: tuple(first_parts), 2: tuple(second_parts)}
    for index in range(rounds):
        own, away = attend_grad(
            infos[index],
            chosen,
            received[index],
            others[index],
            after(grads_in[min(index, 1)], *waits.get(index, ())),
            max(index - 1, 0),
            *kept[index],
        )
        back = lax.ppermute(away, "ctx", swap)
        own_kv = (own[:, :half].astype(F32) + back.astype(F32)).astype(BF16)
        buffer = jnp.concatenate([own_kv, own[:, half:]], 1)
        grad_back.append(exchange(buffer).reshape(chips, 2, depth, LANES))

    grad_normed, parts = 0.0, []
    for index in range(rounds):
        grad_qkv = collect_grad(counts[index], micros, grad_back[index], cos_table, sine_table)
        grad_normed = grad_normed + jnp.einsum(
            "te,de->td", grad_qkv, in_weights[index], preferred_element_type=F32
        )
        final = index == rounds - 1
        if final:
            grad_in, grad_gain = norm_backward(grad_normed, inputs, recip, gain_attn.astype(F32))
        parts.append(owned(chip_summed(outer(normed, grad_qkv), grad_gain if final else None)))
    last_totals = totals_of([after(part, *second_totals) for part in parts[:-1]]) if rounds > 1 else []
    last_totals = last_totals + totals_of([after(parts[-1], *second_totals, *last_totals)])
    grad_inputs = (grad_middle + grad_in).astype(BF16)
    opened_last, grad_gain_attn = opened(last_totals[-1], True)
    opened_parts = [opened(total, False) for total in last_totals[:-1]] + [opened_last]
    grad_w_query, grad_w_key, grad_w_value = (
        jnp.concatenate(
            [
                part[:, which * part.shape[1] // 3 : (which + 1) * part.shape[1] // 3]
                for part in opened_parts
            ],
            1,
        )
        for which in range(3)
    )
    shape = (micros, 1, rows, width)
    return (
        result.reshape(shape),
        grad_inputs.reshape(shape),
        grad_gain_attn,
        grad_w_query,
        grad_w_key,
        grad_w_value,
        grad_w_out,
        grad_gain_mlp,
        grad_w_gate,
        grad_w_up,
        grad_w_down,
    )


def solution(mesh):
    weight, gain = P("fsdp", None), P("fsdp")
    rows = P(None, "fsdp", "ctx", None)
    weights = (gain, weight, weight, weight, weight, gain, weight, weight, weight)
    return jax.shard_map(
        body,
        mesh=mesh,
        in_specs=(rows, rows, P(None, "fsdp", None)) + weights,
        out_specs=(rows, rows) + weights,
        check_vma=False,
    )
```

```python
import functools
import math

import jax
import jax.numpy as jnp
from jax import lax
from jax.experimental import pallas as pl
from jax.experimental.pallas import tpu as pltpu
from jax.sharding import PartitionSpec as P

HEAD_DIM = 64
LANES = 128
EPS = 1e-05
NEG = -1e30
LOG2E = math.log2(math.e)
LN2 = math.log(2.0)
F32 = jnp.float32
BF16 = jnp.bfloat16


def dot_nt(left, right):
    return lax.dot_general(left, right, (((1,), (1,)), ((), ())), preferred_element_type=F32)


def dot_nn(left, right):
    return lax.dot_general(left, right, (((1,), (0,)), ((), ())), preferred_element_type=F32)


def dot_tn(left, right):
    return lax.dot_general(left, right, (((0,), (0,)), ((), ())), preferred_element_type=F32)


def lane_index(rows):
    return lax.broadcasted_iota(jnp.int32, (rows, LANES), 1)


def flip(tile):
    return pltpu.roll(tile, HEAD_DIM, 1)


def params(count):
    return pltpu.CompilerParams(
        dimension_semantics=("arbitrary",) * count, vmem_limit_bytes=60 * 1024 * 1024
    )


def full_block(shape):
    zeros = (0,) * len(shape)
    return pl.BlockSpec(shape, lambda *_: zeros)


def pack_pair(tile):
    count = tile.shape[0] // 2
    low = lane_index(count) < HEAD_DIM
    top, bottom = tile[:count], tile[count:]
    return (jnp.where(low, top, flip(bottom)), jnp.where(low, flip(top), bottom))


def unpack_pair(first, second):
    low = lane_index(first.shape[0]) < HEAD_DIM
    top = jnp.where(low, first, flip(second))
    bottom = jnp.where(low, flip(first), second)
    return jnp.concatenate([top, bottom], 0)


def turn(tile):
    near = (lane_index(tile.shape[0]) % HEAD_DIM) < HEAD_DIM // 2
    return jnp.where(
        near, pltpu.roll(tile, LANES - HEAD_DIM // 2, 1), pltpu.roll(tile, HEAD_DIM // 2, 1)
    )


def project_kernel(count, info, n_ref, c_ref, s_ref, *refs):
    *parts, out, w_ref = refs

    @pl.when((pl.program_id(0) == 0) & (pl.program_id(1) == 0))
    def _():
        if len(parts) == 1:
            w_ref[...] = parts[0][...]
            return
        own, near, far = parts
        deep, wide = near.shape
        side, core = info[0], info[1]
        mine = pl.ds(pl.multiple_of(side * deep, deep), deep)
        away = pl.ds(pl.multiple_of((1 - side) * deep, deep), deep)
        w_ref[mine, :] = own[...]
        w_ref[away, pl.ds(pl.multiple_of(core * wide, wide), wide)] = near[...]
        w_ref[away, pl.ds(pl.multiple_of((1 - core) * wide, wide), wide)] = far[...]

    joined = dot_nn(n_ref[...], w_ref[...])
    cos_table, sine_table = c_ref[...], s_ref[...]
    rows = n_ref.shape[0]
    span = count * HEAD_DIM
    low = lane_index(rows) < HEAD_DIM
    for pair in range(count // 2):
        first = pair * LANES
        q2, k2, v2 = (joined[:, part * span + first : part * span + first + LANES] for part in range(3))
        q2 = (q2 * cos_table + turn(q2) * sine_table) * (LOG2E * HEAD_DIM**-0.5)
        k2 = k2 * cos_table + turn(k2) * sine_table
        packed = pack_pair(q2)
        kv = (jnp.where(low, k2, flip(v2)), jnp.where(low, flip(k2), v2))
        for side in range(2):
            out[2 * pair + side, 0, :rows, :] = kv[side].astype(BF16)
            out[2 * pair + side, 0, rows:, :] = packed[side].astype(BF16)
    if count < out.shape[0]:
        out[count:] = jnp.zeros((out.shape[0] - count,) + out.shape[1:], BF16)


def project(span, count, micros, info, normed, cos_table, sine_table, parts):
    rows, width = normed.shape
    half = rows // (2 * micros)
    depth = half + half // 2
    wide = parts[0].shape[1]
    return pl.pallas_call(
        functools.partial(project_kernel, count),
        grid_spec=pltpu.PrefetchScalarGridSpec(
            num_scalar_prefetch=1,
            grid=(micros, 2),
            in_specs=[
                pl.BlockSpec((half, width), lambda m, i, *_: (2 * m + i, 0)),
                pl.BlockSpec((half, LANES), lambda m, i, *_: (2 * m + i, 0)),
                pl.BlockSpec((half, LANES), lambda m, i, *_: (2 * m + i, 0)),
            ]
            + [full_block(part.shape) for part in parts],
            out_specs=[
                pl.BlockSpec((span, 1, depth, LANES), lambda m, i, *_: (m, i, 0, 0)),
                full_block((width, wide)),
            ],
        ),
        out_shape=[
            jax.ShapeDtypeStruct((micros * span, 2, depth, LANES), BF16),
            jax.ShapeDtypeStruct((width, wide), BF16),
        ],
        compiler_params=params(2),
        cost_estimate=pl.CostEstimate(
            flops=2 * rows * width * wide, bytes_accessed=4 * rows * width, transcendentals=0
        ),
        name="project",
    )(info, normed, cos_table, sine_table, *parts)


def row_begins(starts_ref, positions):
    begins = jnp.zeros_like(positions)
    for index in range(starts_ref.shape[0]):
        start = starts_ref[index]
        begins = jnp.maximum(begins, jnp.where(positions >= start, start, 0))
    return begins


def unpack_one(packed, lanes_low):
    wide = packed.astype(F32)
    low = lane_index(wide.shape[0]) < HEAD_DIM
    keep = low if lanes_low else jnp.logical_not(low)
    turned = flip(wide)
    first, second = (wide, turned) if lanes_low else (turned, wide)
    return jnp.concatenate(
        [jnp.where(keep, first, 0.0), jnp.where(keep, second, 0.0)], 0
    ).astype(BF16)


def attend_kernel(info, starts, mine, other, o_ref, lse_ref):
    block = pl.program_id(0)
    core = info[0]
    lowest, inner = info[1 + 2 * block], info[2 + 2 * block]
    rows = mine.shape[1] * 2 // 3
    low = lane_index(rows) < HEAD_DIM
    queries = unpack_one(mine[block, rows:, :], True)
    row_pos = (2 * block + core) * rows + lax.broadcasted_iota(jnp.int32, (rows, 1), 0)
    begins = row_begins(starts, row_pos)
    lane_low = lane_index(2 * rows) < HEAD_DIM
    column = lax.broadcasted_iota(jnp.int32, (1, 2 * rows), 1)
    offsets = jnp.where(column < rows, column + core * rows, column - core * rows)

    def step(masked, index, carry):
        peak, acc = carry
        kv = jnp.concatenate([mine[index, :rows, :], other[index, :rows, :]], 0)
        ones_v = jnp.where(lane_low, jnp.ones_like(kv), kv)
        scores = dot_nt(queries, kv)
        if masked:
            key_pos = offsets + index * (2 * rows)
            scores = jnp.where((key_pos >= begins) & (key_pos <= row_pos), scores, NEG)
        new_peak = jnp.maximum(peak, jnp.max(scores, -1, keepdims=True))
        weights = jnp.exp2(scores - new_peak)
        acc = acc * jnp.exp2(peak - new_peak) + dot_nn(weights.astype(BF16), ones_v)
        return (new_peak, acc)

    carry = step(True, block, (jnp.full((rows, 1), NEG, F32), jnp.zeros((rows, LANES), F32)))
    carry = lax.fori_loop(lowest, inner, functools.partial(step, True), carry)
    peak, acc = lax.fori_loop(inner, block, functools.partial(step, False), carry)
    result = acc / flip(acc)
    count = rows // 2
    small_low = lane_index(count) < HEAD_DIM
    o_ref[0] = jnp.where(small_low, flip(result[:count]), result[count:]).astype(BF16)
    lse = jnp.where(low, peak + jnp.log2(acc), 0.0)
    lse_ref[0] = jnp.transpose(lse)[0:1, :]


def attend(info, starts, mine, other):
    blocks, depth, _ = mine.shape
    rows = depth * 2 // 3
    return pl.pallas_call(
        attend_kernel,
        grid_spec=pltpu.PrefetchScalarGridSpec(
            num_scalar_prefetch=2,
            grid=(blocks,),
            in_specs=[
                pl.BlockSpec(mine.shape, lambda i, *_: (0, 0, 0)),
                pl.BlockSpec(other.shape, lambda i, *_: (0, 0, 0)),
            ],
            out_specs=[
                pl.BlockSpec((1, rows // 2, LANES), lambda i, *_: (i, 0, 0)),
                pl.BlockSpec((1, 1, rows), lambda i, *_: (i, 0, 0)),
            ],
        ),
        out_shape=[
            jax.ShapeDtypeStruct((blocks, rows // 2, LANES), BF16),
            jax.ShapeDtypeStruct((blocks, 1, rows), F32),
        ],
        compiler_params=params(1),
        cost_estimate=pl.CostEstimate(
            flops=16 * 10**9, bytes_accessed=10**7, transcendentals=10**7
        ),
        name="attend",
    )(info, starts, mine, other)


def attend_grad_kernel(
    info, starts, mine, other, do_ref, o_ref, lse_ref, dm_ref, dp_ref, acc_mine, acc_other
):
    block = pl.program_id(0)
    core = info[0]
    lowest, inner = info[1 + 2 * block], info[2 + 2 * block]
    rows = mine.shape[1] * 2 // 3
    count = rows // 2

    @pl.when(block == 0)
    def _():
        acc_mine[...] = jnp.zeros_like(acc_mine)
        acc_other[...] = jnp.zeros_like(acc_other)

    queries = unpack_one(mine[block, rows:, :], True)
    grad_out = unpack_one(do_ref[0], False)
    both = jnp.concatenate([queries, grad_out], 0)
    product = jnp.transpose(do_ref[0].astype(F32) * o_ref[0].astype(F32))
    delta = jnp.concatenate(
        [
            jnp.sum(product[:HEAD_DIM], 0, keepdims=True),
            jnp.sum(product[HEAD_DIM:], 0, keepdims=True),
        ],
        1,
    )
    lse = lse_ref[0]
    row_pos = (2 * block + core) * rows + lax.broadcasted_iota(jnp.int32, (1, rows), 1)
    begins = row_begins(starts, row_pos)
    line = lax.broadcasted_iota(jnp.int32, (2 * rows, 1), 0)
    offsets = jnp.where(line < rows, line + core * rows, line - core * rows)

    def step(masked, index, grad_q):
        kv = jnp.concatenate([mine[index, :rows, :], other[index, :rows, :]], 0)
        scores = dot_nt(kv, queries)
        weights = jnp.exp2(scores - lse)
        if masked:
            key_pos = offsets + index * (2 * rows)
            weights = jnp.where((key_pos >= begins) & (key_pos <= row_pos), weights, 0.0)
        grad_weights = dot_nt(kv, grad_out)
        grad_scores = (weights * (grad_weights - delta)).astype(BF16)
        grad_kv = dot_nn(jnp.concatenate([grad_scores, weights.astype(BF16)], 1), both)
        acc_mine[index] += grad_kv[:rows]
        acc_other[index] += grad_kv[rows:]
        return grad_q + dot_tn(grad_scores, kv)

    grad_q = step(True, block, jnp.zeros((rows, LANES), F32))
    grad_q = lax.fori_loop(lowest, inner, functools.partial(step, True), grad_q)
    grad_q = lax.fori_loop(inner, block, functools.partial(step, False), grad_q)
    grad_q = grad_q * HEAD_DIM**-0.5
    small_low = lane_index(count) < HEAD_DIM
    dm_ref[block, rows:, :] = jnp.where(small_low, grad_q[:count], flip(grad_q[count:])).astype(
        BF16
    )

    @pl.when(block == pl.num_programs(0) - 1)
    def _():
        scale = jnp.where(lane_index(rows) < HEAD_DIM, LN2, 1.0)

        def flush(index, _):
            dm_ref[index, :rows, :] = (acc_mine[index] * scale).astype(BF16)
            dp_ref[index] = (acc_other[index] * scale).astype(BF16)
            return 0

        lax.fori_loop(0, mine.shape[0], flush, 0)


def attend_grad(info, starts, mine, other, grad_out, spot, out, lse):
    blocks, depth, _ = mine.shape
    rows = depth * 2 // 3
    whole = pl.BlockSpec(mine.shape, lambda i, *_: (0, 0, 0))
    small = pl.BlockSpec((1, rows // 2, LANES), lambda i, *_: (i, 0, 0))
    return pl.pallas_call(
        attend_grad_kernel,
        grid_spec=pltpu.PrefetchScalarGridSpec(
            num_scalar_prefetch=2,
            grid=(blocks,),
            in_specs=[
                whole,
                whole,
                pl.BlockSpec((1, rows // 2, LANES), lambda i, *_: (i, spot, 0)),
                small,
                pl.BlockSpec((1, 1, rows), lambda i, *_: (i, 0, 0)),
            ],
            out_specs=[whole, pl.BlockSpec((blocks, rows, LANES), lambda i, *_: (0, 0, 0))],
            scratch_shapes=[
                pltpu.VMEM((blocks, rows, LANES), F32),
                pltpu.VMEM((blocks, rows, LANES), F32),
            ],
        ),
        out_shape=[
            jax.ShapeDtypeStruct(mine.shape, BF16),
            jax.ShapeDtypeStruct((blocks, rows, LANES), BF16),
        ],
        compiler_params=params(1),
        cost_estimate=pl.CostEstimate(
            flops=32 * 10**9, bytes_accessed=10**7, transcendentals=10**7
        ),
        name="attend_grad",
    )(info, starts, mine, other, grad_out, out, lse)


def collect_kernel(counts, *refs):
    ins, out = refs[:-1], refs[-1]
    length = out.shape[0] // 2
    pieces = [(array, first) for array in ins for first in range(0, array.shape[2], length)]
    pair = 0
    for (array, first), count in zip(pieces, counts):
        cut = slice(first, first + length)
        for spot in range(0, count, 2):
            tiles = [array[spot + side, 0, cut, :].astype(F32) for side in range(2)]
            out[:, pair * LANES : (pair + 1) * LANES] = unpack_pair(*tiles).astype(BF16)
            pair += 1


def collect(counts, micros, arrays):
    units = arrays[0].shape[0]
    length = sum(array.shape[2] for array in arrays) // len(counts)
    width = sum(counts) * HEAD_DIM
    return pl.pallas_call(
        functools.partial(collect_kernel, counts),
        grid=(micros, 2),
        in_specs=[
            pl.BlockSpec((units // micros, 1, array.shape[2], LANES), lambda m, i: (m, i, 0, 0))
            for array in arrays
        ],
        out_specs=pl.BlockSpec((2 * length, width), lambda m, i: (2 * m + i, 0)),
        out_shape=jax.ShapeDtypeStruct((micros * 4 * length, width), BF16),
        compiler_params=params(2),
        cost_estimate=pl.CostEstimate(flops=0, bytes_accessed=4 * 10**6, transcendentals=0),
        name="collect",
    )(*arrays)


def spread_kernel(counts, x_ref, *outs):
    length = x_ref.shape[0] // 2
    pieces = [(out, first) for out in outs for first in range(0, out.shape[2], length)]
    pair = 0
    for (out, first), count in zip(pieces, counts):
        cut = slice(first, first + length)
        for spot in range(0, count, 2):
            tile = x_ref[:, pair * LANES : (pair + 1) * LANES].astype(F32)
            packed = pack_pair(tile)
            for side in range(2):
                out[spot + side, 0, cut, :] = packed[side].astype(BF16)
            pair += 1
        for spot in range(count, out.shape[0]):
            out[spot, 0, cut, :] = jnp.zeros((length, LANES), BF16)


def spread(span, counts, micros, rows_array):
    rows, width = rows_array.shape
    half = rows // (2 * micros)
    lengths = [half // 2] + ([half // 2 * (len(counts) - 1)] if len(counts) > 1 else [])
    return pl.pallas_call(
        functools.partial(spread_kernel, counts),
        grid=(micros, 2),
        in_specs=[pl.BlockSpec((half, width), lambda m, i: (2 * m + i, 0))],
        out_specs=[
            pl.BlockSpec((span, 1, length, LANES), lambda m, i: (m, i, 0, 0)) for length in lengths
        ],
        out_shape=[
            jax.ShapeDtypeStruct((micros * span, 2, length, LANES), BF16) for length in lengths
        ],
        compiler_params=params(2),
        cost_estimate=pl.CostEstimate(flops=0, bytes_accessed=4 * 10**6, transcendentals=0),
        name="spread",
    )(rows_array)


def turn_back(tile, cos_table, sine_table):
    near = (lane_index(tile.shape[0]) % HEAD_DIM) < HEAD_DIM // 2
    scaled = tile * sine_table
    moved = jnp.where(
        near,
        pltpu.roll(scaled, LANES - HEAD_DIM // 2, 1),
        pltpu.roll(scaled, HEAD_DIM // 2, 1),
    )
    return tile * cos_table + moved


def collect_grad_kernel(count, c_ref, s_ref, in_ref, out):
    cos_table, sine_table = c_ref[...], s_ref[...]
    rows = cos_table.shape[0]
    span = count * HEAD_DIM
    low = lane_index(rows) < HEAD_DIM
    for pair in range(count // 2):
        kvs = [in_ref[2 * pair + side, 0, :rows, :].astype(F32) for side in range(2)]
        packed = [in_ref[2 * pair + side, 0, rows:, :].astype(F32) for side in range(2)]
        grad_k = jnp.where(low, kvs[0], flip(kvs[1]))
        grad_v = jnp.where(low, flip(kvs[0]), kvs[1])
        grad_q = turn_back(unpack_pair(*packed), cos_table, sine_table)
        grad_k = turn_back(grad_k, cos_table, sine_table)
        for part, value in enumerate((grad_q, grad_k, grad_v)):
            first = part * span + pair * LANES
            out[:, first : first + LANES] = value.astype(BF16)


def collect_grad(count, micros, array, cos_table, sine_table):
    units, _, depth, _ = array.shape
    half = depth * 2 // 3
    width = 3 * count * HEAD_DIM
    table = pl.BlockSpec((half, LANES), lambda m, i: (2 * m + i, 0))
    return pl.pallas_call(
        functools.partial(collect_grad_kernel, count),
        grid=(micros, 2),
        in_specs=[
            table,
            table,
            pl.BlockSpec((units // micros, 1, depth, LANES), lambda m, i: (m, i, 0, 0)),
        ],
        out_specs=pl.BlockSpec((half, width), lambda m, i: (2 * m + i, 0)),
        out_shape=jax.ShapeDtypeStruct((micros * 2 * half, width), BF16),
        compiler_params=params(2),
        cost_estimate=pl.CostEstimate(flops=0, bytes_accessed=6 * 10**6, transcendentals=0),
        name="collect_grad",
    )(cos_table, sine_table, array)


def matmul(left, right):
    return jnp.dot(left, right, preferred_element_type=F32)


def norm_backward(grad_out, values, recip_rows, gain):
    scaled = grad_out * gain
    grad_in = recip_rows * scaled - values * (recip_rows * recip_rows * recip_rows) * jnp.mean(
        scaled * values, -1, keepdims=True
    )
    return (grad_in, jnp.sum(grad_out * values * recip_rows, 0))


def feed_forward(tokens, cotangent, attended, w_out, gain_mlp, w_gate, w_up, w_down):
    inputs = tokens.astype(F32)
    gain = gain_mlp.astype(F32)
    middle = inputs + matmul(attended, w_out)
    recip = lax.rsqrt(jnp.mean(middle * middle, -1, keepdims=True) + EPS)
    mlp_low = (middle * recip * gain).astype(BF16)
    gate_pre = matmul(mlp_low, w_gate)
    up_pre = matmul(mlp_low, w_up)
    gate_sigmoid = jax.nn.sigmoid(gate_pre)
    silu_value = gate_pre * gate_sigmoid
    hidden_low = (silu_value * up_pre).astype(BF16)
    result = (middle + matmul(hidden_low, w_down)).astype(BF16)
    grad_hidden = jnp.einsum("td,fd->tf", cotangent, w_down, preferred_element_type=F32)
    grad_gate = (
        grad_hidden * up_pre * gate_sigmoid * (1.0 + gate_pre * (1.0 - gate_sigmoid))
    ).astype(BF16)
    grad_up = (grad_hidden * silu_value).astype(BF16)
    grad_normed = jnp.einsum(
        "tf,df->td", grad_gate, w_gate, preferred_element_type=F32
    ) + jnp.einsum("tf,df->td", grad_up, w_up, preferred_element_type=F32)
    grad_mid, grad_gain = norm_backward(grad_normed, middle, recip, gain)
    grad_middle = cotangent.astype(F32) + grad_mid
    grad_branch = grad_middle.astype(BF16)
    grad_att = jnp.einsum("te,de->td", grad_branch, w_out, preferred_element_type=F32).astype(BF16)
    return result, grad_middle, grad_att, grad_gain, (
        (attended, grad_branch),
        (mlp_low, grad_gate),
        (mlp_low, grad_up),
        (hidden_low, cotangent),
    )


def outer(left, right):
    return jnp.einsum("td,te->de", left, right, preferred_element_type=F32).astype(BF16)


def after(value, *others):
    return lax.optimization_barrier((value,) + others)[0]


def body(
    tokens, cotangent, doc_lengths, gain_attn, w_query, w_key, w_value, w_out, gain_mlp, w_gate, w_up, w_down
):
    micros, _, rows, width = tokens.shape
    heads = width // HEAD_DIM
    devices = lax.axis_size("ctx")
    shards = lax.axis_size("fsdp")
    place = lax.axis_index("ctx")
    side = lax.axis_index("fsdp")
    chips = devices // 2
    core = place % 2
    half = rows // 2
    depth = half + half // 2
    span = chips // micros
    rounds = -(-heads // span)
    counts = tuple(min(span, heads - index * span) for index in range(rounds))
    swap = [(i, i ^ 1) for i in range(devices)]
    cross = [(0, 1), (1, 0)]

    def pick(array, index, axis):
        return lax.dynamic_index_in_dim(array, index, axis, keepdims=False)

    def gathered(shard):
        return lax.all_gather(shard, "fsdp", axis=0, tiled=True)

    def fetched(shard):
        if shards != 2:
            return [gathered(shard)]
        wide = shard.shape[1] // 2
        near = lax.dynamic_slice_in_dim(shard, core * wide, wide, 1)
        near = lax.ppermute(near, "fsdp", cross)
        return [shard, near, lax.ppermute(near, "ctx", swap)]

    def fetched_lines(lines):
        if shards != 2:
            return [gathered(line) for line in lines]
        lines = jnp.stack(lines)
        away = lax.ppermute(lines, "fsdp", cross)
        return jnp.where(
            side == 0, jnp.concatenate([lines, away], 1), jnp.concatenate([away, lines], 1)
        )

    def columns(index):
        cut = slice(index * span * HEAD_DIM, (index * span + counts[index]) * HEAD_DIM)
        return jnp.concatenate([w_query[:, cut], w_key[:, cut], w_value[:, cut]], 1)

    gain_attn, gain_mlp = fetched_lines([gain_attn, gain_mlp])
    weight_parts = [fetched(columns(index)) for index in range(rounds)]
    spot = jnp.stack([side, core]).astype(jnp.int32)
    w_out, w_gate, w_up, w_down = (gathered(shard) for shard in (w_out, w_gate, w_up, w_down))
    lengths = doc_lengths[:, 0]
    doc_ends = jnp.cumsum(lengths, -1)
    starts = (doc_ends - lengths).astype(jnp.int32)

    def begins_of(micro_starts, positions):
        reached = positions[:, None] >= micro_starts[None, :]
        return jnp.max(jnp.where(reached, micro_starts[None, :], 0), -1)

    lane = jnp.arange(LANES)
    inverse = jnp.power(10000.0, -(lane % (HEAD_DIM // 2)).astype(F32) / (HEAD_DIM // 2))
    sign = jnp.where((lane % HEAD_DIM) < HEAD_DIM // 2, -1.0, 1.0)
    positions = place * rows + jnp.arange(rows, dtype=jnp.int32)
    offsets = jnp.concatenate(
        [positions - begins_of(starts[micro], positions) for micro in range(micros)]
    ).astype(F32)
    angles = offsets[:, None] * inverse[None, :]
    cos_table, sine_table = jnp.cos(angles), jnp.sin(angles) * sign

    def exchange(buffer):
        return lax.all_to_all(buffer, "ctx", split_axis=0, concat_axis=0, tiled=True)

    tokens = tokens.reshape(micros * rows, width)
    cotangent = cotangent.reshape(micros * rows, width)
    inputs = tokens.astype(F32)
    recip = lax.rsqrt(jnp.mean(inputs * inputs, -1, keepdims=True) + EPS)
    normed = (inputs * recip * gain_attn.astype(F32)).astype(BF16)

    block = jnp.arange(devices, dtype=jnp.int32)
    block_first = block * rows + core * half
    chosen = pick(starts, place // 2 // span, 0)
    lowest = begins_of(chosen, block_first) // rows
    inner = jnp.minimum(-(-begins_of(chosen, block_first + half - 1) // rows), block)

    received, infos, others, attended_back, kept, in_weights = [], [], [], [], [], []
    for index in range(rounds):
        live = index * span + place // 2 % span < heads
        bounds = jnp.stack([jnp.where(live, lowest, block), jnp.where(live, inner, block)], 1)
        infos.append(jnp.concatenate([core[None], bounds.reshape(-1)]).astype(jnp.int32))
        buffer, weight = project(
            span, counts[index], micros, spot, normed, cos_table, sine_table, weight_parts[index]
        )
        in_weights.append(weight)
        buffer = buffer.reshape(devices, depth, LANES)
        if index >= 2:
            buffer = after(buffer, kept[index - 2][1])
        received.append(exchange(buffer))
        whole = received[index]
        if index:
            whole = after(whole, kept[index - 1][1])
        others.append(lax.ppermute(whole, "ctx", swap))
        out, lse = attend(infos[index], chosen, received[index], others[index])
        kept.append((out, lse))
    def came_back(pieces):
        joined = pieces[0] if len(pieces) == 1 else jnp.concatenate(pieces, 1)
        joined = exchange(joined)
        return joined.reshape((chips, 2) + joined.shape[1:])

    early = [after(out, received[-1]) for out, _ in kept[:-1]]
    attended_back = ([came_back(early)] if early else []) + [came_back([kept[-1][0]])]

    attended = collect(counts, micros, attended_back)
    result, grad_middle, grad_att, grad_gain_mlp, pairs = feed_forward(
        tokens, cotangent, attended, w_out, gain_mlp, w_gate, w_up, w_down
    )
    grads_in = [
        exchange(buffer.reshape((devices,) + buffer.shape[2:]))
        for buffer in spread(span, counts, micros, grad_att)
    ]

    def paired(stay, leave, axis, routes):
        return (stay.astype(F32) + lax.ppermute(leave, axis, routes).astype(F32)).astype(BF16)

    def chip_summed(full, gain=None):
        count, wide = full.shape[0] // (2 * shards), full.shape[1]
        parts = full.reshape(shards, 2, count, wide)
        if gain is not None:
            line = gain.astype(BF16).reshape(shards, 2, 1, -1)
            line = jnp.pad(line, ((0, 0), (0, 0), (0, 15), (0, wide - line.shape[-1])))
            parts = jnp.concatenate([parts, line], 2)
        return paired(pick(parts, core, 1), pick(parts, 1 - core, 1), "ctx", swap)

    def owned(parts):
        if shards == 2:
            return paired(pick(parts, side, 0), pick(parts, 1 - side, 0), "fsdp", cross)
        return lax.psum_scatter(parts, "fsdp", scatter_dimension=0, tiled=False)

    def spaced(part):
        return jnp.where((core == jnp.arange(2))[:, None, None], part[None], 0)

    def totals_of(parts):
        return list(lax.psum(tuple(parts), "ctx"))

    def opened(total, has_gain):
        wide = total.shape[-1]
        count = total.shape[1] - (16 if has_gain else 0)
        rows_part = total[:, :count].reshape(2 * count, wide).astype(F32)
        if not has_gain:
            return rows_part
        return rows_part, total[:, count, : width // (2 * shards)].reshape(-1).astype(F32)

    pair_out, pair_gate, pair_up, pair_down = pairs
    chip_down = chip_summed(outer(*pair_down))
    chip_gate = chip_summed(outer(*pair_gate))
    chip_up = chip_summed(outer(*pair_up))
    chip_out = chip_summed(outer(*pair_out), grad_gain_mlp)
    first_parts = [spaced(owned(chip_out)), spaced(owned(chip_down))]
    second_parts = [spaced(owned(chip_gate)), spaced(owned(chip_up))]
    first_totals = totals_of(first_parts)
    second_totals = totals_of([after(part, *first_totals) for part in second_parts])
    grad_w_out, grad_gain_mlp = opened(first_totals[0], True)
    grad_w_down = opened(first_totals[1], False)
    grad_w_gate, grad_w_up = (opened(total, False) for total in second_totals)

    grad_back, sent_back = [], []
    waits = {0: (chip_out, chip_down, chip_gate, chip_up), 1: tuple(first_parts), 2: (*second_parts, *first_totals)}
    for index in range(rounds):
        own, away = attend_grad(
            infos[index],
            chosen,
            received[index],
            others[index],
            after(
                grads_in[min(index, 1)], *waits.get(index, ()), *sent_back[-1:], *grad_back[-2:-1]
            ),
            max(index - 1, 0),
            *kept[index],
        )
        back = lax.ppermute(away, "ctx", swap)
        own_kv = (own[:, :half].astype(F32) + back.astype(F32)).astype(BF16)
        buffer = jnp.concatenate([own_kv, own[:, half:]], 1)
        sent_back.append(buffer)
        grad_back.append(exchange(buffer).reshape(chips, 2, depth, LANES))

    grad_back[0] = after(grad_back[0], *second_totals)
    grad_normed, parts = 0.0, []
    for index in range(rounds):
        grad_qkv = collect_grad(counts[index], micros, grad_back[index], cos_table, sine_table)
        grad_normed = grad_normed + jnp.einsum(
            "te,de->td", grad_qkv, in_weights[index], preferred_element_type=F32
        )
        final = index == rounds - 1
        if final:
            grad_in, grad_gain = norm_backward(grad_normed, inputs, recip, gain_attn.astype(F32))
        parts.append(
            spaced(owned(chip_summed(outer(normed, grad_qkv), grad_gain if final else None)))
        )
    last_totals = totals_of(parts[:-1]) if rounds > 1 else []
    last_totals = last_totals + totals_of([after(parts[-1], *last_totals)])
    grad_inputs = (grad_middle + grad_in).astype(BF16)
    opened_last, grad_gain_attn = opened(last_totals[-1], True)
    opened_parts = [opened(total, False) for total in last_totals[:-1]] + [opened_last]
    grad_w_query, grad_w_key, grad_w_value = (
        jnp.concatenate(
            [
                part[:, which * part.shape[1] // 3 : (which + 1) * part.shape[1] // 3]
                for part in opened_parts
            ],
            1,
        )
        for which in range(3)
    )
    shape = (micros, 1, rows, width)
    return (
        result.reshape(shape),
        grad_inputs.reshape(shape),
        grad_gain_attn,
        grad_w_query,
        grad_w_key,
        grad_w_value,
        grad_w_out,
        grad_gain_mlp,
        grad_w_gate,
        grad_w_up,
        grad_w_down,
    )


def solution(mesh):
    weight, gain = P("fsdp", None), P("fsdp")
    rows = P(None, "fsdp", "ctx", None)
    weights = (gain, weight, weight, weight, weight, gain, weight, weight, weight)
    return jax.shard_map(
        body,
        mesh=mesh,
        in_specs=(rows, rows, P(None, "fsdp", None)) + weights,
        out_specs=(rows, rows) + weights,
        check_vma=False,
    )
```

```python
import functools
import math

import jax
import jax.numpy as jnp
from jax import lax
from jax.experimental import pallas as pl
from jax.experimental.pallas import tpu as pltpu
from jax.sharding import PartitionSpec as P

HEAD_DIM = 64
LANES = 128
EPS = 1e-05
NEG = -1e30
LOG2E = math.log2(math.e)
LN2 = math.log(2.0)
F32 = jnp.float32
BF16 = jnp.bfloat16


def dot_nt(left, right):
    return lax.dot_general(left, right, (((1,), (1,)), ((), ())), preferred_element_type=F32)


def dot_nn(left, right):
    return lax.dot_general(left, right, (((1,), (0,)), ((), ())), preferred_element_type=F32)


def dot_tn(left, right):
    return lax.dot_general(left, right, (((0,), (0,)), ((), ())), preferred_element_type=F32)


def lane_index(rows):
    return lax.broadcasted_iota(jnp.int32, (rows, LANES), 1)


def flip(tile):
    return pltpu.roll(tile, HEAD_DIM, 1)


def params(count):
    return pltpu.CompilerParams(
        dimension_semantics=("arbitrary",) * count, vmem_limit_bytes=60 * 1024 * 1024
    )


def full_block(shape):
    zeros = (0,) * len(shape)
    return pl.BlockSpec(shape, lambda *_: zeros)


def pack_pair(tile):
    count = tile.shape[0] // 2
    low = lane_index(count) < HEAD_DIM
    top, bottom = tile[:count], tile[count:]
    return (jnp.where(low, top, flip(bottom)), jnp.where(low, flip(top), bottom))


def unpack_pair(first, second):
    low = lane_index(first.shape[0]) < HEAD_DIM
    top = jnp.where(low, first, flip(second))
    bottom = jnp.where(low, flip(first), second)
    return jnp.concatenate([top, bottom], 0)


def turn(tile):
    near = (lane_index(tile.shape[0]) % HEAD_DIM) < HEAD_DIM // 2
    return jnp.where(
        near, pltpu.roll(tile, LANES - HEAD_DIM // 2, 1), pltpu.roll(tile, HEAD_DIM // 2, 1)
    )


def project_kernel(count, info, n_ref, c_ref, s_ref, *refs):
    *parts, out, w_ref = refs

    @pl.when((pl.program_id(0) == 0) & (pl.program_id(1) == 0))
    def _():
        if len(parts) == 1:
            w_ref[...] = parts[0][...]
            return
        own, near, far = parts
        deep, wide = near.shape
        side, core = info[0], info[1]
        mine = pl.ds(pl.multiple_of(side * deep, deep), deep)
        away = pl.ds(pl.multiple_of((1 - side) * deep, deep), deep)
        w_ref[mine, :] = own[...]
        w_ref[away, pl.ds(pl.multiple_of(core * wide, wide), wide)] = near[...]
        w_ref[away, pl.ds(pl.multiple_of((1 - core) * wide, wide), wide)] = far[...]

    joined = dot_nn(n_ref[...], w_ref[...])
    cos_table, sine_table = c_ref[...], s_ref[...]
    rows = n_ref.shape[0]
    span = count * HEAD_DIM
    low = lane_index(rows) < HEAD_DIM
    for pair in range(count // 2):
        first = pair * LANES
        q2, k2, v2 = (joined[:, part * span + first : part * span + first + LANES] for part in range(3))
        q2 = (q2 * cos_table + turn(q2) * sine_table) * (LOG2E * HEAD_DIM**-0.5)
        k2 = k2 * cos_table + turn(k2) * sine_table
        packed = pack_pair(q2)
        kv = (jnp.where(low, k2, flip(v2)), jnp.where(low, flip(k2), v2))
        for side in range(2):
            out[2 * pair + side, 0, :rows, :] = kv[side].astype(BF16)
            out[2 * pair + side, 0, rows:, :] = packed[side].astype(BF16)
    if count < out.shape[0]:
        out[count:] = jnp.zeros((out.shape[0] - count,) + out.shape[1:], BF16)


def project(span, count, micros, info, normed, cos_table, sine_table, parts):
    rows, width = normed.shape
    half = rows // (2 * micros)
    depth = half + half // 2
    wide = parts[0].shape[1]
    return pl.pallas_call(
        functools.partial(project_kernel, count),
        grid_spec=pltpu.PrefetchScalarGridSpec(
            num_scalar_prefetch=1,
            grid=(micros, 2),
            in_specs=[
                pl.BlockSpec((half, width), lambda m, i, *_: (2 * m + i, 0)),
                pl.BlockSpec((half, LANES), lambda m, i, *_: (2 * m + i, 0)),
                pl.BlockSpec((half, LANES), lambda m, i, *_: (2 * m + i, 0)),
            ]
            + [full_block(part.shape) for part in parts],
            out_specs=[
                pl.BlockSpec((span, 1, depth, LANES), lambda m, i, *_: (m, i, 0, 0)),
                full_block((width, wide)),
            ],
        ),
        out_shape=[
            jax.ShapeDtypeStruct((micros * span, 2, depth, LANES), BF16),
            jax.ShapeDtypeStruct((width, wide), BF16),
        ],
        compiler_params=params(2),
        cost_estimate=pl.CostEstimate(
            flops=2 * rows * width * wide, bytes_accessed=4 * rows * width, transcendentals=0
        ),
        name="project",
    )(info, normed, cos_table, sine_table, *parts)


def row_begins(starts_ref, positions):
    begins = jnp.zeros_like(positions)
    for index in range(starts_ref.shape[0]):
        start = starts_ref[index]
        begins = jnp.maximum(begins, jnp.where(positions >= start, start, 0))
    return begins


def unpack_one(packed, lanes_low):
    wide = packed.astype(F32)
    low = lane_index(wide.shape[0]) < HEAD_DIM
    keep = low if lanes_low else jnp.logical_not(low)
    turned = flip(wide)
    first, second = (wide, turned) if lanes_low else (turned, wide)
    return jnp.concatenate(
        [jnp.where(keep, first, 0.0), jnp.where(keep, second, 0.0)], 0
    ).astype(BF16)


def attend_kernel(info, starts, mine, other, o_ref, lse_ref):
    block = pl.program_id(0)
    core = info[0]
    lowest, inner = info[1 + 2 * block], info[2 + 2 * block]
    rows = mine.shape[1] * 2 // 3
    low = lane_index(rows) < HEAD_DIM
    queries = unpack_one(mine[block, rows:, :], True)
    row_pos = (2 * block + core) * rows + lax.broadcasted_iota(jnp.int32, (rows, 1), 0)
    begins = row_begins(starts, row_pos)
    lane_low = lane_index(2 * rows) < HEAD_DIM
    column = lax.broadcasted_iota(jnp.int32, (1, 2 * rows), 1)
    offsets = jnp.where(column < rows, column + core * rows, column - core * rows)

    def step(masked, index, carry):
        peak, acc = carry
        kv = jnp.concatenate([mine[index, :rows, :], other[index, :rows, :]], 0)
        ones_v = jnp.where(lane_low, jnp.ones_like(kv), kv)
        scores = dot_nt(queries, kv)
        if masked:
            key_pos = offsets + index * (2 * rows)
            scores = jnp.where((key_pos >= begins) & (key_pos <= row_pos), scores, NEG)
        new_peak = jnp.maximum(peak, jnp.max(scores, -1, keepdims=True))
        weights = jnp.exp2(scores - new_peak)
        acc = acc * jnp.exp2(peak - new_peak) + dot_nn(weights.astype(BF16), ones_v)
        return (new_peak, acc)

    carry = step(True, block, (jnp.full((rows, 1), NEG, F32), jnp.zeros((rows, LANES), F32)))
    carry = lax.fori_loop(lowest, inner, functools.partial(step, True), carry)
    peak, acc = lax.fori_loop(inner, block, functools.partial(step, False), carry)
    result = acc / flip(acc)
    count = rows // 2
    small_low = lane_index(count) < HEAD_DIM
    o_ref[0] = jnp.where(small_low, flip(result[:count]), result[count:]).astype(BF16)
    lse = jnp.where(low, peak + jnp.log2(acc), 0.0)
    lse_ref[0] = jnp.transpose(lse)[0:1, :]


def attend(info, starts, mine, other):
    blocks, depth, _ = mine.shape
    rows = depth * 2 // 3
    return pl.pallas_call(
        attend_kernel,
        grid_spec=pltpu.PrefetchScalarGridSpec(
            num_scalar_prefetch=2,
            grid=(blocks,),
            in_specs=[
                pl.BlockSpec(mine.shape, lambda i, *_: (0, 0, 0)),
                pl.BlockSpec(other.shape, lambda i, *_: (0, 0, 0)),
            ],
            out_specs=[
                pl.BlockSpec((1, rows // 2, LANES), lambda i, *_: (i, 0, 0)),
                pl.BlockSpec((1, 1, rows), lambda i, *_: (i, 0, 0)),
            ],
        ),
        out_shape=[
            jax.ShapeDtypeStruct((blocks, rows // 2, LANES), BF16),
            jax.ShapeDtypeStruct((blocks, 1, rows), F32),
        ],
        compiler_params=params(1),
        cost_estimate=pl.CostEstimate(
            flops=16 * 10**9, bytes_accessed=10**7, transcendentals=10**7
        ),
        name="attend",
    )(info, starts, mine, other)


def attend_grad_kernel(
    info, starts, mine, other, do_ref, o_ref, lse_ref, dm_ref, dp_ref, acc_mine, acc_other
):
    block = pl.program_id(0)
    core = info[0]
    lowest, inner = info[1 + 2 * block], info[2 + 2 * block]
    rows = mine.shape[1] * 2 // 3
    count = rows // 2

    @pl.when(block == 0)
    def _():
        acc_mine[...] = jnp.zeros_like(acc_mine)
        acc_other[...] = jnp.zeros_like(acc_other)

    queries = unpack_one(mine[block, rows:, :], True)
    grad_out = unpack_one(do_ref[0], False)
    both = jnp.concatenate([queries, grad_out], 0)
    product = jnp.transpose(do_ref[0].astype(F32) * o_ref[0].astype(F32))
    delta = jnp.concatenate(
        [
            jnp.sum(product[:HEAD_DIM], 0, keepdims=True),
            jnp.sum(product[HEAD_DIM:], 0, keepdims=True),
        ],
        1,
    )
    lse = lse_ref[0]
    row_pos = (2 * block + core) * rows + lax.broadcasted_iota(jnp.int32, (1, rows), 1)
    begins = row_begins(starts, row_pos)
    line = lax.broadcasted_iota(jnp.int32, (2 * rows, 1), 0)
    offsets = jnp.where(line < rows, line + core * rows, line - core * rows)

    def step(masked, index, grad_q):
        kv = jnp.concatenate([mine[index, :rows, :], other[index, :rows, :]], 0)
        scores = dot_nt(kv, queries)
        weights = jnp.exp2(scores - lse)
        if masked:
            key_pos = offsets + index * (2 * rows)
            weights = jnp.where((key_pos >= begins) & (key_pos <= row_pos), weights, 0.0)
        grad_weights = dot_nt(kv, grad_out)
        grad_scores = (weights * (grad_weights - delta)).astype(BF16)
        grad_kv = dot_nn(jnp.concatenate([grad_scores, weights.astype(BF16)], 1), both)
        acc_mine[index] += grad_kv[:rows]
        acc_other[index] += grad_kv[rows:]
        return grad_q + dot_tn(grad_scores, kv)

    grad_q = step(True, block, jnp.zeros((rows, LANES), F32))
    grad_q = lax.fori_loop(lowest, inner, functools.partial(step, True), grad_q)
    grad_q = lax.fori_loop(inner, block, functools.partial(step, False), grad_q)
    grad_q = grad_q * HEAD_DIM**-0.5
    small_low = lane_index(count) < HEAD_DIM
    dm_ref[block, rows:, :] = jnp.where(small_low, grad_q[:count], flip(grad_q[count:])).astype(
        BF16
    )

    @pl.when(block == pl.num_programs(0) - 1)
    def _():
        scale = jnp.where(lane_index(rows) < HEAD_DIM, LN2, 1.0)

        def flush(index, _):
            dm_ref[index, :rows, :] = (acc_mine[index] * scale).astype(BF16)
            dp_ref[index] = (acc_other[index] * scale).astype(BF16)
            return 0

        lax.fori_loop(0, mine.shape[0], flush, 0)


def attend_grad(info, starts, mine, other, grad_out, spot, out, lse):
    blocks, depth, _ = mine.shape
    rows = depth * 2 // 3
    whole = pl.BlockSpec(mine.shape, lambda i, *_: (0, 0, 0))
    small = pl.BlockSpec((1, rows // 2, LANES), lambda i, *_: (i, 0, 0))
    return pl.pallas_call(
        attend_grad_kernel,
        grid_spec=pltpu.PrefetchScalarGridSpec(
            num_scalar_prefetch=2,
            grid=(blocks,),
            in_specs=[
                whole,
                whole,
                pl.BlockSpec((1, rows // 2, LANES), lambda i, *_: (i, spot, 0)),
                small,
                pl.BlockSpec((1, 1, rows), lambda i, *_: (i, 0, 0)),
            ],
            out_specs=[whole, pl.BlockSpec((blocks, rows, LANES), lambda i, *_: (0, 0, 0))],
            scratch_shapes=[
                pltpu.VMEM((blocks, rows, LANES), F32),
                pltpu.VMEM((blocks, rows, LANES), F32),
            ],
        ),
        out_shape=[
            jax.ShapeDtypeStruct(mine.shape, BF16),
            jax.ShapeDtypeStruct((blocks, rows, LANES), BF16),
        ],
        compiler_params=params(1),
        cost_estimate=pl.CostEstimate(
            flops=32 * 10**9, bytes_accessed=10**7, transcendentals=10**7
        ),
        name="attend_grad",
    )(info, starts, mine, other, grad_out, out, lse)


def collect_kernel(counts, *refs):
    ins, out = refs[:-1], refs[-1]
    length = out.shape[0] // 2
    pieces = [(array, first) for array in ins for first in range(0, array.shape[2], length)]
    pair = 0
    for (array, first), count in zip(pieces, counts):
        cut = slice(first, first + length)
        for spot in range(0, count, 2):
            tiles = [array[spot + side, 0, cut, :].astype(F32) for side in range(2)]
            out[:, pair * LANES : (pair + 1) * LANES] = unpack_pair(*tiles).astype(BF16)
            pair += 1


def collect(counts, micros, arrays):
    units = arrays[0].shape[0]
    length = sum(array.shape[2] for array in arrays) // len(counts)
    width = sum(counts) * HEAD_DIM
    return pl.pallas_call(
        functools.partial(collect_kernel, counts),
        grid=(micros, 2),
        in_specs=[
            pl.BlockSpec((units // micros, 1, array.shape[2], LANES), lambda m, i: (m, i, 0, 0))
            for array in arrays
        ],
        out_specs=pl.BlockSpec((2 * length, width), lambda m, i: (2 * m + i, 0)),
        out_shape=jax.ShapeDtypeStruct((micros * 4 * length, width), BF16),
        compiler_params=params(2),
        cost_estimate=pl.CostEstimate(flops=0, bytes_accessed=4 * 10**6, transcendentals=0),
        name="collect",
    )(*arrays)


def spread_kernel(counts, x_ref, *outs):
    length = x_ref.shape[0] // 2
    pieces = [(out, first) for out in outs for first in range(0, out.shape[2], length)]
    pair = 0
    for (out, first), count in zip(pieces, counts):
        cut = slice(first, first + length)
        for spot in range(0, count, 2):
            tile = x_ref[:, pair * LANES : (pair + 1) * LANES].astype(F32)
            packed = pack_pair(tile)
            for side in range(2):
                out[spot + side, 0, cut, :] = packed[side].astype(BF16)
            pair += 1
        for spot in range(count, out.shape[0]):
            out[spot, 0, cut, :] = jnp.zeros((length, LANES), BF16)


def spread(span, counts, micros, rows_array):
    rows, width = rows_array.shape
    half = rows // (2 * micros)
    lengths = [half // 2] + ([half // 2 * (len(counts) - 1)] if len(counts) > 1 else [])
    return pl.pallas_call(
        functools.partial(spread_kernel, counts),
        grid=(micros, 2),
        in_specs=[pl.BlockSpec((half, width), lambda m, i: (2 * m + i, 0))],
        out_specs=[
            pl.BlockSpec((span, 1, length, LANES), lambda m, i: (m, i, 0, 0)) for length in lengths
        ],
        out_shape=[
            jax.ShapeDtypeStruct((micros * span, 2, length, LANES), BF16) for length in lengths
        ],
        compiler_params=params(2),
        cost_estimate=pl.CostEstimate(flops=0, bytes_accessed=4 * 10**6, transcendentals=0),
        name="spread",
    )(rows_array)


def turn_back(tile, cos_table, sine_table):
    near = (lane_index(tile.shape[0]) % HEAD_DIM) < HEAD_DIM // 2
    scaled = tile * sine_table
    moved = jnp.where(
        near,
        pltpu.roll(scaled, LANES - HEAD_DIM // 2, 1),
        pltpu.roll(scaled, HEAD_DIM // 2, 1),
    )
    return tile * cos_table + moved


def collect_grad_kernel(count, c_ref, s_ref, in_ref, out):
    cos_table, sine_table = c_ref[...], s_ref[...]
    rows = cos_table.shape[0]
    span = count * HEAD_DIM
    low = lane_index(rows) < HEAD_DIM
    for pair in range(count // 2):
        kvs = [in_ref[2 * pair + side, 0, :rows, :].astype(F32) for side in range(2)]
        packed = [in_ref[2 * pair + side, 0, rows:, :].astype(F32) for side in range(2)]
        grad_k = jnp.where(low, kvs[0], flip(kvs[1]))
        grad_v = jnp.where(low, flip(kvs[0]), kvs[1])
        grad_q = turn_back(unpack_pair(*packed), cos_table, sine_table)
        grad_k = turn_back(grad_k, cos_table, sine_table)
        for part, value in enumerate((grad_q, grad_k, grad_v)):
            first = part * span + pair * LANES
            out[:, first : first + LANES] = value.astype(BF16)


def collect_grad(count, micros, array, cos_table, sine_table):
    units, _, depth, _ = array.shape
    half = depth * 2 // 3
    width = 3 * count * HEAD_DIM
    table = pl.BlockSpec((half, LANES), lambda m, i: (2 * m + i, 0))
    return pl.pallas_call(
        functools.partial(collect_grad_kernel, count),
        grid=(micros, 2),
        in_specs=[
            table,
            table,
            pl.BlockSpec((units // micros, 1, depth, LANES), lambda m, i: (m, i, 0, 0)),
        ],
        out_specs=pl.BlockSpec((half, width), lambda m, i: (2 * m + i, 0)),
        out_shape=jax.ShapeDtypeStruct((micros * 2 * half, width), BF16),
        compiler_params=params(2),
        cost_estimate=pl.CostEstimate(flops=0, bytes_accessed=6 * 10**6, transcendentals=0),
        name="collect_grad",
    )(cos_table, sine_table, array)


SUM_STEPS = 6
PLANE_Z, PLANE_Y, FAR_Z, TWIN = 4, 2, 8, 1


def add_rows(out, left, right):
    def step(index, _):
        cut = pl.ds(pl.multiple_of(index * 16, 16), 16)
        out[cut, :] = (left[cut, :].astype(F32) + right[cut, :].astype(F32)).astype(BF16)
        return 0

    lax.fori_loop(0, out.shape[0] // 16, step, 0)


def ctx_sum_kernel(count, *refs):
    ins, outs = refs[:count], refs[count : 2 * count]
    halves, quarters, sums, fars = (refs[(2 + k) * count : (3 + k) * count] for k in range(4))
    send_sems, recv_sems = refs[6 * count :]
    place = lax.axis_index("ctx")
    side = lax.axis_index("fsdp")

    def bit(weight):
        return place // weight % 2

    def partner(weight):
        return (place + weight * (1 - 2 * bit(weight)), side)

    barrier = pltpu.get_barrier_semaphore()
    for weight in (PLANE_Z, PLANE_Y, FAR_Z, TWIN):
        pl.semaphore_signal(
            barrier, inc=1, device_id=partner(weight), device_id_type=pl.DeviceIdType.MESH
        )
    pl.semaphore_wait(barrier, 4)

    def send(index, step, source, target, weight):
        copy = pltpu.make_async_remote_copy(
            src_ref=source,
            dst_ref=target,
            send_sem=send_sems.at[index, step],
            recv_sem=recv_sems.at[index, step],
            device_id=partner(weight),
            device_id_type=pl.DeviceIdType.MESH,
        )
        copy.start()
        return copy

    axes = [(PLANE_Z, PLANE_Y) if index % 2 == 0 else (PLANE_Y, PLANE_Z) for index in range(count)]
    core = bit(TWIN)
    started = []
    for index, (first, second) in enumerate(axes):
        leave = ins[index].at[pl.ds(2 * (1 - bit(first)), 2)]
        started.append(send(index, 0, leave, halves[index], first))
    copies = list(started)
    for index, (first, second) in enumerate(axes):
        started[index].wait_recv()
        for part in range(2):
            half = halves[index].at[part]
            add_rows(half, ins[index].at[2 * bit(first) + part], half)
        leave = halves[index].at[1 - bit(second)]
        started[index] = send(index, 1, leave, quarters[index], second)
    copies += started
    for index, (first, second) in enumerate(axes):
        started[index].wait_recv()
        add_rows(sums[index], halves[index].at[bit(second)], quarters[index])
        started[index] = send(index, 2, sums[index], fars[index], FAR_Z)
    copies += started
    for index, (first, second) in enumerate(axes):
        started[index].wait_recv()
        spot = outs[index].at[core, 2 * bit(first) + bit(second)]
        add_rows(spot, sums[index], fars[index])
        started[index] = send(index, 3, spot, spot, second)
    copies += started
    for index, (first, second) in enumerate(axes):
        started[index].wait_recv()
        spot = outs[index].at[core, pl.ds(2 * bit(first), 2)]
        started[index] = send(index, 4, spot, spot, first)
    copies += started
    for index in range(count):
        started[index].wait_recv()
        spot = outs[index].at[core]
        started[index] = send(index, 5, spot, spot, TWIN)
    copies += started
    for index in range(count):
        started[index].wait_recv()
    for copy in copies:
        copy.wait_send()


def ctx_sum(parts):
    count = len(parts)
    shapes = [(part.shape[0] // 4, part.shape[1]) for part in parts]
    sent = sum(6 * part.size for part in parts)
    vmem = pl.BlockSpec(memory_space=pltpu.VMEM)
    totals = pl.pallas_call(
        functools.partial(ctx_sum_kernel, count),
        in_specs=[vmem] * count,
        out_specs=[vmem] * count,
        out_shape=[jax.ShapeDtypeStruct((2, 4) + shape, BF16) for shape in shapes],
        scratch_shapes=[pltpu.VMEM((2,) + shape, BF16) for shape in shapes]
        + [pltpu.VMEM(shape, BF16) for shape in shapes] * 3
        + [pltpu.SemaphoreType.DMA((count, SUM_STEPS))] * 2,
        compiler_params=pltpu.CompilerParams(
            collective_id=0, has_side_effects=True, vmem_limit_bytes=60 * 1024 * 1024
        ),
        cost_estimate=pl.CostEstimate(flops=0, bytes_accessed=4 * sent, transcendentals=0),
        name="ctx_sum",
    )(*[part.reshape((4,) + shape) for part, shape in zip(parts, shapes)])
    return [total.reshape((2,) + part.shape) for total, part in zip(totals, parts)]


def matmul(left, right):
    return jnp.dot(left, right, preferred_element_type=F32)


def norm_backward(grad_out, values, recip_rows, gain):
    scaled = grad_out * gain
    grad_in = recip_rows * scaled - values * (recip_rows * recip_rows * recip_rows) * jnp.mean(
        scaled * values, -1, keepdims=True
    )
    return (grad_in, jnp.sum(grad_out * values * recip_rows, 0))


def feed_forward(tokens, cotangent, attended, w_out, gain_mlp, w_gate, w_up, w_down):
    inputs = tokens.astype(F32)
    gain = gain_mlp.astype(F32)
    middle = inputs + matmul(attended, w_out)
    recip = lax.rsqrt(jnp.mean(middle * middle, -1, keepdims=True) + EPS)
    mlp_low = (middle * recip * gain).astype(BF16)
    gate_pre = matmul(mlp_low, w_gate)
    up_pre = matmul(mlp_low, w_up)
    gate_sigmoid = jax.nn.sigmoid(gate_pre)
    silu_value = gate_pre * gate_sigmoid
    hidden_low = (silu_value * up_pre).astype(BF16)
    result = (middle + matmul(hidden_low, w_down)).astype(BF16)
    grad_hidden = jnp.einsum("td,fd->tf", cotangent, w_down, preferred_element_type=F32)
    grad_gate = (
        grad_hidden * up_pre * gate_sigmoid * (1.0 + gate_pre * (1.0 - gate_sigmoid))
    ).astype(BF16)
    grad_up = (grad_hidden * silu_value).astype(BF16)
    grad_normed = jnp.einsum(
        "tf,df->td", grad_gate, w_gate, preferred_element_type=F32
    ) + jnp.einsum("tf,df->td", grad_up, w_up, preferred_element_type=F32)
    grad_mid, grad_gain = norm_backward(grad_normed, middle, recip, gain)
    grad_middle = cotangent.astype(F32) + grad_mid
    grad_branch = grad_middle.astype(BF16)
    grad_att = jnp.einsum("te,de->td", grad_branch, w_out, preferred_element_type=F32).astype(BF16)
    return result, grad_middle, grad_att, grad_gain, (
        (attended, grad_branch),
        (mlp_low, grad_gate),
        (mlp_low, grad_up),
        (hidden_low, cotangent),
    )


def outer(left, right):
    return jnp.einsum("td,te->de", left, right, preferred_element_type=F32).astype(BF16)


def after(value, *others):
    return lax.optimization_barrier((value,) + others)[0]


def body(
    tokens, cotangent, doc_lengths, gain_attn, w_query, w_key, w_value, w_out, gain_mlp, w_gate, w_up, w_down
):
    micros, _, rows, width = tokens.shape
    heads = width // HEAD_DIM
    devices = lax.axis_size("ctx")
    shards = lax.axis_size("fsdp")
    place = lax.axis_index("ctx")
    side = lax.axis_index("fsdp")
    chips = devices // 2
    core = place % 2
    half = rows // 2
    depth = half + half // 2
    span = chips // micros
    rounds = -(-heads // span)
    counts = tuple(min(span, heads - index * span) for index in range(rounds))
    swap = [(i, i ^ 1) for i in range(devices)]
    cross = [(0, 1), (1, 0)]

    def pick(array, index, axis):
        return lax.dynamic_index_in_dim(array, index, axis, keepdims=False)

    def gathered(shard):
        return lax.all_gather(shard, "fsdp", axis=0, tiled=True)

    def fetched(shard):
        if shards != 2:
            return [gathered(shard)]
        wide = shard.shape[1] // 2
        near = lax.dynamic_slice_in_dim(shard, core * wide, wide, 1)
        near = lax.ppermute(near, "fsdp", cross)
        return [shard, near, lax.ppermute(near, "ctx", swap)]

    def fetched_lines(lines):
        if shards != 2:
            return [gathered(line) for line in lines]
        lines = jnp.stack(lines)
        away = lax.ppermute(lines, "fsdp", cross)
        return jnp.where(
            side == 0, jnp.concatenate([lines, away], 1), jnp.concatenate([away, lines], 1)
        )

    def columns(index):
        cut = slice(index * span * HEAD_DIM, (index * span + counts[index]) * HEAD_DIM)
        return jnp.concatenate([w_query[:, cut], w_key[:, cut], w_value[:, cut]], 1)

    gain_attn, gain_mlp = fetched_lines([gain_attn, gain_mlp])
    weight_parts = [fetched(columns(index)) for index in range(rounds)]
    spot = jnp.stack([side, core]).astype(jnp.int32)
    w_out, w_gate, w_up, w_down = (gathered(shard) for shard in (w_out, w_gate, w_up, w_down))
    lengths = doc_lengths[:, 0]
    doc_ends = jnp.cumsum(lengths, -1)
    starts = (doc_ends - lengths).astype(jnp.int32)

    def begins_of(micro_starts, positions):
        reached = positions[:, None] >= micro_starts[None, :]
        return jnp.max(jnp.where(reached, micro_starts[None, :], 0), -1)

    lane = jnp.arange(LANES)
    inverse = jnp.power(10000.0, -(lane % (HEAD_DIM // 2)).astype(F32) / (HEAD_DIM // 2))
    sign = jnp.where((lane % HEAD_DIM) < HEAD_DIM // 2, -1.0, 1.0)
    positions = place * rows + jnp.arange(rows, dtype=jnp.int32)
    offsets = jnp.concatenate(
        [positions - begins_of(starts[micro], positions) for micro in range(micros)]
    ).astype(F32)
    angles = offsets[:, None] * inverse[None, :]
    cos_table, sine_table = jnp.cos(angles), jnp.sin(angles) * sign

    def exchange(buffer):
        return lax.all_to_all(buffer, "ctx", split_axis=0, concat_axis=0, tiled=True)

    tokens = tokens.reshape(micros * rows, width)
    cotangent = cotangent.reshape(micros * rows, width)
    inputs = tokens.astype(F32)
    recip = lax.rsqrt(jnp.mean(inputs * inputs, -1, keepdims=True) + EPS)
    normed = (inputs * recip * gain_attn.astype(F32)).astype(BF16)

    block = jnp.arange(devices, dtype=jnp.int32)
    block_first = block * rows + core * half
    chosen = pick(starts, place // 2 // span, 0)
    lowest = begins_of(chosen, block_first) // rows
    inner = jnp.minimum(-(-begins_of(chosen, block_first + half - 1) // rows), block)

    received, infos, others, attended_back, kept, in_weights = [], [], [], [], [], []
    for index in range(rounds):
        live = index * span + place // 2 % span < heads
        bounds = jnp.stack([jnp.where(live, lowest, block), jnp.where(live, inner, block)], 1)
        infos.append(jnp.concatenate([core[None], bounds.reshape(-1)]).astype(jnp.int32))
        buffer, weight = project(
            span, counts[index], micros, spot, normed, cos_table, sine_table, weight_parts[index]
        )
        in_weights.append(weight)
        buffer = buffer.reshape(devices, depth, LANES)
        if index >= 2:
            buffer = after(buffer, kept[index - 2][1])
        received.append(exchange(buffer))
        whole = received[index]
        if index:
            whole = after(whole, kept[index - 1][1])
        others.append(lax.ppermute(whole, "ctx", swap))
        out, lse = attend(infos[index], chosen, received[index], others[index])
        kept.append((out, lse))
    def came_back(pieces):
        joined = pieces[0] if len(pieces) == 1 else jnp.concatenate(pieces, 1)
        joined = exchange(joined)
        return joined.reshape((chips, 2) + joined.shape[1:])

    early = [after(out, received[-1]) for out, _ in kept[:-1]]
    attended_back = ([came_back(early)] if early else []) + [came_back([kept[-1][0]])]

    attended = collect(counts, micros, attended_back)
    result, grad_middle, grad_att, grad_gain_mlp, pairs = feed_forward(
        tokens, cotangent, attended, w_out, gain_mlp, w_gate, w_up, w_down
    )
    grads_in = [
        exchange(buffer.reshape((devices,) + buffer.shape[2:]))
        for buffer in spread(span, counts, micros, grad_att)
    ]

    def paired(stay, leave, axis, routes):
        return (stay.astype(F32) + lax.ppermute(leave, axis, routes).astype(F32)).astype(BF16)

    def chip_summed(full, gain=None):
        count, wide = full.shape[0] // (2 * shards), full.shape[1]
        parts = full.reshape(shards, 2, count, wide)
        if gain is not None:
            line = gain.astype(BF16).reshape(shards, 2, 1, -1)
            line = jnp.pad(line, ((0, 0), (0, 0), (0, 63), (0, wide - line.shape[-1])))
            parts = jnp.concatenate([parts, line], 2)
        return paired(pick(parts, core, 1), pick(parts, 1 - core, 1), "ctx", swap)

    def owned(parts):
        if shards == 2:
            return paired(pick(parts, side, 0), pick(parts, 1 - side, 0), "fsdp", cross)
        return lax.psum_scatter(parts, "fsdp", scatter_dimension=0, tiled=False)

    def spaced(part):
        return jnp.where((core == jnp.arange(2))[:, None, None], part[None], 0)

    def totals_of(parts):
        if devices == 16:
            return ctx_sum(parts)
        return list(lax.psum(tuple(spaced(part) for part in parts), "ctx"))

    def opened(total, has_gain):
        wide = total.shape[-1]
        count = total.shape[1] - (64 if has_gain else 0)
        rows_part = total[:, :count].reshape(2 * count, wide).astype(F32)
        if not has_gain:
            return rows_part
        return rows_part, total[:, count, : width // (2 * shards)].reshape(-1).astype(F32)

    pair_out, pair_gate, pair_up, pair_down = pairs
    chip_down = chip_summed(outer(*pair_down))
    chip_gate = chip_summed(outer(*pair_gate))
    chip_up = chip_summed(outer(*pair_up))
    chip_out = chip_summed(outer(*pair_out), grad_gain_mlp)
    mid_parts = [owned(chip) for chip in (chip_out, chip_down, chip_gate, chip_up)]

    grad_back, sent_back = [], []
    waits = {0: (chip_out, chip_down, chip_gate, chip_up), 1: tuple(mid_parts)}
    for index in range(rounds):
        own, away = attend_grad(
            infos[index],
            chosen,
            received[index],
            others[index],
            after(
                grads_in[min(index, 1)], *waits.get(index, ()), *sent_back[-1:], *grad_back[-2:-1]
            ),
            max(index - 1, 0),
            *kept[index],
        )
        back = lax.ppermute(away, "ctx", swap)
        own_kv = (own[:, :half].astype(F32) + back.astype(F32)).astype(BF16)
        buffer = jnp.concatenate([own_kv, own[:, half:]], 1)
        sent_back.append(buffer)
        grad_back.append(exchange(buffer).reshape(chips, 2, depth, LANES))

    grad_normed, parts = 0.0, []
    for index in range(rounds):
        grad_qkv = collect_grad(counts[index], micros, grad_back[index], cos_table, sine_table)
        grad_normed = grad_normed + jnp.einsum(
            "te,de->td", grad_qkv, in_weights[index], preferred_element_type=F32
        )
        final = index == rounds - 1
        if final:
            grad_in, grad_gain = norm_backward(grad_normed, inputs, recip, gain_attn.astype(F32))
        parts.append(owned(chip_summed(outer(normed, grad_qkv), grad_gain if final else None)))
    totals = totals_of(mid_parts + parts)
    mid_totals, last_totals = totals[: len(mid_parts)], totals[len(mid_parts) :]
    grad_w_out, grad_gain_mlp = opened(mid_totals[0], True)
    grad_w_down, grad_w_gate, grad_w_up = (opened(total, False) for total in mid_totals[1:])
    grad_inputs = (grad_middle + grad_in).astype(BF16)
    opened_last, grad_gain_attn = opened(last_totals[-1], True)
    opened_parts = [opened(total, False) for total in last_totals[:-1]] + [opened_last]
    grad_w_query, grad_w_key, grad_w_value = (
        jnp.concatenate(
            [
                part[:, which * part.shape[1] // 3 : (which + 1) * part.shape[1] // 3]
                for part in opened_parts
            ],
            1,
        )
        for which in range(3)
    )
    shape = (micros, 1, rows, width)
    return (
        result.reshape(shape),
        grad_inputs.reshape(shape),
        grad_gain_attn,
        grad_w_query,
        grad_w_key,
        grad_w_value,
        grad_w_out,
        grad_gain_mlp,
        grad_w_gate,
        grad_w_up,
        grad_w_down,
    )


def solution(mesh):
    weight, gain = P("fsdp", None), P("fsdp")
    rows = P(None, "fsdp", "ctx", None)
    weights = (gain, weight, weight, weight, weight, gain, weight, weight, weight)
    return jax.shard_map(
        body,
        mesh=mesh,
        in_specs=(rows, rows, P(None, "fsdp", None)) + weights,
        out_specs=(rows, rows) + weights,
        check_vma=False,
    )
```

```python
import functools
import math

import jax
import jax.numpy as jnp
from jax import lax
from jax.experimental import pallas as pl
from jax.experimental.pallas import tpu as pltpu
from jax.sharding import PartitionSpec as P

HEAD_DIM = 64
LANES = 128
EPS = 1e-05
NEG = -1e30
LOG2E = math.log2(math.e)
LN2 = math.log(2.0)
F32 = jnp.float32
BF16 = jnp.bfloat16


def dot_nt(left, right):
    return lax.dot_general(left, right, (((1,), (1,)), ((), ())), preferred_element_type=F32)


def dot_nn(left, right):
    return lax.dot_general(left, right, (((1,), (0,)), ((), ())), preferred_element_type=F32)


def dot_tn(left, right):
    return lax.dot_general(left, right, (((0,), (0,)), ((), ())), preferred_element_type=F32)


def lane_index(rows):
    return lax.broadcasted_iota(jnp.int32, (rows, LANES), 1)


def flip(tile):
    return pltpu.roll(tile, HEAD_DIM, 1)


def params(count):
    return pltpu.CompilerParams(
        dimension_semantics=("arbitrary",) * count, vmem_limit_bytes=60 * 1024 * 1024
    )


def full_block(shape):
    zeros = (0,) * len(shape)
    return pl.BlockSpec(shape, lambda *_: zeros)


def pack_pair(tile):
    count = tile.shape[0] // 2
    low = lane_index(count) < HEAD_DIM
    top, bottom = tile[:count], tile[count:]
    return (jnp.where(low, top, flip(bottom)), jnp.where(low, flip(top), bottom))


def unpack_pair(first, second):
    low = lane_index(first.shape[0]) < HEAD_DIM
    top = jnp.where(low, first, flip(second))
    bottom = jnp.where(low, flip(first), second)
    return jnp.concatenate([top, bottom], 0)


def turn(tile):
    near = (lane_index(tile.shape[0]) % HEAD_DIM) < HEAD_DIM // 2
    return jnp.where(
        near, pltpu.roll(tile, LANES - HEAD_DIM // 2, 1), pltpu.roll(tile, HEAD_DIM // 2, 1)
    )


def project_kernel(count, info, n_ref, c_ref, s_ref, *refs):
    *parts, out, w_ref = refs

    @pl.when((pl.program_id(0) == 0) & (pl.program_id(1) == 0))
    def _():
        if len(parts) == 1:
            w_ref[...] = parts[0][...]
            return
        own, near, far = parts
        deep, wide = near.shape
        side, core = info[0], info[1]
        mine = pl.ds(pl.multiple_of(side * deep, deep), deep)
        away = pl.ds(pl.multiple_of((1 - side) * deep, deep), deep)
        w_ref[mine, :] = own[...]
        w_ref[away, pl.ds(pl.multiple_of(core * wide, wide), wide)] = near[...]
        w_ref[away, pl.ds(pl.multiple_of((1 - core) * wide, wide), wide)] = far[...]

    joined = dot_nn(n_ref[...], w_ref[...])
    cos_table, sine_table = c_ref[...], s_ref[...]
    rows = n_ref.shape[0]
    span = count * HEAD_DIM
    low = lane_index(rows) < HEAD_DIM
    for pair in range(count // 2):
        first = pair * LANES
        q2, k2, v2 = (joined[:, part * span + first : part * span + first + LANES] for part in range(3))
        q2 = (q2 * cos_table + turn(q2) * sine_table) * (LOG2E * HEAD_DIM**-0.5)
        k2 = k2 * cos_table + turn(k2) * sine_table
        packed = pack_pair(q2)
        kv = (jnp.where(low, k2, flip(v2)), jnp.where(low, flip(k2), v2))
        for side in range(2):
            out[2 * pair + side, 0, :rows, :] = kv[side].astype(BF16)
            out[2 * pair + side, 0, rows:, :] = packed[side].astype(BF16)
    if count < out.shape[0]:
        out[count:] = jnp.zeros((out.shape[0] - count,) + out.shape[1:], BF16)


def project(span, count, micros, info, normed, cos_table, sine_table, parts, column):
    rows, width = normed.shape
    half = rows // (2 * micros)
    depth = half + half // 2
    wide = parts[0].shape[1]
    return pl.pallas_call(
        functools.partial(project_kernel, count),
        grid_spec=pltpu.PrefetchScalarGridSpec(
            num_scalar_prefetch=1,
            grid=(micros, 2),
            in_specs=[
                pl.BlockSpec((half, width), lambda m, i, *_: (2 * m + i, 0)),
                pl.BlockSpec((half, LANES), lambda m, i, *_: (2 * m + i, 0)),
                pl.BlockSpec((half, LANES), lambda m, i, *_: (2 * m + i, 0)),
            ]
            + [full_block(part.shape) for part in parts[:1]]
            + [
                pl.BlockSpec((part.shape[0], wide // 2), lambda m, i, *_: (0, column))
                for part in parts[1:]
            ],
            out_specs=[
                pl.BlockSpec((span, 1, depth, LANES), lambda m, i, *_: (m, i, 0, 0)),
                full_block((width, wide)),
            ],
        ),
        out_shape=[
            jax.ShapeDtypeStruct((micros * span, 2, depth, LANES), BF16),
            jax.ShapeDtypeStruct((width, wide), BF16),
        ],
        compiler_params=params(2),
        cost_estimate=pl.CostEstimate(
            flops=2 * rows * width * wide, bytes_accessed=4 * rows * width, transcendentals=0
        ),
        name="project",
    )(info, normed, cos_table, sine_table, *parts)


def row_begins(starts_ref, positions):
    begins = jnp.zeros_like(positions)
    for index in range(starts_ref.shape[0]):
        start = starts_ref[index]
        begins = jnp.maximum(begins, jnp.where(positions >= start, start, 0))
    return begins


def unpack_one(packed, lanes_low):
    wide = packed.astype(F32)
    low = lane_index(wide.shape[0]) < HEAD_DIM
    keep = low if lanes_low else jnp.logical_not(low)
    turned = flip(wide)
    first, second = (wide, turned) if lanes_low else (turned, wide)
    return jnp.concatenate(
        [jnp.where(keep, first, 0.0), jnp.where(keep, second, 0.0)], 0
    ).astype(BF16)


def attend_kernel(info, starts, mine, other, o_ref, lse_ref):
    block = pl.program_id(0)
    core = info[0]
    lowest, inner = info[1 + 2 * block], info[2 + 2 * block]
    rows = mine.shape[1] * 2 // 3
    low = lane_index(rows) < HEAD_DIM
    queries = unpack_one(mine[block, rows:, :], True)
    row_pos = (2 * block + core) * rows + lax.broadcasted_iota(jnp.int32, (rows, 1), 0)
    begins = row_begins(starts, row_pos)
    lane_low = lane_index(2 * rows) < HEAD_DIM
    column = lax.broadcasted_iota(jnp.int32, (1, 2 * rows), 1)
    offsets = jnp.where(column < rows, column + core * rows, column - core * rows)

    def step(masked, index, carry):
        peak, acc = carry
        kv = jnp.concatenate([mine[index, :rows, :], other[index, :rows, :]], 0)
        ones_v = jnp.where(lane_low, jnp.ones_like(kv), kv)
        scores = dot_nt(queries, kv)
        if masked:
            key_pos = offsets + index * (2 * rows)
            scores = jnp.where((key_pos >= begins) & (key_pos <= row_pos), scores, NEG)
        new_peak = jnp.maximum(peak, jnp.max(scores, -1, keepdims=True))
        weights = jnp.exp2(scores - new_peak)
        acc = acc * jnp.exp2(peak - new_peak) + dot_nn(weights.astype(BF16), ones_v)
        return (new_peak, acc)

    carry = step(True, block, (jnp.full((rows, 1), NEG, F32), jnp.zeros((rows, LANES), F32)))
    carry = lax.fori_loop(lowest, inner, functools.partial(step, True), carry)
    peak, acc = lax.fori_loop(inner, block, functools.partial(step, False), carry)
    result = acc / flip(acc)
    count = rows // 2
    small_low = lane_index(count) < HEAD_DIM
    o_ref[0] = jnp.where(small_low, flip(result[:count]), result[count:]).astype(BF16)
    lse = jnp.where(low, peak + jnp.log2(acc), 0.0)
    lse_ref[0] = jnp.transpose(lse)[0:1, :]


def attend(info, starts, mine, other):
    blocks, depth, _ = mine.shape
    rows = depth * 2 // 3
    return pl.pallas_call(
        attend_kernel,
        grid_spec=pltpu.PrefetchScalarGridSpec(
            num_scalar_prefetch=2,
            grid=(blocks,),
            in_specs=[
                pl.BlockSpec(mine.shape, lambda i, *_: (0, 0, 0)),
                pl.BlockSpec(other.shape, lambda i, *_: (0, 0, 0)),
            ],
            out_specs=[
                pl.BlockSpec((1, rows // 2, LANES), lambda i, *_: (i, 0, 0)),
                pl.BlockSpec((1, 1, rows), lambda i, *_: (i, 0, 0)),
            ],
        ),
        out_shape=[
            jax.ShapeDtypeStruct((blocks, rows // 2, LANES), BF16),
            jax.ShapeDtypeStruct((blocks, 1, rows), F32),
        ],
        compiler_params=params(1),
        cost_estimate=pl.CostEstimate(
            flops=16 * 10**9, bytes_accessed=10**7, transcendentals=10**7
        ),
        name="attend",
    )(info, starts, mine, other)


def attend_grad_kernel(
    info, starts, mine, other, do_ref, o_ref, lse_ref, dm_ref, dp_ref, acc_mine, acc_other
):
    block = pl.program_id(0)
    core = info[0]
    lowest, inner = info[1 + 2 * block], info[2 + 2 * block]
    rows = mine.shape[1] * 2 // 3
    count = rows // 2

    @pl.when(block == 0)
    def _():
        acc_mine[...] = jnp.zeros_like(acc_mine)
        acc_other[...] = jnp.zeros_like(acc_other)

    queries = unpack_one(mine[block, rows:, :], True)
    grad_out = unpack_one(do_ref[0], False)
    both = jnp.concatenate([queries, grad_out], 0)
    product = jnp.transpose(do_ref[0].astype(F32) * o_ref[0].astype(F32))
    delta = jnp.concatenate(
        [
            jnp.sum(product[:HEAD_DIM], 0, keepdims=True),
            jnp.sum(product[HEAD_DIM:], 0, keepdims=True),
        ],
        1,
    )
    lse = lse_ref[0]
    row_pos = (2 * block + core) * rows + lax.broadcasted_iota(jnp.int32, (1, rows), 1)
    begins = row_begins(starts, row_pos)
    line = lax.broadcasted_iota(jnp.int32, (2 * rows, 1), 0)
    offsets = jnp.where(line < rows, line + core * rows, line - core * rows)

    def step(masked, index, grad_q):
        kv = jnp.concatenate([mine[index, :rows, :], other[index, :rows, :]], 0)
        scores = dot_nt(kv, queries)
        weights = jnp.exp2(scores - lse)
        if masked:
            key_pos = offsets + index * (2 * rows)
            weights = jnp.where((key_pos >= begins) & (key_pos <= row_pos), weights, 0.0)
        grad_weights = dot_nt(kv, grad_out)
        grad_scores = (weights * (grad_weights - delta)).astype(BF16)
        grad_kv = dot_nn(jnp.concatenate([grad_scores, weights.astype(BF16)], 1), both)
        acc_mine[index] += grad_kv[:rows]
        acc_other[index] += grad_kv[rows:]
        return grad_q + dot_tn(grad_scores, kv)

    grad_q = step(True, block, jnp.zeros((rows, LANES), F32))
    grad_q = lax.fori_loop(lowest, inner, functools.partial(step, True), grad_q)
    grad_q = lax.fori_loop(inner, block, functools.partial(step, False), grad_q)
    grad_q = grad_q * HEAD_DIM**-0.5
    small_low = lane_index(count) < HEAD_DIM
    dm_ref[block, rows:, :] = jnp.where(small_low, grad_q[:count], flip(grad_q[count:])).astype(
        BF16
    )

    @pl.when(block == pl.num_programs(0) - 1)
    def _():
        scale = jnp.where(lane_index(rows) < HEAD_DIM, LN2, 1.0)

        def flush(index, _):
            dm_ref[index, :rows, :] = (acc_mine[index] * scale).astype(BF16)
            dp_ref[index] = (acc_other[index] * scale).astype(BF16)
            return 0

        lax.fori_loop(0, mine.shape[0], flush, 0)


def attend_grad(info, starts, mine, other, grad_out, spot, out, lse):
    blocks, depth, _ = mine.shape
    rows = depth * 2 // 3
    whole = pl.BlockSpec(mine.shape, lambda i, *_: (0, 0, 0))
    small = pl.BlockSpec((1, rows // 2, LANES), lambda i, *_: (i, 0, 0))
    return pl.pallas_call(
        attend_grad_kernel,
        grid_spec=pltpu.PrefetchScalarGridSpec(
            num_scalar_prefetch=2,
            grid=(blocks,),
            in_specs=[
                whole,
                whole,
                pl.BlockSpec((1, rows // 2, LANES), lambda i, *_: (i, spot, 0)),
                small,
                pl.BlockSpec((1, 1, rows), lambda i, *_: (i, 0, 0)),
            ],
            out_specs=[whole, pl.BlockSpec((blocks, rows, LANES), lambda i, *_: (0, 0, 0))],
            scratch_shapes=[
                pltpu.VMEM((blocks, rows, LANES), F32),
                pltpu.VMEM((blocks, rows, LANES), F32),
            ],
        ),
        out_shape=[
            jax.ShapeDtypeStruct(mine.shape, BF16),
            jax.ShapeDtypeStruct((blocks, rows, LANES), BF16),
        ],
        compiler_params=params(1),
        cost_estimate=pl.CostEstimate(
            flops=32 * 10**9, bytes_accessed=10**7, transcendentals=10**7
        ),
        name="attend_grad",
    )(info, starts, mine, other, grad_out, out, lse)


def merge_kernel(own_ref, back_ref, out):
    rows = back_ref.shape[1]
    out[:, :rows, :] = (own_ref[:, :rows, :].astype(F32) + back_ref[...].astype(F32)).astype(BF16)
    out[:, rows:, :] = own_ref[:, rows:, :]


def merge(own, back):
    blocks, depth, _ = own.shape
    step = blocks // 4
    spec = pl.BlockSpec((step, depth, LANES), lambda i: (i, 0, 0))
    return pl.pallas_call(
        merge_kernel,
        grid=(4,),
        in_specs=[spec, pl.BlockSpec((step, back.shape[1], LANES), lambda i: (i, 0, 0))],
        out_specs=spec,
        out_shape=jax.ShapeDtypeStruct(own.shape, BF16),
        compiler_params=params(1),
        cost_estimate=pl.CostEstimate(flops=0, bytes_accessed=4 * 10**6, transcendentals=0),
        name="merge",
    )(own, back)


def collect_kernel(counts, *refs):
    ins, out = refs[:-1], refs[-1]
    length = out.shape[0] // 2
    pieces = [(array, first) for array in ins for first in range(0, array.shape[2], length)]
    pair = 0
    for (array, first), count in zip(pieces, counts):
        cut = slice(first, first + length)
        for spot in range(0, count, 2):
            tiles = [array[spot + side, 0, cut, :].astype(F32) for side in range(2)]
            out[:, pair * LANES : (pair + 1) * LANES] = unpack_pair(*tiles).astype(BF16)
            pair += 1


def collect(counts, micros, arrays):
    units = arrays[0].shape[0]
    length = sum(array.shape[2] for array in arrays) // len(counts)
    width = sum(counts) * HEAD_DIM
    return pl.pallas_call(
        functools.partial(collect_kernel, counts),
        grid=(micros, 2),
        in_specs=[
            pl.BlockSpec((units // micros, 1, array.shape[2], LANES), lambda m, i: (m, i, 0, 0))
            for array in arrays
        ],
        out_specs=pl.BlockSpec((2 * length, width), lambda m, i: (2 * m + i, 0)),
        out_shape=jax.ShapeDtypeStruct((micros * 4 * length, width), BF16),
        compiler_params=params(2),
        cost_estimate=pl.CostEstimate(flops=0, bytes_accessed=4 * 10**6, transcendentals=0),
        name="collect",
    )(*arrays)


def spread_kernel(counts, x_ref, *outs):
    length = x_ref.shape[0] // 2
    pieces = [(out, first) for out in outs for first in range(0, out.shape[2], length)]
    pair = 0
    for (out, first), count in zip(pieces, counts):
        cut = slice(first, first + length)
        for spot in range(0, count, 2):
            tile = x_ref[:, pair * LANES : (pair + 1) * LANES].astype(F32)
            packed = pack_pair(tile)
            for side in range(2):
                out[spot + side, 0, cut, :] = packed[side].astype(BF16)
            pair += 1
        for spot in range(count, out.shape[0]):
            out[spot, 0, cut, :] = jnp.zeros((length, LANES), BF16)


def spread(span, counts, micros, rows_array):
    rows, width = rows_array.shape
    half = rows // (2 * micros)
    lengths = [half // 2] + ([half // 2 * (len(counts) - 1)] if len(counts) > 1 else [])
    return pl.pallas_call(
        functools.partial(spread_kernel, counts),
        grid=(micros, 2),
        in_specs=[pl.BlockSpec((half, width), lambda m, i: (2 * m + i, 0))],
        out_specs=[
            pl.BlockSpec((span, 1, length, LANES), lambda m, i: (m, i, 0, 0)) for length in lengths
        ],
        out_shape=[
            jax.ShapeDtypeStruct((micros * span, 2, length, LANES), BF16) for length in lengths
        ],
        compiler_params=params(2),
        cost_estimate=pl.CostEstimate(flops=0, bytes_accessed=4 * 10**6, transcendentals=0),
        name="spread",
    )(rows_array)


def turn_back(tile, cos_table, sine_table):
    near = (lane_index(tile.shape[0]) % HEAD_DIM) < HEAD_DIM // 2
    scaled = tile * sine_table
    moved = jnp.where(
        near,
        pltpu.roll(scaled, LANES - HEAD_DIM // 2, 1),
        pltpu.roll(scaled, HEAD_DIM // 2, 1),
    )
    return tile * cos_table + moved


def collect_grad_kernel(count, c_ref, s_ref, in_ref, out):
    cos_table, sine_table = c_ref[...], s_ref[...]
    rows = cos_table.shape[0]
    span = count * HEAD_DIM
    low = lane_index(rows) < HEAD_DIM
    for pair in range(count // 2):
        kvs = [in_ref[2 * pair + side, 0, :rows, :].astype(F32) for side in range(2)]
        packed = [in_ref[2 * pair + side, 0, rows:, :].astype(F32) for side in range(2)]
        grad_k = jnp.where(low, kvs[0], flip(kvs[1]))
        grad_v = jnp.where(low, flip(kvs[0]), kvs[1])
        grad_q = turn_back(unpack_pair(*packed), cos_table, sine_table)
        grad_k = turn_back(grad_k, cos_table, sine_table)
        for part, value in enumerate((grad_q, grad_k, grad_v)):
            first = part * span + pair * LANES
            out[:, first : first + LANES] = value.astype(BF16)


def collect_grad(count, micros, array, cos_table, sine_table):
    units, _, depth, _ = array.shape
    half = depth * 2 // 3
    width = 3 * count * HEAD_DIM
    table = pl.BlockSpec((half, LANES), lambda m, i: (2 * m + i, 0))
    return pl.pallas_call(
        functools.partial(collect_grad_kernel, count),
        grid=(micros, 2),
        in_specs=[
            table,
            table,
            pl.BlockSpec((units // micros, 1, depth, LANES), lambda m, i: (m, i, 0, 0)),
        ],
        out_specs=pl.BlockSpec((half, width), lambda m, i: (2 * m + i, 0)),
        out_shape=jax.ShapeDtypeStruct((micros * 2 * half, width), BF16),
        compiler_params=params(2),
        cost_estimate=pl.CostEstimate(flops=0, bytes_accessed=6 * 10**6, transcendentals=0),
        name="collect_grad",
    )(cos_table, sine_table, array)


SUM_STEPS = 6
PLANE_Z, PLANE_Y, FAR_Z, TWIN = 4, 2, 8, 1


def add_rows(out, left, right):
    def step(index, _):
        cut = pl.ds(pl.multiple_of(index * 16, 16), 16)
        out[cut, :] = (left[cut, :].astype(F32) + right[cut, :].astype(F32)).astype(BF16)
        return 0

    lax.fori_loop(0, out.shape[0] // 16, step, 0)


def ctx_sum_kernel(count, *refs):
    ins, outs = refs[:count], refs[count : 2 * count]
    halves, quarters, sums, fars = (refs[(2 + k) * count : (3 + k) * count] for k in range(4))
    send_sems, recv_sems = refs[6 * count :]
    place = lax.axis_index("ctx")
    side = lax.axis_index("fsdp")

    def bit(weight):
        return place // weight % 2

    def partner(weight):
        return (place + weight * (1 - 2 * bit(weight)), side)

    barrier = pltpu.get_barrier_semaphore()
    for weight in (PLANE_Z, PLANE_Y, FAR_Z, TWIN):
        pl.semaphore_signal(
            barrier, inc=1, device_id=partner(weight), device_id_type=pl.DeviceIdType.MESH
        )
    pl.semaphore_wait(barrier, 4)

    def send(index, step, source, target, weight):
        copy = pltpu.make_async_remote_copy(
            src_ref=source,
            dst_ref=target,
            send_sem=send_sems.at[index, step],
            recv_sem=recv_sems.at[index, step],
            device_id=partner(weight),
            device_id_type=pl.DeviceIdType.MESH,
        )
        copy.start()
        return copy

    axes = [(PLANE_Z, PLANE_Y) if index % 4 == 2 else (PLANE_Y, PLANE_Z) for index in range(count)]
    core = bit(TWIN)
    started, copies = {}, []

    def stage(index, step):
        first, second = axes[index]
        if step:
            started[index].wait_recv()
        if step == 0:
            leave = ins[index].at[pl.ds(2 * (1 - bit(first)), 2)]
            target, weight = halves[index], first
        elif step == 1:
            for part in range(2):
                half = halves[index].at[part]
                add_rows(half, ins[index].at[2 * bit(first) + part], half)
            leave, target, weight = halves[index].at[1 - bit(second)], quarters[index], second
        elif step == 2:
            add_rows(sums[index], halves[index].at[bit(second)], quarters[index])
            leave, target, weight = sums[index], fars[index], FAR_Z
        elif step == 3:
            leave = target = outs[index].at[core, 2 * bit(first) + bit(second)]
            weight = second
            add_rows(leave, sums[index], fars[index])
        elif step == 4:
            leave = target = outs[index].at[core, pl.ds(2 * bit(first), 2)]
            weight = first
        elif step == 5:
            leave = target = outs[index].at[core]
            weight = TWIN
        if step < SUM_STEPS:
            started[index] = send(index, step, leave, target, weight)
            copies.append(started[index])

    for time in range(count + SUM_STEPS + 1):
        if time < count:
            stage(time, 0)
        for step in reversed(range(1, SUM_STEPS + 1)):
            if 0 <= time - step - 1 < count:
                stage(time - step - 1, step)
    for copy in copies:
        copy.wait_send()


def ctx_sum(parts):
    count = len(parts)
    shapes = [(part.shape[0] // 4, part.shape[1]) for part in parts]
    sent = sum(6 * part.size for part in parts)
    vmem = pl.BlockSpec(memory_space=pltpu.VMEM)
    totals = pl.pallas_call(
        functools.partial(ctx_sum_kernel, count),
        in_specs=[vmem] * count,
        out_specs=[vmem] * count,
        out_shape=[jax.ShapeDtypeStruct((2, 4) + shape, BF16) for shape in shapes],
        scratch_shapes=[pltpu.VMEM((2,) + shape, BF16) for shape in shapes]
        + [pltpu.VMEM(shape, BF16) for shape in shapes] * 3
        + [pltpu.SemaphoreType.DMA((count, SUM_STEPS))] * 2,
        compiler_params=pltpu.CompilerParams(
            collective_id=0, has_side_effects=True, vmem_limit_bytes=60 * 1024 * 1024
        ),
        cost_estimate=pl.CostEstimate(flops=0, bytes_accessed=4 * sent, transcendentals=0),
        name="ctx_sum",
    )(*[part.reshape((4,) + shape) for part, shape in zip(parts, shapes)])
    return [total.reshape((2,) + part.shape) for total, part in zip(totals, parts)]


def matmul(left, right):
    return jnp.dot(left, right, preferred_element_type=F32)


def norm_backward(grad_out, values, recip_rows, gain):
    scaled = grad_out * gain
    grad_in = recip_rows * scaled - values * (recip_rows * recip_rows * recip_rows) * jnp.mean(
        scaled * values, -1, keepdims=True
    )
    return (grad_in, jnp.sum(grad_out * values * recip_rows, 0))


def feed_forward(tokens, cotangent, attended, w_out, gain_mlp, w_gate, w_up, w_down):
    inputs = tokens.astype(F32)
    gain = gain_mlp.astype(F32)
    middle = inputs + matmul(attended, w_out)
    recip = lax.rsqrt(jnp.mean(middle * middle, -1, keepdims=True) + EPS)
    mlp_low = (middle * recip * gain).astype(BF16)
    gate_pre = matmul(mlp_low, w_gate)
    up_pre = matmul(mlp_low, w_up)
    gate_sigmoid = jax.nn.sigmoid(gate_pre)
    silu_value = gate_pre * gate_sigmoid
    hidden_low = (silu_value * up_pre).astype(BF16)
    result = (middle + matmul(hidden_low, w_down)).astype(BF16)
    grad_hidden = jnp.einsum("td,fd->tf", cotangent, w_down, preferred_element_type=F32)
    grad_gate = (
        grad_hidden * up_pre * gate_sigmoid * (1.0 + gate_pre * (1.0 - gate_sigmoid))
    ).astype(BF16)
    grad_up = (grad_hidden * silu_value).astype(BF16)
    grad_normed = jnp.einsum(
        "tf,df->td", grad_gate, w_gate, preferred_element_type=F32
    ) + jnp.einsum("tf,df->td", grad_up, w_up, preferred_element_type=F32)
    grad_mid, grad_gain = norm_backward(grad_normed, middle, recip, gain)
    grad_middle = cotangent.astype(F32) + grad_mid
    grad_branch = grad_middle.astype(BF16)
    grad_att = jnp.einsum("te,de->td", grad_branch, w_out, preferred_element_type=F32).astype(BF16)
    return result, grad_middle, grad_att, grad_gain, (
        (attended, grad_branch),
        (mlp_low, grad_gate),
        (mlp_low, grad_up),
        (hidden_low, cotangent),
    )


def outer(left, right):
    return jnp.einsum("td,te->de", left, right, preferred_element_type=F32).astype(BF16)


def after(value, *others):
    return lax.optimization_barrier((value,) + others)[0]


def body(
    tokens, cotangent, doc_lengths, gain_attn, w_query, w_key, w_value, w_out, gain_mlp, w_gate, w_up, w_down
):
    micros, _, rows, width = tokens.shape
    heads = width // HEAD_DIM
    devices = lax.axis_size("ctx")
    shards = lax.axis_size("fsdp")
    place = lax.axis_index("ctx")
    side = lax.axis_index("fsdp")
    chips = devices // 2
    core = place % 2
    half = rows // 2
    depth = half + half // 2
    span = chips // micros
    rounds = -(-heads // span)
    counts = tuple(min(span, heads - index * span) for index in range(rounds))
    swap = [(i, i ^ 1) for i in range(devices)]
    cross = [(0, 1), (1, 0)]

    def pick(array, index, axis):
        return lax.dynamic_index_in_dim(array, index, axis, keepdims=False)

    def gathered(shard):
        return lax.all_gather(shard, "fsdp", axis=0, tiled=True)

    def fetched(pieces):
        if shards != 2:
            return [([gathered(piece)], 0) for piece in pieces]
        nears = []
        for piece in pieces:
            wide = piece.shape[1] // 2
            nears.append(lax.dynamic_slice_in_dim(piece, core * wide, wide, 1))
        near = nears[0] if len(nears) == 1 else jnp.concatenate(nears, 1)
        near = lax.ppermute(near, "fsdp", cross)
        far = lax.ppermute(near, "ctx", swap)
        return [([piece, near, far], index) for index, piece in enumerate(pieces)]

    def fetched_lines(lines):
        if shards != 2:
            return [gathered(line) for line in lines]
        lines = jnp.stack(lines)
        away = lax.ppermute(lines, "fsdp", cross)
        return jnp.where(
            side == 0, jnp.concatenate([lines, away], 1), jnp.concatenate([away, lines], 1)
        )

    def columns(index):
        cut = slice(index * span * HEAD_DIM, (index * span + counts[index]) * HEAD_DIM)
        return jnp.concatenate([w_query[:, cut], w_key[:, cut], w_value[:, cut]], 1)

    gain_attn, gain_mlp = fetched_lines([gain_attn, gain_mlp])
    weight_parts = fetched([columns(0)])
    if rounds > 1:
        weight_parts += fetched([columns(index) for index in range(1, rounds)])
    spot = jnp.stack([side, core]).astype(jnp.int32)
    w_out, w_gate, w_up, w_down = (gathered(shard) for shard in (w_out, w_gate, w_up, w_down))
    lengths = doc_lengths[:, 0]
    doc_ends = jnp.cumsum(lengths, -1)
    starts = (doc_ends - lengths).astype(jnp.int32)

    def begins_of(micro_starts, positions):
        reached = positions[:, None] >= micro_starts[None, :]
        return jnp.max(jnp.where(reached, micro_starts[None, :], 0), -1)

    lane = jnp.arange(LANES)
    inverse = jnp.power(10000.0, -(lane % (HEAD_DIM // 2)).astype(F32) / (HEAD_DIM // 2))
    sign = jnp.where((lane % HEAD_DIM) < HEAD_DIM // 2, -1.0, 1.0)
    positions = place * rows + jnp.arange(rows, dtype=jnp.int32)
    offsets = jnp.concatenate(
        [positions - begins_of(starts[micro], positions) for micro in range(micros)]
    ).astype(F32)
    angles = offsets[:, None] * inverse[None, :]
    cos_table, sine_table = jnp.cos(angles), jnp.sin(angles) * sign

    def exchange(buffer):
        return lax.all_to_all(buffer, "ctx", split_axis=0, concat_axis=0, tiled=True)

    tokens = tokens.reshape(micros * rows, width)
    cotangent = cotangent.reshape(micros * rows, width)
    inputs = tokens.astype(F32)
    recip = lax.rsqrt(jnp.mean(inputs * inputs, -1, keepdims=True) + EPS)
    normed = (inputs * recip * gain_attn.astype(F32)).astype(BF16)

    block = jnp.arange(devices, dtype=jnp.int32)
    block_first = block * rows + core * half
    chosen = pick(starts, place // 2 // span, 0)
    lowest = begins_of(chosen, block_first) // rows
    inner = jnp.minimum(-(-begins_of(chosen, block_first + half - 1) // rows), block)

    received, infos, others, attended_back, kept, in_weights = [], [], [], [], [], []
    for index in range(rounds):
        live = index * span + place // 2 % span < heads
        bounds = jnp.stack([jnp.where(live, lowest, block), jnp.where(live, inner, block)], 1)
        infos.append(jnp.concatenate([core[None], bounds.reshape(-1)]).astype(jnp.int32))
        buffer, weight = project(
            span, counts[index], micros, spot, normed, cos_table, sine_table, *weight_parts[index]
        )
        in_weights.append(weight)
        buffer = buffer.reshape(devices, depth, LANES)
        if index >= 2:
            buffer = after(buffer, kept[index - 2][1])
        received.append(exchange(buffer))
        whole = received[index]
        if index:
            whole = after(whole, kept[index - 1][1])
        others.append(lax.ppermute(whole, "ctx", swap))
        out, lse = attend(infos[index], chosen, received[index], others[index])
        kept.append((out, lse))
    def came_back(pieces):
        joined = pieces[0] if len(pieces) == 1 else jnp.concatenate(pieces, 1)
        joined = exchange(joined)
        return joined.reshape((chips, 2) + joined.shape[1:])

    early = [after(out, received[-1]) for out, _ in kept[:-1]]
    attended_back = ([came_back(early)] if early else []) + [came_back([kept[-1][0]])]

    attended = collect(counts, micros, attended_back)
    result, grad_middle, grad_att, grad_gain_mlp, pairs = feed_forward(
        tokens, cotangent, attended, w_out, gain_mlp, w_gate, w_up, w_down
    )
    grads_in = [
        exchange(buffer.reshape((devices,) + buffer.shape[2:]))
        for buffer in spread(span, counts, micros, grad_att)
    ]

    def paired(stay, leave, axis, routes):
        return (stay.astype(F32) + lax.ppermute(leave, axis, routes).astype(F32)).astype(BF16)

    def chip_summed(full, gain=None):
        count, wide = full.shape[0] // (2 * shards), full.shape[1]
        parts = full.reshape(shards, 2, count, wide)
        if gain is not None:
            line = gain.astype(BF16).reshape(shards, 2, 1, -1)
            line = jnp.pad(line, ((0, 0), (0, 0), (0, 63), (0, wide - line.shape[-1])))
            parts = jnp.concatenate([parts, line], 2)
        return paired(pick(parts, core, 1), pick(parts, 1 - core, 1), "ctx", swap)

    def owned(parts):
        if shards == 2:
            return paired(pick(parts, side, 0), pick(parts, 1 - side, 0), "fsdp", cross)
        return lax.psum_scatter(parts, "fsdp", scatter_dimension=0, tiled=False)

    def spaced(part):
        return jnp.where((core == jnp.arange(2))[:, None, None], part[None], 0)

    def totals_of(parts):
        if devices == 16:
            return ctx_sum(parts)
        return list(lax.psum(tuple(spaced(part) for part in parts), "ctx"))

    def opened(total, has_gain):
        wide = total.shape[-1]
        count = total.shape[1] - (64 if has_gain else 0)
        rows_part = total[:, :count].reshape(2 * count, wide).astype(F32)
        if not has_gain:
            return rows_part
        return rows_part, total[:, count, : width // (2 * shards)].reshape(-1).astype(F32)

    pair_out, pair_gate, pair_up, pair_down = pairs
    chip_down = chip_summed(outer(*pair_down))
    chip_gate = chip_summed(outer(*pair_gate))
    chip_up = chip_summed(outer(*pair_up))
    chip_out = chip_summed(outer(*pair_out), grad_gain_mlp)
    mid_parts = [owned(chip) for chip in (chip_out, chip_down, chip_gate, chip_up)]

    grad_back, sent_back = [], []
    waits = {0: (chip_out, chip_down, chip_gate, chip_up), 2: tuple(mid_parts)}
    for index in range(rounds):
        own, away = attend_grad(
            infos[index],
            chosen,
            received[index],
            others[index],
            after(
                grads_in[min(index, 1)], *waits.get(index, ()), *sent_back[-1:], *grad_back[-2:-1]
            ),
            max(index - 1, 0),
            *kept[index],
        )
        back = lax.ppermute(away, "ctx", swap)
        buffer = merge(own, back)
        sent_back.append(buffer)
        grad_back.append(exchange(buffer).reshape(chips, 2, depth, LANES))

    grad_normed, parts = 0.0, []
    for index in range(rounds):
        grad_qkv = collect_grad(counts[index], micros, grad_back[index], cos_table, sine_table)
        grad_normed = grad_normed + jnp.einsum(
            "te,de->td", grad_qkv, in_weights[index], preferred_element_type=F32
        )
        final = index == rounds - 1
        if final:
            grad_in, grad_gain = norm_backward(grad_normed, inputs, recip, gain_attn.astype(F32))
        parts.append(owned(chip_summed(outer(normed, grad_qkv), grad_gain if final else None)))
    totals = totals_of(mid_parts + parts)
    mid_totals, last_totals = totals[: len(mid_parts)], totals[len(mid_parts) :]
    grad_w_out, grad_gain_mlp = opened(mid_totals[0], True)
    grad_w_down, grad_w_gate, grad_w_up = (opened(total, False) for total in mid_totals[1:])
    grad_inputs = (grad_middle + grad_in).astype(BF16)
    opened_last, grad_gain_attn = opened(last_totals[-1], True)
    opened_parts = [opened(total, False) for total in last_totals[:-1]] + [opened_last]
    grad_w_query, grad_w_key, grad_w_value = (
        jnp.concatenate(
            [
                part[:, which * part.shape[1] // 3 : (which + 1) * part.shape[1] // 3]
                for part in opened_parts
            ],
            1,
        )
        for which in range(3)
    )
    shape = (micros, 1, rows, width)
    return (
        result.reshape(shape),
        grad_inputs.reshape(shape),
        grad_gain_attn,
        grad_w_query,
        grad_w_key,
        grad_w_value,
        grad_w_out,
        grad_gain_mlp,
        grad_w_gate,
        grad_w_up,
        grad_w_down,
    )


def solution(mesh):
    weight, gain = P("fsdp", None), P("fsdp")
    rows = P(None, "fsdp", "ctx", None)
    weights = (gain, weight, weight, weight, weight, gain, weight, weight, weight)
    return jax.shard_map(
        body,
        mesh=mesh,
        in_specs=(rows, rows, P(None, "fsdp", None)) + weights,
        out_specs=(rows, rows) + weights,
        check_vma=False,
    )
```

```python
import functools
import math

import jax
import jax.numpy as jnp
from jax import lax
from jax.experimental import pallas as pl
from jax.experimental.pallas import tpu as pltpu
from jax.sharding import PartitionSpec as P

HEAD_DIM = 64
LANES = 128
EPS = 1e-05
NEG = -1e30
LOG2E = math.log2(math.e)
LN2 = math.log(2.0)
F32 = jnp.float32
BF16 = jnp.bfloat16


def dot_nt(left, right):
    return lax.dot_general(left, right, (((1,), (1,)), ((), ())), preferred_element_type=F32)


def dot_nn(left, right):
    return lax.dot_general(left, right, (((1,), (0,)), ((), ())), preferred_element_type=F32)


def dot_tn(left, right):
    return lax.dot_general(left, right, (((0,), (0,)), ((), ())), preferred_element_type=F32)


def lane_index(rows):
    return lax.broadcasted_iota(jnp.int32, (rows, LANES), 1)


def flip(tile):
    return pltpu.roll(tile, HEAD_DIM, 1)


def params(count):
    return pltpu.CompilerParams(
        dimension_semantics=("arbitrary",) * count, vmem_limit_bytes=60 * 1024 * 1024
    )


def full_block(shape):
    zeros = (0,) * len(shape)
    return pl.BlockSpec(shape, lambda *_: zeros)


def pack_pair(tile):
    count = tile.shape[0] // 2
    low = lane_index(count) < HEAD_DIM
    top, bottom = tile[:count], tile[count:]
    return (jnp.where(low, top, flip(bottom)), jnp.where(low, flip(top), bottom))


def unpack_pair(first, second):
    low = lane_index(first.shape[0]) < HEAD_DIM
    top = jnp.where(low, first, flip(second))
    bottom = jnp.where(low, flip(first), second)
    return jnp.concatenate([top, bottom], 0)


def turn(tile):
    near = (lane_index(tile.shape[0]) % HEAD_DIM) < HEAD_DIM // 2
    return jnp.where(
        near, pltpu.roll(tile, LANES - HEAD_DIM // 2, 1), pltpu.roll(tile, HEAD_DIM // 2, 1)
    )


def project_kernel(count, info, n_ref, c_ref, s_ref, *refs):
    *parts, out, w_ref = refs

    @pl.when((pl.program_id(0) == 0) & (pl.program_id(1) == 0))
    def _():
        if len(parts) == 1:
            w_ref[...] = parts[0][...]
            return
        own, near, far = parts
        deep, wide = near.shape
        side, core = info[0], info[1]
        mine = pl.ds(pl.multiple_of(side * deep, deep), deep)
        away = pl.ds(pl.multiple_of((1 - side) * deep, deep), deep)
        w_ref[mine, :] = own[...]
        w_ref[away, pl.ds(pl.multiple_of(core * wide, wide), wide)] = near[...]
        w_ref[away, pl.ds(pl.multiple_of((1 - core) * wide, wide), wide)] = far[...]

    joined = dot_nn(n_ref[...], w_ref[...])
    cos_table, sine_table = c_ref[...], s_ref[...]
    rows = n_ref.shape[0]
    span = count * HEAD_DIM
    low = lane_index(rows) < HEAD_DIM
    for pair in range(count // 2):
        first = pair * LANES
        q2, k2, v2 = (joined[:, part * span + first : part * span + first + LANES] for part in range(3))
        q2 = (q2 * cos_table + turn(q2) * sine_table) * (LOG2E * HEAD_DIM**-0.5)
        k2 = k2 * cos_table + turn(k2) * sine_table
        packed = pack_pair(q2)
        kv = (jnp.where(low, k2, flip(v2)), jnp.where(low, flip(k2), v2))
        for side in range(2):
            out[2 * pair + side, 0, :rows, :] = kv[side].astype(BF16)
            out[2 * pair + side, 0, rows:, :] = packed[side].astype(BF16)
    if count < out.shape[0]:
        out[count:] = jnp.zeros((out.shape[0] - count,) + out.shape[1:], BF16)


def project(span, count, micros, info, normed, cos_table, sine_table, parts, column):
    rows, width = normed.shape
    half = rows // (2 * micros)
    depth = half + half // 2
    wide = parts[0].shape[1]
    return pl.pallas_call(
        functools.partial(project_kernel, count),
        grid_spec=pltpu.PrefetchScalarGridSpec(
            num_scalar_prefetch=1,
            grid=(micros, 2),
            in_specs=[
                pl.BlockSpec((half, width), lambda m, i, *_: (2 * m + i, 0)),
                pl.BlockSpec((half, LANES), lambda m, i, *_: (2 * m + i, 0)),
                pl.BlockSpec((half, LANES), lambda m, i, *_: (2 * m + i, 0)),
            ]
            + [full_block(part.shape) for part in parts[:1]]
            + [
                pl.BlockSpec((part.shape[0], wide // 2), lambda m, i, *_: (0, column))
                for part in parts[1:]
            ],
            out_specs=[
                pl.BlockSpec((span, 1, depth, LANES), lambda m, i, *_: (m, i, 0, 0)),
                full_block((width, wide)),
            ],
        ),
        out_shape=[
            jax.ShapeDtypeStruct((micros * span, 2, depth, LANES), BF16),
            jax.ShapeDtypeStruct((width, wide), BF16),
        ],
        compiler_params=params(2),
        cost_estimate=pl.CostEstimate(
            flops=2 * rows * width * wide, bytes_accessed=4 * rows * width, transcendentals=0
        ),
        name="project",
    )(info, normed, cos_table, sine_table, *parts)


def row_begins(starts_ref, positions):
    begins = jnp.zeros_like(positions)
    for index in range(starts_ref.shape[0]):
        start = starts_ref[index]
        begins = jnp.maximum(begins, jnp.where(positions >= start, start, 0))
    return begins


def unpack_one(packed, lanes_low):
    wide = packed.astype(F32)
    low = lane_index(wide.shape[0]) < HEAD_DIM
    keep = low if lanes_low else jnp.logical_not(low)
    turned = flip(wide)
    first, second = (wide, turned) if lanes_low else (turned, wide)
    return jnp.concatenate(
        [jnp.where(keep, first, 0.0), jnp.where(keep, second, 0.0)], 0
    ).astype(BF16)


def attend_kernel(info, starts, mine, other, o_ref, lse_ref):
    block = pl.program_id(0)
    core = info[0]
    lowest, inner = info[1 + 2 * block], info[2 + 2 * block]
    rows = mine.shape[1] * 2 // 3
    low = lane_index(rows) < HEAD_DIM
    queries = unpack_one(mine[block, rows:, :], True)
    row_pos = (2 * block + core) * rows + lax.broadcasted_iota(jnp.int32, (rows, 1), 0)
    begins = row_begins(starts, row_pos)
    lane_low = lane_index(2 * rows) < HEAD_DIM
    column = lax.broadcasted_iota(jnp.int32, (1, 2 * rows), 1)
    offsets = jnp.where(column < rows, column + core * rows, column - core * rows)

    def keys(index):
        kv = jnp.concatenate([mine[index, :rows, :], other[index, :rows, :]], 0)
        return kv, jnp.where(lane_low, jnp.ones_like(kv), kv)

    def two_steps(index, carry):
        peak, acc = carry
        first, first_v = keys(inner + 2 * index)
        second, second_v = keys(inner + 2 * index + 1)
        scores, more = dot_nt(queries, first), dot_nt(queries, second)
        new_peak = jnp.maximum(peak, jnp.max(jnp.maximum(scores, more), -1, keepdims=True))
        weights, more = jnp.exp2(scores - new_peak), jnp.exp2(more - new_peak)
        acc = acc * jnp.exp2(peak - new_peak) + (
            dot_nn(weights.astype(BF16), first_v) + dot_nn(more.astype(BF16), second_v)
        )
        return (new_peak, acc)

    def step(masked, index, carry):
        peak, acc = carry
        kv, ones_v = keys(index)
        scores = dot_nt(queries, kv)
        if masked:
            key_pos = offsets + index * (2 * rows)
            scores = jnp.where((key_pos >= begins) & (key_pos <= row_pos), scores, NEG)
        new_peak = jnp.maximum(peak, jnp.max(scores, -1, keepdims=True))
        weights = jnp.exp2(scores - new_peak)
        acc = acc * jnp.exp2(peak - new_peak) + dot_nn(weights.astype(BF16), ones_v)
        return (new_peak, acc)

    carry = step(True, block, (jnp.full((rows, 1), NEG, F32), jnp.zeros((rows, LANES), F32)))
    carry = lax.fori_loop(lowest, inner, functools.partial(step, True), carry)
    twice = (block - inner) // 2
    carry = lax.fori_loop(0, twice, two_steps, carry)
    peak, acc = lax.fori_loop(inner + 2 * twice, block, functools.partial(step, False), carry)
    result = acc / flip(acc)
    count = rows // 2
    small_low = lane_index(count) < HEAD_DIM
    o_ref[0] = jnp.where(small_low, flip(result[:count]), result[count:]).astype(BF16)
    lse = jnp.where(low, peak + jnp.log2(acc), 0.0)
    lse_ref[0] = jnp.transpose(lse)[0:1, :]


def attend(info, starts, mine, other):
    blocks, depth, _ = mine.shape
    rows = depth * 2 // 3
    return pl.pallas_call(
        attend_kernel,
        grid_spec=pltpu.PrefetchScalarGridSpec(
            num_scalar_prefetch=2,
            grid=(blocks,),
            in_specs=[
                pl.BlockSpec(mine.shape, lambda i, *_: (0, 0, 0)),
                pl.BlockSpec(other.shape, lambda i, *_: (0, 0, 0)),
            ],
            out_specs=[
                pl.BlockSpec((1, rows // 2, LANES), lambda i, *_: (i, 0, 0)),
                pl.BlockSpec((1, 1, rows), lambda i, *_: (i, 0, 0)),
            ],
        ),
        out_shape=[
            jax.ShapeDtypeStruct((blocks, rows // 2, LANES), BF16),
            jax.ShapeDtypeStruct((blocks, 1, rows), F32),
        ],
        compiler_params=params(1),
        cost_estimate=pl.CostEstimate(
            flops=16 * 10**9, bytes_accessed=10**7, transcendentals=10**7
        ),
        name="attend",
    )(info, starts, mine, other)


def attend_grad_kernel(
    info, starts, mine, other, do_ref, o_ref, lse_ref, dm_ref, dp_ref, acc_mine, acc_other
):
    block = pl.program_id(0)
    core = info[0]
    lowest, inner = info[1 + 2 * block], info[2 + 2 * block]
    rows = mine.shape[1] * 2 // 3
    count = rows // 2

    @pl.when(block == 0)
    def _():
        acc_mine[...] = jnp.zeros_like(acc_mine)
        acc_other[...] = jnp.zeros_like(acc_other)

    queries = unpack_one(mine[block, rows:, :], True)
    grad_out = unpack_one(do_ref[0], False)
    both = jnp.concatenate([queries, grad_out], 0)
    product = jnp.transpose(do_ref[0].astype(F32) * o_ref[0].astype(F32))
    delta = jnp.concatenate(
        [
            jnp.sum(product[:HEAD_DIM], 0, keepdims=True),
            jnp.sum(product[HEAD_DIM:], 0, keepdims=True),
        ],
        1,
    )
    lse = lse_ref[0]
    row_pos = (2 * block + core) * rows + lax.broadcasted_iota(jnp.int32, (1, rows), 1)
    begins = row_begins(starts, row_pos)
    line = lax.broadcasted_iota(jnp.int32, (2 * rows, 1), 0)
    offsets = jnp.where(line < rows, line + core * rows, line - core * rows)

    def step(masked, index, grad_q):
        kv = jnp.concatenate([mine[index, :rows, :], other[index, :rows, :]], 0)
        scores = dot_nt(kv, queries)
        weights = jnp.exp2(scores - lse)
        if masked:
            key_pos = offsets + index * (2 * rows)
            weights = jnp.where((key_pos >= begins) & (key_pos <= row_pos), weights, 0.0)
        grad_weights = dot_nt(kv, grad_out)
        grad_scores = (weights * (grad_weights - delta)).astype(BF16)
        grad_kv = dot_nn(jnp.concatenate([grad_scores, weights.astype(BF16)], 1), both)
        acc_mine[index] += grad_kv[:rows]
        acc_other[index] += grad_kv[rows:]
        return grad_q + dot_tn(grad_scores, kv)

    grad_q = step(True, block, jnp.zeros((rows, LANES), F32))
    grad_q = lax.fori_loop(lowest, inner, functools.partial(step, True), grad_q)
    twice = (block - inner) // 2

    def two_steps(index, grad_q):
        grad_q = step(False, inner + 2 * index, grad_q)
        return step(False, inner + 2 * index + 1, grad_q)

    grad_q = lax.fori_loop(0, twice, two_steps, grad_q)
    grad_q = lax.fori_loop(inner + 2 * twice, block, functools.partial(step, False), grad_q)
    grad_q = grad_q * HEAD_DIM**-0.5
    small_low = lane_index(count) < HEAD_DIM
    dm_ref[block, rows:, :] = jnp.where(small_low, grad_q[:count], flip(grad_q[count:])).astype(
        BF16
    )

    @pl.when(block == pl.num_programs(0) - 1)
    def _():
        scale = jnp.where(lane_index(rows) < HEAD_DIM, LN2, 1.0)

        def flush(index, _):
            dm_ref[index, :rows, :] = (acc_mine[index] * scale).astype(BF16)
            dp_ref[index] = (acc_other[index] * scale).astype(BF16)
            return 0

        lax.fori_loop(0, mine.shape[0], flush, 0)


def attend_grad(info, starts, mine, other, grad_out, spot, out, lse):
    blocks, depth, _ = mine.shape
    rows = depth * 2 // 3
    whole = pl.BlockSpec(mine.shape, lambda i, *_: (0, 0, 0))
    small = pl.BlockSpec((1, rows // 2, LANES), lambda i, *_: (i, 0, 0))
    return pl.pallas_call(
        attend_grad_kernel,
        grid_spec=pltpu.PrefetchScalarGridSpec(
            num_scalar_prefetch=2,
            grid=(blocks,),
            in_specs=[
                whole,
                whole,
                pl.BlockSpec((1, rows // 2, LANES), lambda i, *_: (i, spot, 0)),
                small,
                pl.BlockSpec((1, 1, rows), lambda i, *_: (i, 0, 0)),
            ],
            out_specs=[whole, pl.BlockSpec((blocks, rows, LANES), lambda i, *_: (0, 0, 0))],
            scratch_shapes=[
                pltpu.VMEM((blocks, rows, LANES), F32),
                pltpu.VMEM((blocks, rows, LANES), F32),
            ],
        ),
        out_shape=[
            jax.ShapeDtypeStruct(mine.shape, BF16),
            jax.ShapeDtypeStruct((blocks, rows, LANES), BF16),
        ],
        compiler_params=params(1),
        cost_estimate=pl.CostEstimate(
            flops=32 * 10**9, bytes_accessed=10**7, transcendentals=10**7
        ),
        name="attend_grad",
    )(info, starts, mine, other, grad_out, out, lse)


def merge_kernel(own_ref, back_ref, out):
    rows = back_ref.shape[1]
    out[:, :rows, :] = (own_ref[:, :rows, :].astype(F32) + back_ref[...].astype(F32)).astype(BF16)
    out[:, rows:, :] = own_ref[:, rows:, :]


def merge(own, back):
    blocks, depth, _ = own.shape
    step = blocks // 4
    spec = pl.BlockSpec((step, depth, LANES), lambda i: (i, 0, 0))
    return pl.pallas_call(
        merge_kernel,
        grid=(4,),
        in_specs=[spec, pl.BlockSpec((step, back.shape[1], LANES), lambda i: (i, 0, 0))],
        out_specs=spec,
        out_shape=jax.ShapeDtypeStruct(own.shape, BF16),
        compiler_params=params(1),
        cost_estimate=pl.CostEstimate(flops=0, bytes_accessed=4 * 10**6, transcendentals=0),
        name="merge",
    )(own, back)


def collect_kernel(counts, *refs):
    ins, out = refs[:-1], refs[-1]
    length = out.shape[0] // 2
    pieces = [(array, first) for array in ins for first in range(0, array.shape[2], length)]
    pair = 0
    for (array, first), count in zip(pieces, counts):
        cut = slice(first, first + length)
        for spot in range(0, count, 2):
            tiles = [array[spot + side, 0, cut, :].astype(F32) for side in range(2)]
            out[:, pair * LANES : (pair + 1) * LANES] = unpack_pair(*tiles).astype(BF16)
            pair += 1


def collect(counts, micros, arrays):
    units = arrays[0].shape[0]
    length = sum(array.shape[2] for array in arrays) // len(counts)
    width = sum(counts) * HEAD_DIM
    return pl.pallas_call(
        functools.partial(collect_kernel, counts),
        grid=(micros, 2),
        in_specs=[
            pl.BlockSpec((units // micros, 1, array.shape[2], LANES), lambda m, i: (m, i, 0, 0))
            for array in arrays
        ],
        out_specs=pl.BlockSpec((2 * length, width), lambda m, i: (2 * m + i, 0)),
        out_shape=jax.ShapeDtypeStruct((micros * 4 * length, width), BF16),
        compiler_params=params(2),
        cost_estimate=pl.CostEstimate(flops=0, bytes_accessed=4 * 10**6, transcendentals=0),
        name="collect",
    )(*arrays)


def spread_kernel(counts, x_ref, *outs):
    length = x_ref.shape[0] // 2
    pieces = [(out, first) for out in outs for first in range(0, out.shape[2], length)]
    pair = 0
    for (out, first), count in zip(pieces, counts):
        cut = slice(first, first + length)
        for spot in range(0, count, 2):
            tile = x_ref[:, pair * LANES : (pair + 1) * LANES].astype(F32)
            packed = pack_pair(tile)
            for side in range(2):
                out[spot + side, 0, cut, :] = packed[side].astype(BF16)
            pair += 1
        for spot in range(count, out.shape[0]):
            out[spot, 0, cut, :] = jnp.zeros((length, LANES), BF16)


def spread(span, counts, micros, rows_array):
    rows, width = rows_array.shape
    half = rows // (2 * micros)
    lengths = [half // 2] + ([half // 2 * (len(counts) - 1)] if len(counts) > 1 else [])
    return pl.pallas_call(
        functools.partial(spread_kernel, counts),
        grid=(micros, 2),
        in_specs=[pl.BlockSpec((half, width), lambda m, i: (2 * m + i, 0))],
        out_specs=[
            pl.BlockSpec((span, 1, length, LANES), lambda m, i: (m, i, 0, 0)) for length in lengths
        ],
        out_shape=[
            jax.ShapeDtypeStruct((micros * span, 2, length, LANES), BF16) for length in lengths
        ],
        compiler_params=params(2),
        cost_estimate=pl.CostEstimate(flops=0, bytes_accessed=4 * 10**6, transcendentals=0),
        name="spread",
    )(rows_array)


def turn_back(tile, cos_table, sine_table):
    near = (lane_index(tile.shape[0]) % HEAD_DIM) < HEAD_DIM // 2
    scaled = tile * sine_table
    moved = jnp.where(
        near,
        pltpu.roll(scaled, LANES - HEAD_DIM // 2, 1),
        pltpu.roll(scaled, HEAD_DIM // 2, 1),
    )
    return tile * cos_table + moved


def collect_grad_kernel(count, c_ref, s_ref, in_ref, out):
    cos_table, sine_table = c_ref[...], s_ref[...]
    rows = cos_table.shape[0]
    span = count * HEAD_DIM
    low = lane_index(rows) < HEAD_DIM
    for pair in range(count // 2):
        kvs = [in_ref[2 * pair + side, 0, :rows, :].astype(F32) for side in range(2)]
        packed = [in_ref[2 * pair + side, 0, rows:, :].astype(F32) for side in range(2)]
        grad_k = jnp.where(low, kvs[0], flip(kvs[1]))
        grad_v = jnp.where(low, flip(kvs[0]), kvs[1])
        grad_q = turn_back(unpack_pair(*packed), cos_table, sine_table)
        grad_k = turn_back(grad_k, cos_table, sine_table)
        for part, value in enumerate((grad_q, grad_k, grad_v)):
            first = part * span + pair * LANES
            out[:, first : first + LANES] = value.astype(BF16)


def collect_grad(count, micros, array, cos_table, sine_table):
    units, _, depth, _ = array.shape
    half = depth * 2 // 3
    width = 3 * count * HEAD_DIM
    table = pl.BlockSpec((half, LANES), lambda m, i: (2 * m + i, 0))
    return pl.pallas_call(
        functools.partial(collect_grad_kernel, count),
        grid=(micros, 2),
        in_specs=[
            table,
            table,
            pl.BlockSpec((units // micros, 1, depth, LANES), lambda m, i: (m, i, 0, 0)),
        ],
        out_specs=pl.BlockSpec((half, width), lambda m, i: (2 * m + i, 0)),
        out_shape=jax.ShapeDtypeStruct((micros * 2 * half, width), BF16),
        compiler_params=params(2),
        cost_estimate=pl.CostEstimate(flops=0, bytes_accessed=6 * 10**6, transcendentals=0),
        name="collect_grad",
    )(cos_table, sine_table, array)


SUM_STEPS = 6
PLANE_Z, PLANE_Y, FAR_Z, TWIN = 4, 2, 8, 1


def add_rows(out, left, right):
    def step(index, _):
        cut = pl.ds(pl.multiple_of(index * 16, 16), 16)
        out[cut, :] = (left[cut, :].astype(F32) + right[cut, :].astype(F32)).astype(BF16)
        return 0

    lax.fori_loop(0, out.shape[0] // 16, step, 0)


def ctx_sum_kernel(count, *refs):
    ins, outs = refs[:count], refs[count : 2 * count]
    halves, quarters, sums, fars = (refs[(2 + k) * count : (3 + k) * count] for k in range(4))
    send_sems, recv_sems = refs[6 * count :]
    place = lax.axis_index("ctx")
    side = lax.axis_index("fsdp")

    def bit(weight):
        return place // weight % 2

    def partner(weight):
        return (place + weight * (1 - 2 * bit(weight)), side)

    barrier = pltpu.get_barrier_semaphore()
    for weight in (PLANE_Z, PLANE_Y, FAR_Z, TWIN):
        pl.semaphore_signal(
            barrier, inc=1, device_id=partner(weight), device_id_type=pl.DeviceIdType.MESH
        )
    pl.semaphore_wait(barrier, 4)

    def send(index, step, source, target, weight):
        copy = pltpu.make_async_remote_copy(
            src_ref=source,
            dst_ref=target,
            send_sem=send_sems.at[index, step],
            recv_sem=recv_sems.at[index, step],
            device_id=partner(weight),
            device_id_type=pl.DeviceIdType.MESH,
        )
        copy.start()
        return copy

    axes = [(PLANE_Z, PLANE_Y) if index % 4 == 2 else (PLANE_Y, PLANE_Z) for index in range(count)]
    core = bit(TWIN)
    started, copies = {}, []

    def stage(index, step):
        first, second = axes[index]
        if step:
            started[index].wait_recv()
        if step == 0:
            leave = ins[index].at[pl.ds(2 * (1 - bit(first)), 2)]
            target, weight = halves[index], first
        elif step == 1:
            for part in range(2):
                half = halves[index].at[part]
                add_rows(half, ins[index].at[2 * bit(first) + part], half)
            leave, target, weight = halves[index].at[1 - bit(second)], quarters[index], second
        elif step == 2:
            add_rows(sums[index], halves[index].at[bit(second)], quarters[index])
            leave, target, weight = sums[index], fars[index], FAR_Z
        elif step == 3:
            leave = target = outs[index].at[core, 2 * bit(first) + bit(second)]
            weight = second
            add_rows(leave, sums[index], fars[index])
        elif step == 4:
            leave = target = outs[index].at[core, pl.ds(2 * bit(first), 2)]
            weight = first
        elif step == 5:
            leave = target = outs[index].at[core]
            weight = TWIN
        if step < SUM_STEPS:
            started[index] = send(index, step, leave, target, weight)
            copies.append(started[index])

    for time in range(count + SUM_STEPS + 1):
        if time < count:
            stage(time, 0)
        for step in reversed(range(1, SUM_STEPS + 1)):
            if 0 <= time - step - 1 < count:
                stage(time - step - 1, step)
    for copy in copies:
        copy.wait_send()


def ctx_sum(parts):
    count = len(parts)
    shapes = [(part.shape[0] // 4, part.shape[1]) for part in parts]
    sent = sum(6 * part.size for part in parts)
    vmem = pl.BlockSpec(memory_space=pltpu.VMEM)
    totals = pl.pallas_call(
        functools.partial(ctx_sum_kernel, count),
        in_specs=[vmem] * count,
        out_specs=[vmem] * count,
        out_shape=[jax.ShapeDtypeStruct((2, 4) + shape, BF16) for shape in shapes],
        scratch_shapes=[pltpu.VMEM((2,) + shape, BF16) for shape in shapes]
        + [pltpu.VMEM(shape, BF16) for shape in shapes] * 3
        + [pltpu.SemaphoreType.DMA((count, SUM_STEPS))] * 2,
        compiler_params=pltpu.CompilerParams(
            collective_id=0, has_side_effects=True, vmem_limit_bytes=60 * 1024 * 1024
        ),
        cost_estimate=pl.CostEstimate(flops=0, bytes_accessed=4 * sent, transcendentals=0),
        name="ctx_sum",
    )(*[part.reshape((4,) + shape) for part, shape in zip(parts, shapes)])
    return [total.reshape((2,) + part.shape) for total, part in zip(totals, parts)]


def matmul(left, right):
    return jnp.dot(left, right, preferred_element_type=F32)


def norm_backward(grad_out, values, recip_rows, gain):
    scaled = grad_out * gain
    grad_in = recip_rows * scaled - values * (recip_rows * recip_rows * recip_rows) * jnp.mean(
        scaled * values, -1, keepdims=True
    )
    return (grad_in, jnp.sum(grad_out * values * recip_rows, 0))


def mlp_kernel(
    n_ref, nt_ref, cot_ref, mid_ref, wg_ref, wu_ref, wd_ref, out, gn_out, gwg_out, gwu_out, gwd_out, acc
):
    index = pl.program_id(0)

    @pl.when(index == 0)
    def _():
        acc[...] = mid_ref[...]
        gn_out[...] = jnp.zeros_like(gn_out)

    gate_pre = dot_nn(n_ref[...], wg_ref[...])
    up_pre = dot_nn(n_ref[...], wu_ref[...])
    grad_hidden = dot_nt(cot_ref[...], wd_ref[...])
    gate_sigmoid = 1.0 / (1.0 + jnp.exp(-gate_pre))
    silu_value = gate_pre * gate_sigmoid
    hidden_low = (silu_value * up_pre).astype(BF16)
    grad_gate = (
        grad_hidden * up_pre * gate_sigmoid * (1.0 + gate_pre * (1.0 - gate_sigmoid))
    ).astype(BF16)
    grad_up = (grad_hidden * silu_value).astype(BF16)
    acc[...] += dot_nn(hidden_low, wd_ref[...])
    gn_out[...] += dot_nt(grad_gate, wg_ref[...]) + dot_nt(grad_up, wu_ref[...])
    gwg_out[...] = dot_nn(nt_ref[...], grad_gate).astype(BF16)
    gwu_out[...] = dot_nn(nt_ref[...], grad_up).astype(BF16)
    gwd_out[...] = dot_tn(hidden_low, cot_ref[...]).astype(BF16)

    @pl.when(index == pl.num_programs(0) - 1)
    def _():
        out[...] = acc[...].astype(BF16)


def mlp(normed, cotangent, middle, w_gate, w_up, w_down):
    rows, width = normed.shape
    units = w_gate.shape[1]
    wide = 256
    across = pl.BlockSpec((width, wide), lambda j: (0, j))
    down = pl.BlockSpec((wide, width), lambda j: (j, 0))
    whole = full_block((rows, width))
    return pl.pallas_call(
        mlp_kernel,
        grid=(units // wide,),
        in_specs=[whole, full_block((width, rows)), whole, whole, across, across, down],
        out_specs=[whole, whole, across, across, down],
        out_shape=[
            jax.ShapeDtypeStruct((rows, width), BF16),
            jax.ShapeDtypeStruct((rows, width), F32),
            jax.ShapeDtypeStruct((width, units), BF16),
            jax.ShapeDtypeStruct((width, units), BF16),
            jax.ShapeDtypeStruct((units, width), BF16),
        ],
        scratch_shapes=[pltpu.VMEM((rows, width), F32)],
        compiler_params=params(1),
        cost_estimate=pl.CostEstimate(
            flops=18 * rows * width * units, bytes_accessed=12 * width * units, transcendentals=0
        ),
        name="mlp",
    )(normed, normed.T, cotangent, middle, w_gate, w_up, w_down)


def feed_forward(tokens, cotangent, attended, w_out, gain_mlp, w_gate, w_up, w_down):
    inputs = tokens.astype(F32)
    gain = gain_mlp.astype(F32)
    middle = inputs + matmul(attended, w_out)
    recip = lax.rsqrt(jnp.mean(middle * middle, -1, keepdims=True) + EPS)
    mlp_low = (middle * recip * gain).astype(BF16)
    result, grad_normed, *grads = mlp(mlp_low, cotangent, middle, w_gate, w_up, w_down)
    grad_mid, grad_gain = norm_backward(grad_normed, middle, recip, gain)
    grad_middle = cotangent.astype(F32) + grad_mid
    grad_branch = grad_middle.astype(BF16)
    grad_att = jnp.einsum("te,de->td", grad_branch, w_out, preferred_element_type=F32).astype(BF16)
    return result, grad_middle, grad_att, grad_gain, [outer(attended, grad_branch), *grads]


def outer(left, right):
    return jnp.einsum("td,te->de", left, right, preferred_element_type=F32).astype(BF16)


def after(value, *others):
    return lax.optimization_barrier((value,) + others)[0]


def body(
    tokens, cotangent, doc_lengths, gain_attn, w_query, w_key, w_value, w_out, gain_mlp, w_gate, w_up, w_down
):
    micros, _, rows, width = tokens.shape
    heads = width // HEAD_DIM
    devices = lax.axis_size("ctx")
    shards = lax.axis_size("fsdp")
    place = lax.axis_index("ctx")
    side = lax.axis_index("fsdp")
    chips = devices // 2
    core = place % 2
    half = rows // 2
    depth = half + half // 2
    span = chips // micros
    rounds = -(-heads // span)
    counts = tuple(min(span, heads - index * span) for index in range(rounds))
    swap = [(i, i ^ 1) for i in range(devices)]
    cross = [(0, 1), (1, 0)]

    def pick(array, index, axis):
        return lax.dynamic_index_in_dim(array, index, axis, keepdims=False)

    def gathered(shard):
        return lax.all_gather(shard, "fsdp", axis=0, tiled=True)

    def fetched(pieces):
        if shards != 2:
            return [([gathered(piece)], 0) for piece in pieces]
        nears = []
        for piece in pieces:
            wide = piece.shape[1] // 2
            nears.append(lax.dynamic_slice_in_dim(piece, core * wide, wide, 1))
        near = nears[0] if len(nears) == 1 else jnp.concatenate(nears, 1)
        near = lax.ppermute(near, "fsdp", cross)
        far = lax.ppermute(near, "ctx", swap)
        return [([piece, near, far], index) for index, piece in enumerate(pieces)]

    def fetched_lines(lines):
        if shards != 2:
            return [gathered(line) for line in lines]
        lines = jnp.stack(lines)
        away = lax.ppermute(lines, "fsdp", cross)
        return jnp.where(
            side == 0, jnp.concatenate([lines, away], 1), jnp.concatenate([away, lines], 1)
        )

    def columns(index):
        cut = slice(index * span * HEAD_DIM, (index * span + counts[index]) * HEAD_DIM)
        return jnp.concatenate([w_query[:, cut], w_key[:, cut], w_value[:, cut]], 1)

    gain_attn, gain_mlp = fetched_lines([gain_attn, gain_mlp])
    weight_parts = fetched([columns(0)])
    if rounds > 1:
        weight_parts += fetched([columns(index) for index in range(1, rounds)])
    spot = jnp.stack([side, core]).astype(jnp.int32)
    w_out, w_gate, w_up, w_down = (gathered(shard) for shard in (w_out, w_gate, w_up, w_down))
    lengths = doc_lengths[:, 0]
    doc_ends = jnp.cumsum(lengths, -1)
    starts = (doc_ends - lengths).astype(jnp.int32)

    def begins_of(micro_starts, positions):
        reached = positions[:, None] >= micro_starts[None, :]
        return jnp.max(jnp.where(reached, micro_starts[None, :], 0), -1)

    lane = jnp.arange(LANES)
    inverse = jnp.power(10000.0, -(lane % (HEAD_DIM // 2)).astype(F32) / (HEAD_DIM // 2))
    sign = jnp.where((lane % HEAD_DIM) < HEAD_DIM // 2, -1.0, 1.0)
    positions = place * rows + jnp.arange(rows, dtype=jnp.int32)
    offsets = jnp.concatenate(
        [positions - begins_of(starts[micro], positions) for micro in range(micros)]
    ).astype(F32)
    angles = offsets[:, None] * inverse[None, :]
    cos_table, sine_table = jnp.cos(angles), jnp.sin(angles) * sign

    def exchange(buffer):
        return lax.all_to_all(buffer, "ctx", split_axis=0, concat_axis=0, tiled=True)

    tokens = tokens.reshape(micros * rows, width)
    cotangent = cotangent.reshape(micros * rows, width)
    inputs = tokens.astype(F32)
    recip = lax.rsqrt(jnp.mean(inputs * inputs, -1, keepdims=True) + EPS)
    normed = (inputs * recip * gain_attn.astype(F32)).astype(BF16)

    block = jnp.arange(devices, dtype=jnp.int32)
    block_first = block * rows + core * half
    chosen = pick(starts, place // 2 // span, 0)
    lowest = begins_of(chosen, block_first) // rows
    inner = jnp.minimum(-(-begins_of(chosen, block_first + half - 1) // rows), block)

    received, infos, others, attended_back, kept, in_weights = [], [], [], [], [], []
    for index in range(rounds):
        live = index * span + place // 2 % span < heads
        bounds = jnp.stack([jnp.where(live, lowest, block), jnp.where(live, inner, block)], 1)
        infos.append(jnp.concatenate([core[None], bounds.reshape(-1)]).astype(jnp.int32))
        buffer, weight = project(
            span, counts[index], micros, spot, normed, cos_table, sine_table, *weight_parts[index]
        )
        in_weights.append(weight)
        buffer = buffer.reshape(devices, depth, LANES)
        if index >= 2:
            buffer = after(buffer, kept[index - 2][1])
        received.append(exchange(buffer))
        whole = received[index]
        if index:
            whole = after(whole, kept[index - 1][1])
        others.append(lax.ppermute(whole, "ctx", swap))
        out, lse = attend(infos[index], chosen, received[index], others[index])
        kept.append((out, lse))
    def came_back(pieces):
        joined = pieces[0] if len(pieces) == 1 else jnp.concatenate(pieces, 1)
        joined = exchange(joined)
        return joined.reshape((chips, 2) + joined.shape[1:])

    early = [after(out, received[-1]) for out, _ in kept[:-1]]
    attended_back = ([came_back(early)] if early else []) + [came_back([kept[-1][0]])]

    attended = collect(counts, micros, attended_back)
    result, grad_middle, grad_att, grad_gain_mlp, mid_grads = feed_forward(
        tokens, cotangent, attended, w_out, gain_mlp, w_gate, w_up, w_down
    )
    grads_in = [
        exchange(buffer.reshape((devices,) + buffer.shape[2:]))
        for buffer in spread(span, counts, micros, grad_att)
    ]

    def paired(stay, leave, axis, routes):
        return (stay.astype(F32) + lax.ppermute(leave, axis, routes).astype(F32)).astype(BF16)

    def chip_summed(full, gain=None):
        count, wide = full.shape[0] // (2 * shards), full.shape[1]
        parts = full.reshape(shards, 2, count, wide)
        if gain is not None:
            line = gain.astype(BF16).reshape(shards, 2, 1, -1)
            line = jnp.pad(line, ((0, 0), (0, 0), (0, 63), (0, wide - line.shape[-1])))
            parts = jnp.concatenate([parts, line], 2)
        return paired(pick(parts, core, 1), pick(parts, 1 - core, 1), "ctx", swap)

    def owned(parts):
        if shards == 2:
            return paired(pick(parts, side, 0), pick(parts, 1 - side, 0), "fsdp", cross)
        return lax.psum_scatter(parts, "fsdp", scatter_dimension=0, tiled=False)

    def spaced(part):
        return jnp.where((core == jnp.arange(2))[:, None, None], part[None], 0)

    def totals_of(parts):
        if devices == 16:
            return ctx_sum(parts)
        return list(lax.psum(tuple(spaced(part) for part in parts), "ctx"))

    def opened(total, has_gain):
        wide = total.shape[-1]
        count = total.shape[1] - (64 if has_gain else 0)
        rows_part = total[:, :count].reshape(2 * count, wide).astype(F32)
        if not has_gain:
            return rows_part
        return rows_part, total[:, count, : width // (2 * shards)].reshape(-1).astype(F32)

    grad_out, grad_gate, grad_up, grad_down = mid_grads
    chip_down, chip_gate, chip_up = (chip_summed(grad) for grad in (grad_down, grad_gate, grad_up))
    chip_out = chip_summed(grad_out, grad_gain_mlp)
    mid_parts = [owned(chip) for chip in (chip_out, chip_down, chip_gate, chip_up)]

    grad_back, sent_back = [], []
    waits = {0: (chip_out, chip_down, chip_gate, chip_up), 2: tuple(mid_parts)}
    for index in range(rounds):
        own, away = attend_grad(
            infos[index],
            chosen,
            received[index],
            others[index],
            after(
                grads_in[min(index, 1)], *waits.get(index, ()), *sent_back[-1:], *grad_back[-2:-1]
            ),
            max(index - 1, 0),
            *kept[index],
        )
        back = lax.ppermute(away, "ctx", swap)
        buffer = merge(own, back)
        sent_back.append(buffer)
        grad_back.append(exchange(buffer).reshape(chips, 2, depth, LANES))

    grad_normed, parts = 0.0, []
    for index in range(rounds):
        grad_qkv = collect_grad(counts[index], micros, grad_back[index], cos_table, sine_table)
        grad_normed = grad_normed + jnp.einsum(
            "te,de->td", grad_qkv, in_weights[index], preferred_element_type=F32
        )
        final = index == rounds - 1
        if final:
            grad_in, grad_gain = norm_backward(grad_normed, inputs, recip, gain_attn.astype(F32))
        parts.append(owned(chip_summed(outer(normed, grad_qkv), grad_gain if final else None)))
    totals = totals_of(mid_parts + parts)
    mid_totals, last_totals = totals[: len(mid_parts)], totals[len(mid_parts) :]
    grad_w_out, grad_gain_mlp = opened(mid_totals[0], True)
    grad_w_down, grad_w_gate, grad_w_up = (opened(total, False) for total in mid_totals[1:])
    grad_inputs = (grad_middle + grad_in).astype(BF16)
    opened_last, grad_gain_attn = opened(last_totals[-1], True)
    opened_parts = [opened(total, False) for total in last_totals[:-1]] + [opened_last]
    grad_w_query, grad_w_key, grad_w_value = (
        jnp.concatenate(
            [
                part[:, which * part.shape[1] // 3 : (which + 1) * part.shape[1] // 3]
                for part in opened_parts
            ],
            1,
        )
        for which in range(3)
    )
    shape = (micros, 1, rows, width)
    return (
        result.reshape(shape),
        grad_inputs.reshape(shape),
        grad_gain_attn,
        grad_w_query,
        grad_w_key,
        grad_w_value,
        grad_w_out,
        grad_gain_mlp,
        grad_w_gate,
        grad_w_up,
        grad_w_down,
    )


def solution(mesh):
    weight, gain = P("fsdp", None), P("fsdp")
    rows = P(None, "fsdp", "ctx", None)
    weights = (gain, weight, weight, weight, weight, gain, weight, weight, weight)
    return jax.shard_map(
        body,
        mesh=mesh,
        in_specs=(rows, rows, P(None, "fsdp", None)) + weights,
        out_specs=(rows, rows) + weights,
        check_vma=False,
    )
```

```python
import functools
import math

import jax
import jax.numpy as jnp
from jax import lax
from jax.experimental import pallas as pl
from jax.experimental.pallas import tpu as pltpu
from jax.sharding import PartitionSpec as P

HEAD_DIM = 64
LANES = 128
EPS = 1e-05
NEG = -1e30
LOG2E = math.log2(math.e)
LN2 = math.log(2.0)
F32 = jnp.float32
BF16 = jnp.bfloat16


def dot_nt(left, right):
    return lax.dot_general(left, right, (((1,), (1,)), ((), ())), preferred_element_type=F32)


def dot_nn(left, right):
    return lax.dot_general(left, right, (((1,), (0,)), ((), ())), preferred_element_type=F32)


def dot_tn(left, right):
    return lax.dot_general(left, right, (((0,), (0,)), ((), ())), preferred_element_type=F32)


def lane_index(rows):
    return lax.broadcasted_iota(jnp.int32, (rows, LANES), 1)


def flip(tile):
    return pltpu.roll(tile, HEAD_DIM, 1)


def params(count):
    return pltpu.CompilerParams(
        dimension_semantics=("arbitrary",) * count, vmem_limit_bytes=60 * 1024 * 1024
    )


def full_block(shape):
    zeros = (0,) * len(shape)
    return pl.BlockSpec(shape, lambda *_: zeros)


def pack_pair(tile):
    count = tile.shape[0] // 2
    low = lane_index(count) < HEAD_DIM
    top, bottom = tile[:count], tile[count:]
    return (jnp.where(low, top, flip(bottom)), jnp.where(low, flip(top), bottom))


def unpack_pair(first, second):
    low = lane_index(first.shape[0]) < HEAD_DIM
    top = jnp.where(low, first, flip(second))
    bottom = jnp.where(low, flip(first), second)
    return jnp.concatenate([top, bottom], 0)


def turn(tile):
    near = (lane_index(tile.shape[0]) % HEAD_DIM) < HEAD_DIM // 2
    return jnp.where(
        near, pltpu.roll(tile, LANES - HEAD_DIM // 2, 1), pltpu.roll(tile, HEAD_DIM // 2, 1)
    )


def project_kernel(count, info, n_ref, c_ref, s_ref, *refs):
    *parts, out, w_ref = refs

    @pl.when((pl.program_id(0) == 0) & (pl.program_id(1) == 0))
    def _():
        if len(parts) == 1:
            w_ref[...] = parts[0][...]
            return
        own, near, far = parts
        deep, wide = near.shape
        side, core = info[0], info[1]
        mine = pl.ds(pl.multiple_of(side * deep, deep), deep)
        away = pl.ds(pl.multiple_of((1 - side) * deep, deep), deep)
        w_ref[mine, :] = own[...]
        w_ref[away, pl.ds(pl.multiple_of(core * wide, wide), wide)] = near[...]
        w_ref[away, pl.ds(pl.multiple_of((1 - core) * wide, wide), wide)] = far[...]

    joined = dot_nn(n_ref[...], w_ref[...])
    cos_table, sine_table = c_ref[...], s_ref[...]
    rows = n_ref.shape[0]
    span = count * HEAD_DIM
    low = lane_index(rows) < HEAD_DIM
    for pair in range(count // 2):
        first = pair * LANES
        q2, k2, v2 = (joined[:, part * span + first : part * span + first + LANES] for part in range(3))
        q2 = (q2 * cos_table + turn(q2) * sine_table) * (LOG2E * HEAD_DIM**-0.5)
        k2 = k2 * cos_table + turn(k2) * sine_table
        packed = pack_pair(q2)
        kv = (jnp.where(low, k2, flip(v2)), jnp.where(low, flip(k2), v2))
        for side in range(2):
            out[2 * pair + side, 0, :rows, :] = kv[side].astype(BF16)
            out[2 * pair + side, 0, rows:, :] = packed[side].astype(BF16)
    if count < out.shape[0]:
        out[count:] = jnp.zeros((out.shape[0] - count,) + out.shape[1:], BF16)


def project(span, count, micros, info, normed, cos_table, sine_table, parts, column):
    rows, width = normed.shape
    half = rows // (2 * micros)
    depth = half + half // 2
    wide = parts[0].shape[1]
    return pl.pallas_call(
        functools.partial(project_kernel, count),
        grid_spec=pltpu.PrefetchScalarGridSpec(
            num_scalar_prefetch=1,
            grid=(micros, 2),
            in_specs=[
                pl.BlockSpec((half, width), lambda m, i, *_: (2 * m + i, 0)),
                pl.BlockSpec((half, LANES), lambda m, i, *_: (2 * m + i, 0)),
                pl.BlockSpec((half, LANES), lambda m, i, *_: (2 * m + i, 0)),
            ]
            + [full_block(part.shape) for part in parts[:1]]
            + [
                pl.BlockSpec((part.shape[0], wide // 2), lambda m, i, *_: (0, column))
                for part in parts[1:]
            ],
            out_specs=[
                pl.BlockSpec((span, 1, depth, LANES), lambda m, i, *_: (m, i, 0, 0)),
                full_block((width, wide)),
            ],
        ),
        out_shape=[
            jax.ShapeDtypeStruct((micros * span, 2, depth, LANES), BF16),
            jax.ShapeDtypeStruct((width, wide), BF16),
        ],
        compiler_params=params(2),
        cost_estimate=pl.CostEstimate(
            flops=2 * rows * width * wide, bytes_accessed=4 * rows * width, transcendentals=0
        ),
        name="project",
    )(info, normed, cos_table, sine_table, *parts)


def row_begins(starts_ref, positions):
    begins = jnp.zeros_like(positions)
    for index in range(starts_ref.shape[0]):
        start = starts_ref[index]
        begins = jnp.maximum(begins, jnp.where(positions >= start, start, 0))
    return begins


def unpack_one(packed, lanes_low):
    wide = packed.astype(F32)
    low = lane_index(wide.shape[0]) < HEAD_DIM
    keep = low if lanes_low else jnp.logical_not(low)
    turned = flip(wide)
    first, second = (wide, turned) if lanes_low else (turned, wide)
    return jnp.concatenate(
        [jnp.where(keep, first, 0.0), jnp.where(keep, second, 0.0)], 0
    ).astype(BF16)


def attend_kernel(info, starts, mine, other, o_ref, lse_ref):
    block = pl.program_id(0)
    core = info[0]
    lowest, inner = info[1 + 2 * block], info[2 + 2 * block]
    rows = mine.shape[1] * 2 // 3
    low = lane_index(rows) < HEAD_DIM
    queries = unpack_one(mine[block, rows:, :], True)
    row_pos = (2 * block + core) * rows + lax.broadcasted_iota(jnp.int32, (rows, 1), 0)
    begins = row_begins(starts, row_pos)
    lane_low = lane_index(2 * rows) < HEAD_DIM
    column = lax.broadcasted_iota(jnp.int32, (1, 2 * rows), 1)
    offsets = jnp.where(column < rows, column + core * rows, column - core * rows)

    def keys(index):
        kv = jnp.concatenate([mine[index, :rows, :], other[index, :rows, :]], 0)
        return kv, jnp.where(lane_low, jnp.ones_like(kv), kv)

    def two_steps(index, carry):
        peak, acc = carry
        first, first_v = keys(inner + 2 * index)
        second, second_v = keys(inner + 2 * index + 1)
        scores, more = dot_nt(queries, first), dot_nt(queries, second)
        new_peak = jnp.maximum(peak, jnp.max(jnp.maximum(scores, more), -1, keepdims=True))
        weights, more = jnp.exp2(scores - new_peak), jnp.exp2(more - new_peak)
        acc = acc * jnp.exp2(peak - new_peak) + (
            dot_nn(weights.astype(BF16), first_v) + dot_nn(more.astype(BF16), second_v)
        )
        return (new_peak, acc)

    def step(masked, index, carry):
        peak, acc = carry
        kv, ones_v = keys(index)
        scores = dot_nt(queries, kv)
        if masked:
            key_pos = offsets + index * (2 * rows)
            scores = jnp.where((key_pos >= begins) & (key_pos <= row_pos), scores, NEG)
        new_peak = jnp.maximum(peak, jnp.max(scores, -1, keepdims=True))
        weights = jnp.exp2(scores - new_peak)
        acc = acc * jnp.exp2(peak - new_peak) + dot_nn(weights.astype(BF16), ones_v)
        return (new_peak, acc)

    carry = step(True, block, (jnp.full((rows, 1), NEG, F32), jnp.zeros((rows, LANES), F32)))
    carry = lax.fori_loop(lowest, inner, functools.partial(step, True), carry)
    twice = (block - inner) // 2
    carry = lax.fori_loop(0, twice, two_steps, carry)
    peak, acc = lax.fori_loop(inner + 2 * twice, block, functools.partial(step, False), carry)
    result = acc / flip(acc)
    count = rows // 2
    small_low = lane_index(count) < HEAD_DIM
    o_ref[0] = jnp.where(small_low, flip(result[:count]), result[count:]).astype(BF16)
    lse = jnp.where(low, peak + jnp.log2(acc), 0.0)
    lse_ref[0] = jnp.transpose(lse)[0:1, :]


def attend(info, starts, mine, other):
    blocks, depth, _ = mine.shape
    rows = depth * 2 // 3
    return pl.pallas_call(
        attend_kernel,
        grid_spec=pltpu.PrefetchScalarGridSpec(
            num_scalar_prefetch=2,
            grid=(blocks,),
            in_specs=[
                pl.BlockSpec(mine.shape, lambda i, *_: (0, 0, 0)),
                pl.BlockSpec(other.shape, lambda i, *_: (0, 0, 0)),
            ],
            out_specs=[
                pl.BlockSpec((1, rows // 2, LANES), lambda i, *_: (i, 0, 0)),
                pl.BlockSpec((1, 1, rows), lambda i, *_: (i, 0, 0)),
            ],
        ),
        out_shape=[
            jax.ShapeDtypeStruct((blocks, rows // 2, LANES), BF16),
            jax.ShapeDtypeStruct((blocks, 1, rows), F32),
        ],
        compiler_params=params(1),
        cost_estimate=pl.CostEstimate(
            flops=16 * 10**9, bytes_accessed=10**7, transcendentals=10**7
        ),
        name="attend",
    )(info, starts, mine, other)


def attend_grad_kernel(
    info, starts, mine, other, do_ref, o_ref, lse_ref, dm_ref, dp_ref, acc_mine, acc_other
):
    block = pl.program_id(0)
    core = info[0]
    lowest, inner = info[1 + 2 * block], info[2 + 2 * block]
    rows = mine.shape[1] * 2 // 3
    count = rows // 2

    @pl.when(block == 0)
    def _():
        acc_mine[...] = jnp.zeros_like(acc_mine)
        acc_other[...] = jnp.zeros_like(acc_other)

    queries = unpack_one(mine[block, rows:, :], True)
    grad_out = unpack_one(do_ref[0], False)
    both = jnp.concatenate([queries, grad_out], 0)
    product = jnp.transpose(do_ref[0].astype(F32) * o_ref[0].astype(F32))
    delta = jnp.concatenate(
        [
            jnp.sum(product[:HEAD_DIM], 0, keepdims=True),
            jnp.sum(product[HEAD_DIM:], 0, keepdims=True),
        ],
        1,
    )
    lse = lse_ref[0]
    row_pos = (2 * block + core) * rows + lax.broadcasted_iota(jnp.int32, (1, rows), 1)
    begins = row_begins(starts, row_pos)
    line = lax.broadcasted_iota(jnp.int32, (2 * rows, 1), 0)
    offsets = jnp.where(line < rows, line + core * rows, line - core * rows)

    def step(masked, index, grad_q):
        kv = jnp.concatenate([mine[index, :rows, :], other[index, :rows, :]], 0)
        scores = dot_nt(kv, queries)
        weights = jnp.exp2(scores - lse)
        if masked:
            key_pos = offsets + index * (2 * rows)
            weights = jnp.where((key_pos >= begins) & (key_pos <= row_pos), weights, 0.0)
        grad_weights = dot_nt(kv, grad_out)
        grad_scores = (weights * (grad_weights - delta)).astype(BF16)
        grad_kv = dot_nn(jnp.concatenate([grad_scores, weights.astype(BF16)], 1), both)
        acc_mine[index] += grad_kv[:rows]
        acc_other[index] += grad_kv[rows:]
        return grad_q + dot_tn(grad_scores, kv)

    grad_q = step(True, block, jnp.zeros((rows, LANES), F32))
    grad_q = lax.fori_loop(lowest, inner, functools.partial(step, True), grad_q)
    twice = (block - inner) // 2

    def two_steps(index, grad_q):
        grad_q = step(False, inner + 2 * index, grad_q)
        return step(False, inner + 2 * index + 1, grad_q)

    grad_q = lax.fori_loop(0, twice, two_steps, grad_q)
    grad_q = lax.fori_loop(inner + 2 * twice, block, functools.partial(step, False), grad_q)
    grad_q = grad_q * HEAD_DIM**-0.5
    small_low = lane_index(count) < HEAD_DIM
    dm_ref[block, rows:, :] = jnp.where(small_low, grad_q[:count], flip(grad_q[count:])).astype(
        BF16
    )

    @pl.when(block == pl.num_programs(0) - 1)
    def _():
        scale = jnp.where(lane_index(rows) < HEAD_DIM, LN2, 1.0)

        def flush(index, _):
            dm_ref[index, :rows, :] = (acc_mine[index] * scale).astype(BF16)
            dp_ref[index] = (acc_other[index] * scale).astype(BF16)
            return 0

        lax.fori_loop(0, mine.shape[0], flush, 0)


def attend_grad(info, starts, mine, other, grad_out, spot, out, lse):
    blocks, depth, _ = mine.shape
    rows = depth * 2 // 3
    whole = pl.BlockSpec(mine.shape, lambda i, *_: (0, 0, 0))
    small = pl.BlockSpec((1, rows // 2, LANES), lambda i, *_: (i, 0, 0))
    return pl.pallas_call(
        attend_grad_kernel,
        grid_spec=pltpu.PrefetchScalarGridSpec(
            num_scalar_prefetch=2,
            grid=(blocks,),
            in_specs=[
                whole,
                whole,
                pl.BlockSpec((1, rows // 2, LANES), lambda i, *_: (i, spot, 0)),
                small,
                pl.BlockSpec((1, 1, rows), lambda i, *_: (i, 0, 0)),
            ],
            out_specs=[whole, pl.BlockSpec((blocks, rows, LANES), lambda i, *_: (0, 0, 0))],
            scratch_shapes=[
                pltpu.VMEM((blocks, rows, LANES), F32),
                pltpu.VMEM((blocks, rows, LANES), F32),
            ],
        ),
        out_shape=[
            jax.ShapeDtypeStruct(mine.shape, BF16),
            jax.ShapeDtypeStruct((blocks, rows, LANES), BF16),
        ],
        compiler_params=params(1),
        cost_estimate=pl.CostEstimate(
            flops=32 * 10**9, bytes_accessed=10**7, transcendentals=10**7
        ),
        name="attend_grad",
    )(info, starts, mine, other, grad_out, out, lse)


def merge_kernel(own_ref, back_ref, out):
    rows = back_ref.shape[1]
    out[:, :rows, :] = (own_ref[:, :rows, :].astype(F32) + back_ref[...].astype(F32)).astype(BF16)
    out[:, rows:, :] = own_ref[:, rows:, :]


def merge(own, back):
    blocks, depth, _ = own.shape
    step = blocks // 4
    spec = pl.BlockSpec((step, depth, LANES), lambda i: (i, 0, 0))
    return pl.pallas_call(
        merge_kernel,
        grid=(4,),
        in_specs=[spec, pl.BlockSpec((step, back.shape[1], LANES), lambda i: (i, 0, 0))],
        out_specs=spec,
        out_shape=jax.ShapeDtypeStruct(own.shape, BF16),
        compiler_params=params(1),
        cost_estimate=pl.CostEstimate(flops=0, bytes_accessed=4 * 10**6, transcendentals=0),
        name="merge",
    )(own, back)


def collect_kernel(counts, *refs):
    ins, out = refs[:-1], refs[-1]
    length = out.shape[0] // 2
    pieces = [(array, first) for array in ins for first in range(0, array.shape[2], length)]
    pair = 0
    for (array, first), count in zip(pieces, counts):
        cut = slice(first, first + length)
        for spot in range(0, count, 2):
            tiles = [array[spot + side, 0, cut, :].astype(F32) for side in range(2)]
            out[:, pair * LANES : (pair + 1) * LANES] = unpack_pair(*tiles).astype(BF16)
            pair += 1


def collect(counts, micros, arrays):
    units = arrays[0].shape[0]
    length = sum(array.shape[2] for array in arrays) // len(counts)
    width = sum(counts) * HEAD_DIM
    return pl.pallas_call(
        functools.partial(collect_kernel, counts),
        grid=(micros, 2),
        in_specs=[
            pl.BlockSpec((units // micros, 1, array.shape[2], LANES), lambda m, i: (m, i, 0, 0))
            for array in arrays
        ],
        out_specs=pl.BlockSpec((2 * length, width), lambda m, i: (2 * m + i, 0)),
        out_shape=jax.ShapeDtypeStruct((micros * 4 * length, width), BF16),
        compiler_params=params(2),
        cost_estimate=pl.CostEstimate(flops=0, bytes_accessed=4 * 10**6, transcendentals=0),
        name="collect",
    )(*arrays)


def spread_kernel(counts, x_ref, *outs):
    length = x_ref.shape[0] // 2
    pieces = [(out, first) for out in outs for first in range(0, out.shape[2], length)]
    pair = 0
    for (out, first), count in zip(pieces, counts):
        cut = slice(first, first + length)
        for spot in range(0, count, 2):
            tile = x_ref[:, pair * LANES : (pair + 1) * LANES].astype(F32)
            packed = pack_pair(tile)
            for side in range(2):
                out[spot + side, 0, cut, :] = packed[side].astype(BF16)
            pair += 1
        for spot in range(count, out.shape[0]):
            out[spot, 0, cut, :] = jnp.zeros((length, LANES), BF16)


def spread(span, counts, micros, rows_array):
    rows, width = rows_array.shape
    half = rows // (2 * micros)
    lengths = [half // 2] + ([half // 2 * (len(counts) - 1)] if len(counts) > 1 else [])
    return pl.pallas_call(
        functools.partial(spread_kernel, counts),
        grid=(micros, 2),
        in_specs=[pl.BlockSpec((half, width), lambda m, i: (2 * m + i, 0))],
        out_specs=[
            pl.BlockSpec((span, 1, length, LANES), lambda m, i: (m, i, 0, 0)) for length in lengths
        ],
        out_shape=[
            jax.ShapeDtypeStruct((micros * span, 2, length, LANES), BF16) for length in lengths
        ],
        compiler_params=params(2),
        cost_estimate=pl.CostEstimate(flops=0, bytes_accessed=4 * 10**6, transcendentals=0),
        name="spread",
    )(rows_array)


def turn_back(tile, cos_table, sine_table):
    near = (lane_index(tile.shape[0]) % HEAD_DIM) < HEAD_DIM // 2
    scaled = tile * sine_table
    moved = jnp.where(
        near,
        pltpu.roll(scaled, LANES - HEAD_DIM // 2, 1),
        pltpu.roll(scaled, HEAD_DIM // 2, 1),
    )
    return tile * cos_table + moved


def collect_grad_kernel(count, c_ref, s_ref, in_ref, out):
    cos_table, sine_table = c_ref[...], s_ref[...]
    rows = cos_table.shape[0]
    span = count * HEAD_DIM
    low = lane_index(rows) < HEAD_DIM
    for pair in range(count // 2):
        kvs = [in_ref[2 * pair + side, 0, :rows, :].astype(F32) for side in range(2)]
        packed = [in_ref[2 * pair + side, 0, rows:, :].astype(F32) for side in range(2)]
        grad_k = jnp.where(low, kvs[0], flip(kvs[1]))
        grad_v = jnp.where(low, flip(kvs[0]), kvs[1])
        grad_q = turn_back(unpack_pair(*packed), cos_table, sine_table)
        grad_k = turn_back(grad_k, cos_table, sine_table)
        for part, value in enumerate((grad_q, grad_k, grad_v)):
            first = part * span + pair * LANES
            out[:, first : first + LANES] = value.astype(BF16)


def collect_grad(count, micros, array, cos_table, sine_table):
    units, _, depth, _ = array.shape
    half = depth * 2 // 3
    width = 3 * count * HEAD_DIM
    table = pl.BlockSpec((half, LANES), lambda m, i: (2 * m + i, 0))
    return pl.pallas_call(
        functools.partial(collect_grad_kernel, count),
        grid=(micros, 2),
        in_specs=[
            table,
            table,
            pl.BlockSpec((units // micros, 1, depth, LANES), lambda m, i: (m, i, 0, 0)),
        ],
        out_specs=pl.BlockSpec((half, width), lambda m, i: (2 * m + i, 0)),
        out_shape=jax.ShapeDtypeStruct((micros * 2 * half, width), BF16),
        compiler_params=params(2),
        cost_estimate=pl.CostEstimate(flops=0, bytes_accessed=6 * 10**6, transcendentals=0),
        name="collect_grad",
    )(cos_table, sine_table, array)


SUM_STEPS = 6
PLANE_Z, PLANE_Y, FAR_Z, TWIN, SIDE = 4, 2, 8, 1, 0


def add_rows(out, left, right):
    def step(index, _):
        cut = pl.ds(pl.multiple_of(index * 16, 16), 16)
        out[cut, :] = (left[cut, :].astype(F32) + right[cut, :].astype(F32)).astype(BF16)
        return 0

    lax.fori_loop(0, out.shape[0] // 16, step, 0)


def ctx_sum_kernel(count, *refs):
    ins, outs = list(refs[:count]), refs[count : 2 * count]
    halves, quarters, sums, fars = (refs[(2 + k) * count : (3 + k) * count] for k in range(4))
    twins, crossed, send_sems, recv_sems = refs[6 * count :]
    raw, ins[-1] = ins[-1], crossed
    place = lax.axis_index("ctx")
    side = lax.axis_index("fsdp")

    def bit(weight):
        return place // weight % 2

    def partner(weight):
        if weight == SIDE:
            return (place, 1 - side)
        return (place + weight * (1 - 2 * bit(weight)), side)

    barrier = pltpu.get_barrier_semaphore()
    for weight in (PLANE_Z, PLANE_Y, FAR_Z, TWIN, SIDE):
        pl.semaphore_signal(
            barrier, inc=1, device_id=partner(weight), device_id_type=pl.DeviceIdType.MESH
        )
    pl.semaphore_wait(barrier, 5)

    def send(index, step, source, target, weight):
        copy = pltpu.make_async_remote_copy(
            src_ref=source,
            dst_ref=target,
            send_sem=send_sems.at[index, step],
            recv_sem=recv_sems.at[index, step],
            device_id=partner(weight),
            device_id_type=pl.DeviceIdType.MESH,
        )
        copy.start()
        return copy

    axes = [(PLANE_Z, PLANE_Y) if index % 4 == 2 else (PLANE_Y, PLANE_Z) for index in range(count)]
    core = bit(TWIN)
    started, copies = {}, []

    quarter_range = range(4)
    apart = send(count - 1, SUM_STEPS, raw.at[:, 1 - core], twins, TWIN)
    copies.append(apart)

    def sum_chip():
        apart.wait_recv()
        for owner in range(2):
            for part in quarter_range:
                spot = twins.at[owner, part]
                add_rows(spot, raw.at[owner, core, part], spot)
        copies.append(send(count - 1, SUM_STEPS + 1, twins.at[1 - side], crossed, SIDE))

    def stage(index, step):
        first, second = axes[index]
        if step:
            started[index].wait_recv()
        if step == 0:
            leave = ins[index].at[pl.ds(2 * (1 - bit(first)), 2)]
            target, weight = halves[index], first
        elif step == 1:
            for part in range(2):
                half = halves[index].at[part]
                add_rows(half, ins[index].at[2 * bit(first) + part], half)
            leave, target, weight = halves[index].at[1 - bit(second)], quarters[index], second
        elif step == 2:
            add_rows(sums[index], halves[index].at[bit(second)], quarters[index])
            leave, target, weight = sums[index], fars[index], FAR_Z
        elif step == 3:
            leave = target = outs[index].at[core, 2 * bit(first) + bit(second)]
            weight = second
            add_rows(leave, sums[index], fars[index])
        elif step == 4:
            leave = target = outs[index].at[core, pl.ds(2 * bit(first), 2)]
            weight = first
        elif step == 5:
            leave = target = outs[index].at[core]
            weight = TWIN
        if step < SUM_STEPS:
            started[index] = send(index, step, leave, target, weight)
            copies.append(started[index])

    stage(0, 0)
    stage(1, 0)
    sum_chip()
    across = copies[-1]
    for time in range(2, count + SUM_STEPS + 1):
        if time == count - 1:
            across.wait_recv()
            for part in quarter_range:
                add_rows(crossed.at[part], twins.at[side, part], crossed.at[part])
        if time < count:
            stage(time, 0)
        for step in reversed(range(1, SUM_STEPS + 1)):
            if 0 <= time - step - 1 < count:
                stage(time - step - 1, step)
    for copy in copies:
        copy.wait_send()


def ctx_sum(parts):
    count = len(parts)
    shapes = [(part.shape[-2] // 4, part.shape[-1]) for part in parts]
    sent = sum(6 * part.size for part in parts[:-1])
    vmem = pl.BlockSpec(memory_space=pltpu.VMEM)
    totals = pl.pallas_call(
        functools.partial(ctx_sum_kernel, count),
        in_specs=[vmem] * count,
        out_specs=[vmem] * count,
        out_shape=[jax.ShapeDtypeStruct((2, 4) + shape, BF16) for shape in shapes],
        scratch_shapes=[pltpu.VMEM((2,) + shape, BF16) for shape in shapes]
        + [pltpu.VMEM(shape, BF16) for shape in shapes] * 3
        + [pltpu.VMEM((2, 4) + shapes[-1], BF16), pltpu.VMEM((4,) + shapes[-1], BF16)]
        + [pltpu.SemaphoreType.DMA((count, SUM_STEPS + 2))] * 2,
        compiler_params=pltpu.CompilerParams(
            collective_id=0, has_side_effects=True, vmem_limit_bytes=60 * 1024 * 1024
        ),
        cost_estimate=pl.CostEstimate(flops=0, bytes_accessed=4 * sent, transcendentals=0),
        name="ctx_sum",
    )(*[part.reshape(part.shape[:-2] + (4,) + shape) for part, shape in zip(parts, shapes)])
    return [total.reshape((2,) + part.shape[-2:]) for total, part in zip(totals, parts)]


def matmul(left, right):
    return jnp.dot(left, right, preferred_element_type=F32)


def norm_backward(grad_out, values, recip_rows, gain):
    scaled = grad_out * gain
    grad_in = recip_rows * scaled - values * (recip_rows * recip_rows * recip_rows) * jnp.mean(
        scaled * values, -1, keepdims=True
    )
    return (grad_in, jnp.sum(grad_out * values * recip_rows, 0))


def mlp_kernel(
    n_ref, nt_ref, cot_ref, mid_ref, wg_ref, wu_ref, wd_ref, out, gn_out, gwg_out, gwu_out, gwd_out, acc
):
    index = pl.program_id(0)

    @pl.when(index == 0)
    def _():
        acc[...] = mid_ref[...]
        gn_out[...] = jnp.zeros_like(gn_out)

    gate_pre = dot_nn(n_ref[...], wg_ref[...])
    up_pre = dot_nn(n_ref[...], wu_ref[...])
    grad_hidden = dot_nt(cot_ref[...], wd_ref[...])
    gate_sigmoid = 1.0 / (1.0 + jnp.exp(-gate_pre))
    silu_value = gate_pre * gate_sigmoid
    hidden_low = (silu_value * up_pre).astype(BF16)
    grad_gate = (
        grad_hidden * up_pre * gate_sigmoid * (1.0 + gate_pre * (1.0 - gate_sigmoid))
    ).astype(BF16)
    grad_up = (grad_hidden * silu_value).astype(BF16)
    acc[...] += dot_nn(hidden_low, wd_ref[...])
    gn_out[...] += dot_nt(grad_gate, wg_ref[...]) + dot_nt(grad_up, wu_ref[...])
    gwg_out[...] = dot_nn(nt_ref[...], grad_gate).astype(BF16)
    gwu_out[...] = dot_nn(nt_ref[...], grad_up).astype(BF16)
    gwd_out[...] = dot_tn(hidden_low, cot_ref[...]).astype(BF16)

    @pl.when(index == pl.num_programs(0) - 1)
    def _():
        out[...] = acc[...].astype(BF16)


def mlp(normed, cotangent, middle, w_gate, w_up, w_down):
    rows, width = normed.shape
    units = w_gate.shape[1]
    wide = 256
    across = pl.BlockSpec((width, wide), lambda j: (0, j))
    down = pl.BlockSpec((wide, width), lambda j: (j, 0))
    whole = full_block((rows, width))
    return pl.pallas_call(
        mlp_kernel,
        grid=(units // wide,),
        in_specs=[whole, full_block((width, rows)), whole, whole, across, across, down],
        out_specs=[whole, whole, across, across, down],
        out_shape=[
            jax.ShapeDtypeStruct((rows, width), BF16),
            jax.ShapeDtypeStruct((rows, width), F32),
            jax.ShapeDtypeStruct((width, units), BF16),
            jax.ShapeDtypeStruct((width, units), BF16),
            jax.ShapeDtypeStruct((units, width), BF16),
        ],
        scratch_shapes=[pltpu.VMEM((rows, width), F32)],
        compiler_params=params(1),
        cost_estimate=pl.CostEstimate(
            flops=18 * rows * width * units, bytes_accessed=12 * width * units, transcendentals=0
        ),
        name="mlp",
    )(normed, normed.T, cotangent, middle, w_gate, w_up, w_down)


def feed_forward(tokens, cotangent, attended, w_out, gain_mlp, w_gate, w_up, w_down):
    inputs = tokens.astype(F32)
    gain = gain_mlp.astype(F32)
    middle = inputs + matmul(attended, w_out)
    recip = lax.rsqrt(jnp.mean(middle * middle, -1, keepdims=True) + EPS)
    mlp_low = (middle * recip * gain).astype(BF16)
    result, grad_normed, *grads = mlp(mlp_low, cotangent, middle, w_gate, w_up, w_down)
    grad_mid, grad_gain = norm_backward(grad_normed, middle, recip, gain)
    grad_middle = cotangent.astype(F32) + grad_mid
    grad_branch = grad_middle.astype(BF16)
    grad_att = jnp.einsum("te,de->td", grad_branch, w_out, preferred_element_type=F32).astype(BF16)
    return result, grad_middle, grad_att, grad_gain, [outer(attended, grad_branch), *grads]


def outer(left, right):
    return jnp.einsum("td,te->de", left, right, preferred_element_type=F32).astype(BF16)


def after(value, *others):
    return lax.optimization_barrier((value,) + others)[0]


def body(
    tokens, cotangent, doc_lengths, gain_attn, w_query, w_key, w_value, w_out, gain_mlp, w_gate, w_up, w_down
):
    micros, _, rows, width = tokens.shape
    heads = width // HEAD_DIM
    devices = lax.axis_size("ctx")
    shards = lax.axis_size("fsdp")
    place = lax.axis_index("ctx")
    side = lax.axis_index("fsdp")
    chips = devices // 2
    core = place % 2
    half = rows // 2
    depth = half + half // 2
    span = chips // micros
    rounds = -(-heads // span)
    counts = tuple(min(span, heads - index * span) for index in range(rounds))
    swap = [(i, i ^ 1) for i in range(devices)]
    cross = [(0, 1), (1, 0)]

    def pick(array, index, axis):
        return lax.dynamic_index_in_dim(array, index, axis, keepdims=False)

    def gathered(shard):
        return lax.all_gather(shard, "fsdp", axis=0, tiled=True)

    def fetched(pieces):
        if shards != 2:
            return [([gathered(piece)], 0) for piece in pieces]
        nears = []
        for piece in pieces:
            wide = piece.shape[1] // 2
            nears.append(lax.dynamic_slice_in_dim(piece, core * wide, wide, 1))
        near = nears[0] if len(nears) == 1 else jnp.concatenate(nears, 1)
        near = lax.ppermute(near, "fsdp", cross)
        far = lax.ppermute(near, "ctx", swap)
        return [([piece, near, far], index) for index, piece in enumerate(pieces)]

    def fetched_lines(lines):
        if shards != 2:
            return [gathered(line) for line in lines]
        lines = jnp.stack(lines)
        away = lax.ppermute(lines, "fsdp", cross)
        return jnp.where(
            side == 0, jnp.concatenate([lines, away], 1), jnp.concatenate([away, lines], 1)
        )

    def columns(index):
        cut = slice(index * span * HEAD_DIM, (index * span + counts[index]) * HEAD_DIM)
        return jnp.concatenate([w_query[:, cut], w_key[:, cut], w_value[:, cut]], 1)

    gain_attn, gain_mlp = fetched_lines([gain_attn, gain_mlp])
    weight_parts = fetched([columns(0)])
    if rounds > 1:
        weight_parts += fetched([columns(index) for index in range(1, rounds)])
    spot = jnp.stack([side, core]).astype(jnp.int32)
    w_out, w_gate, w_up, w_down = (
        gathered(after(shard, weight_parts[-1][0][-1])) for shard in (w_out, w_gate, w_up, w_down)
    )
    lengths = doc_lengths[:, 0]
    doc_ends = jnp.cumsum(lengths, -1)
    starts = (doc_ends - lengths).astype(jnp.int32)

    def begins_of(micro_starts, positions):
        reached = positions[:, None] >= micro_starts[None, :]
        return jnp.max(jnp.where(reached, micro_starts[None, :], 0), -1)

    lane = jnp.arange(LANES)
    inverse = jnp.power(10000.0, -(lane % (HEAD_DIM // 2)).astype(F32) / (HEAD_DIM // 2))
    sign = jnp.where((lane % HEAD_DIM) < HEAD_DIM // 2, -1.0, 1.0)
    positions = place * rows + jnp.arange(rows, dtype=jnp.int32)
    offsets = jnp.concatenate(
        [positions - begins_of(starts[micro], positions) for micro in range(micros)]
    ).astype(F32)
    angles = offsets[:, None] * inverse[None, :]
    cos_table, sine_table = jnp.cos(angles), jnp.sin(angles) * sign

    def exchange(buffer):
        return lax.all_to_all(buffer, "ctx", split_axis=0, concat_axis=0, tiled=True)

    tokens = tokens.reshape(micros * rows, width)
    cotangent = cotangent.reshape(micros * rows, width)
    inputs = tokens.astype(F32)
    recip = lax.rsqrt(jnp.mean(inputs * inputs, -1, keepdims=True) + EPS)
    normed = (inputs * recip * gain_attn.astype(F32)).astype(BF16)

    block = jnp.arange(devices, dtype=jnp.int32)
    block_first = block * rows + core * half
    chosen = pick(starts, place // 2 // span, 0)
    lowest = begins_of(chosen, block_first) // rows
    inner = jnp.minimum(-(-begins_of(chosen, block_first + half - 1) // rows), block)

    received, infos, others, attended_back, kept, in_weights = [], [], [], [], [], []
    buffers = []
    for index in range(rounds):
        buffer, weight = project(
            span, counts[index], micros, spot, normed, cos_table, sine_table, *weight_parts[index]
        )
        in_weights.append(weight)
        buffers.append(buffer.reshape(devices, depth, LANES))
    for index in range(rounds):
        live = index * span + place // 2 % span < heads
        bounds = jnp.stack([jnp.where(live, lowest, block), jnp.where(live, inner, block)], 1)
        infos.append(jnp.concatenate([core[None], bounds.reshape(-1)]).astype(jnp.int32))
        buffer = buffers[index]
        if index >= 2:
            buffer = after(buffer, kept[index - 2][1])
        received.append(exchange(buffer))
        whole = received[index]
        whole = after(whole, kept[index - 1][1]) if index else after(whole, *buffers[1:])
        others.append(lax.ppermute(whole, "ctx", swap))
        out, lse = attend(infos[index], chosen, received[index], others[index])
        kept.append((out, lse))
    def came_back(pieces):
        joined = pieces[0] if len(pieces) == 1 else jnp.concatenate(pieces, 1)
        joined = exchange(joined)
        return joined.reshape((chips, 2) + joined.shape[1:])

    early = [after(out, received[-1]) for out, _ in kept[:-1]]
    attended_back = ([came_back(early)] if early else []) + [came_back([kept[-1][0]])]

    attended = collect(counts, micros, attended_back)
    result, grad_middle, grad_att, grad_gain_mlp, mid_grads = feed_forward(
        tokens, cotangent, attended, w_out, gain_mlp, w_gate, w_up, w_down
    )
    grads_in = [
        exchange(buffer.reshape((devices,) + buffer.shape[2:]))
        for buffer in spread(span, counts, micros, grad_att)
    ]

    def paired(stay, leave, axis, routes):
        return (stay.astype(F32) + lax.ppermute(leave, axis, routes).astype(F32)).astype(BF16)

    def split(full, gain=None):
        count, wide = full.shape[0] // (2 * shards), full.shape[1]
        parts = full.reshape(shards, 2, count, wide)
        if gain is not None:
            line = gain.astype(BF16).reshape(shards, 2, 1, -1)
            line = jnp.pad(line, ((0, 0), (0, 0), (0, 63), (0, wide - line.shape[-1])))
            parts = jnp.concatenate([parts, line], 2)
        return parts

    def chip_summed(full, gain=None):
        parts = split(full, gain)
        return paired(pick(parts, core, 1), pick(parts, 1 - core, 1), "ctx", swap)

    def owned(parts):
        if shards == 2:
            return paired(pick(parts, side, 0), pick(parts, 1 - side, 0), "fsdp", cross)
        return lax.psum_scatter(parts, "fsdp", scatter_dimension=0, tiled=False)

    def spaced(part):
        return jnp.where((core == jnp.arange(2))[:, None, None], part[None], 0)

    def totals_of(parts):
        if devices == 16 and shards == 2:
            return ctx_sum(parts)
        return list(lax.psum(tuple(spaced(part) for part in parts), "ctx"))

    def opened(total, has_gain):
        wide = total.shape[-1]
        count = total.shape[1] - (64 if has_gain else 0)
        rows_part = total[:, :count].reshape(2 * count, wide).astype(F32)
        if not has_gain:
            return rows_part
        return rows_part, total[:, count, : width // (2 * shards)].reshape(-1).astype(F32)

    grad_out, grad_gate, grad_up, grad_down = mid_grads
    chip_down, chip_gate, chip_up = (chip_summed(grad) for grad in (grad_down, grad_gate, grad_up))
    chip_out = chip_summed(grad_out, grad_gain_mlp)
    mid_parts = [owned(chip) for chip in (chip_out, chip_down, chip_gate, chip_up)]

    grad_back, sent_back = [], []
    waits = {0: (chip_out, chip_down, chip_gate, chip_up), 2: tuple(mid_parts)}
    for index in range(rounds):
        own, away = attend_grad(
            infos[index],
            chosen,
            received[index],
            others[index],
            after(
                grads_in[min(index, 1)], *waits.get(index, ()), *sent_back[-1:], *grad_back[-2:-1]
            ),
            max(index - 1, 0),
            *kept[index],
        )
        back = lax.ppermute(away, "ctx", swap)
        buffer = merge(own, back)
        sent_back.append(buffer)
        grad_back.append(exchange(buffer).reshape(chips, 2, depth, LANES))

    grad_normed, parts = 0.0, []
    for index in range(rounds):
        grad_qkv = collect_grad(counts[index], micros, grad_back[index], cos_table, sine_table)
        grad_normed = grad_normed + jnp.einsum(
            "te,de->td", grad_qkv, in_weights[index], preferred_element_type=F32
        )
        final = index == rounds - 1
        if final:
            grad_in, grad_gain = norm_backward(grad_normed, inputs, recip, gain_attn.astype(F32))
        grad_weight = outer(normed, grad_qkv)
        if final and devices == 16 and shards == 2:
            parts.append(split(grad_weight, grad_gain))
        else:
            parts.append(owned(chip_summed(grad_weight, grad_gain if final else None)))
    totals = totals_of(mid_parts + parts)
    mid_totals, last_totals = totals[: len(mid_parts)], totals[len(mid_parts) :]
    grad_w_out, grad_gain_mlp = opened(mid_totals[0], True)
    grad_w_down, grad_w_gate, grad_w_up = (opened(total, False) for total in mid_totals[1:])
    grad_inputs = (grad_middle + grad_in).astype(BF16)
    opened_last, grad_gain_attn = opened(last_totals[-1], True)
    opened_parts = [opened(total, False) for total in last_totals[:-1]] + [opened_last]
    grad_w_query, grad_w_key, grad_w_value = (
        jnp.concatenate(
            [
                part[:, which * part.shape[1] // 3 : (which + 1) * part.shape[1] // 3]
                for part in opened_parts
            ],
            1,
        )
        for which in range(3)
    )
    shape = (micros, 1, rows, width)
    return (
        result.reshape(shape),
        grad_inputs.reshape(shape),
        grad_gain_attn,
        grad_w_query,
        grad_w_key,
        grad_w_value,
        grad_w_out,
        grad_gain_mlp,
        grad_w_gate,
        grad_w_up,
        grad_w_down,
    )


def solution(mesh):
    weight, gain = P("fsdp", None), P("fsdp")
    rows = P(None, "fsdp", "ctx", None)
    weights = (gain, weight, weight, weight, weight, gain, weight, weight, weight)
    return jax.shard_map(
        body,
        mesh=mesh,
        in_specs=(rows, rows, P(None, "fsdp", None)) + weights,
        out_specs=(rows, rows) + weights,
        check_vma=False,
    )
```

```python
import functools
import math

import jax
import jax.numpy as jnp
from jax import lax
from jax.experimental import pallas as pl
from jax.experimental.pallas import tpu as pltpu
from jax.sharding import PartitionSpec as P

HEAD_DIM = 64
LANES = 128
EPS = 1e-05
NEG = -1e30
LOG2E = math.log2(math.e)
LN2 = math.log(2.0)
F32 = jnp.float32
BF16 = jnp.bfloat16


def dot_nt(left, right):
    return lax.dot_general(left, right, (((1,), (1,)), ((), ())), preferred_element_type=F32)


def dot_nn(left, right):
    return lax.dot_general(left, right, (((1,), (0,)), ((), ())), preferred_element_type=F32)


def dot_tn(left, right):
    return lax.dot_general(left, right, (((0,), (0,)), ((), ())), preferred_element_type=F32)


def lane_index(rows):
    return lax.broadcasted_iota(jnp.int32, (rows, LANES), 1)


def flip(tile):
    return pltpu.roll(tile, HEAD_DIM, 1)


def params(count):
    return pltpu.CompilerParams(
        dimension_semantics=("arbitrary",) * count, vmem_limit_bytes=60 * 1024 * 1024
    )


def full_block(shape):
    zeros = (0,) * len(shape)
    return pl.BlockSpec(shape, lambda *_: zeros)


def pack_pair(tile):
    count = tile.shape[0] // 2
    low = lane_index(count) < HEAD_DIM
    top, bottom = tile[:count], tile[count:]
    return (jnp.where(low, top, flip(bottom)), jnp.where(low, flip(top), bottom))


def unpack_pair(first, second):
    low = lane_index(first.shape[0]) < HEAD_DIM
    top = jnp.where(low, first, flip(second))
    bottom = jnp.where(low, flip(first), second)
    return jnp.concatenate([top, bottom], 0)


def turn(tile):
    near = (lane_index(tile.shape[0]) % HEAD_DIM) < HEAD_DIM // 2
    return jnp.where(
        near, pltpu.roll(tile, LANES - HEAD_DIM // 2, 1), pltpu.roll(tile, HEAD_DIM // 2, 1)
    )


def project_kernel(count, info, n_ref, c_ref, s_ref, *refs):
    *parts, out, w_ref = refs

    @pl.when((pl.program_id(0) == 0) & (pl.program_id(1) == 0))
    def _():
        if len(parts) == 1:
            w_ref[...] = parts[0][...]
            return
        own, near, far = parts
        deep, wide = near.shape
        side, core = info[0], info[1]
        mine = pl.ds(pl.multiple_of(side * deep, deep), deep)
        away = pl.ds(pl.multiple_of((1 - side) * deep, deep), deep)
        w_ref[mine, :] = own[...]
        w_ref[away, pl.ds(pl.multiple_of(core * wide, wide), wide)] = near[...]
        w_ref[away, pl.ds(pl.multiple_of((1 - core) * wide, wide), wide)] = far[...]

    joined = dot_nn(n_ref[...], w_ref[...])
    cos_table, sine_table = c_ref[...], s_ref[...]
    rows = n_ref.shape[0]
    span = count * HEAD_DIM
    low = lane_index(rows) < HEAD_DIM
    for pair in range(count // 2):
        first = pair * LANES
        q2, k2, v2 = (joined[:, part * span + first : part * span + first + LANES] for part in range(3))
        q2 = (q2 * cos_table + turn(q2) * sine_table) * (LOG2E * HEAD_DIM**-0.5)
        k2 = k2 * cos_table + turn(k2) * sine_table
        packed = pack_pair(q2)
        kv = (jnp.where(low, k2, flip(v2)), jnp.where(low, flip(k2), v2))
        for side in range(2):
            out[2 * pair + side, 0, :rows, :] = kv[side].astype(BF16)
            out[2 * pair + side, 0, rows:, :] = packed[side].astype(BF16)
    if count < out.shape[0]:
        out[count:] = jnp.zeros((out.shape[0] - count,) + out.shape[1:], BF16)


def project(span, count, micros, info, normed, cos_table, sine_table, parts, column):
    rows, width = normed.shape
    half = rows // (2 * micros)
    depth = half + half // 2
    wide = parts[0].shape[1]
    return pl.pallas_call(
        functools.partial(project_kernel, count),
        grid_spec=pltpu.PrefetchScalarGridSpec(
            num_scalar_prefetch=1,
            grid=(micros, 2),
            in_specs=[
                pl.BlockSpec((half, width), lambda m, i, *_: (2 * m + i, 0)),
                pl.BlockSpec((half, LANES), lambda m, i, *_: (2 * m + i, 0)),
                pl.BlockSpec((half, LANES), lambda m, i, *_: (2 * m + i, 0)),
            ]
            + [full_block(part.shape) for part in parts[:1]]
            + [
                pl.BlockSpec((part.shape[0], wide // 2), lambda m, i, *_: (0, column))
                for part in parts[1:]
            ],
            out_specs=[
                pl.BlockSpec((span, 1, depth, LANES), lambda m, i, *_: (m, i, 0, 0)),
                full_block((width, wide)),
            ],
        ),
        out_shape=[
            jax.ShapeDtypeStruct((micros * span, 2, depth, LANES), BF16),
            jax.ShapeDtypeStruct((width, wide), BF16),
        ],
        compiler_params=params(2),
        cost_estimate=pl.CostEstimate(
            flops=2 * rows * width * wide, bytes_accessed=4 * rows * width, transcendentals=0
        ),
        name="project",
    )(info, normed, cos_table, sine_table, *parts)


def row_begins(starts_ref, positions):
    begins = jnp.zeros_like(positions)
    for index in range(starts_ref.shape[0]):
        start = starts_ref[index]
        begins = jnp.maximum(begins, jnp.where(positions >= start, start, 0))
    return begins


def unpack_one(packed, lanes_low):
    wide = packed.astype(F32)
    low = lane_index(wide.shape[0]) < HEAD_DIM
    keep = low if lanes_low else jnp.logical_not(low)
    turned = flip(wide)
    first, second = (wide, turned) if lanes_low else (turned, wide)
    return jnp.concatenate(
        [jnp.where(keep, first, 0.0), jnp.where(keep, second, 0.0)], 0
    ).astype(BF16)


def attend_kernel(info, starts, mine, other, o_ref, lse_ref):
    block = pl.program_id(0)
    core = info[0]
    lowest, inner = info[1 + 2 * block], info[2 + 2 * block]
    rows = mine.shape[1] * 2 // 3
    low = lane_index(rows) < HEAD_DIM
    queries = unpack_one(mine[block, rows:, :], True)
    row_pos = (2 * block + core) * rows + lax.broadcasted_iota(jnp.int32, (rows, 1), 0)
    begins = row_begins(starts, row_pos)
    lane_low = lane_index(2 * rows) < HEAD_DIM
    column = lax.broadcasted_iota(jnp.int32, (1, 2 * rows), 1)
    offsets = jnp.where(column < rows, column + core * rows, column - core * rows)

    def keys(index):
        kv = jnp.concatenate([mine[index, :rows, :], other[index, :rows, :]], 0)
        return kv, jnp.where(lane_low, jnp.ones_like(kv), kv)

    def two_steps(index, carry):
        peak, acc = carry
        first, first_v = keys(inner + 2 * index)
        second, second_v = keys(inner + 2 * index + 1)
        scores, more = dot_nt(queries, first), dot_nt(queries, second)
        new_peak = jnp.maximum(peak, jnp.max(jnp.maximum(scores, more), -1, keepdims=True))
        weights, more = jnp.exp2(scores - new_peak), jnp.exp2(more - new_peak)
        acc = acc * jnp.exp2(peak - new_peak) + (
            dot_nn(weights.astype(BF16), first_v) + dot_nn(more.astype(BF16), second_v)
        )
        return (new_peak, acc)

    def step(masked, index, carry):
        peak, acc = carry
        kv, ones_v = keys(index)
        scores = dot_nt(queries, kv)
        if masked:
            key_pos = offsets + index * (2 * rows)
            scores = jnp.where((key_pos >= begins) & (key_pos <= row_pos), scores, NEG)
        new_peak = jnp.maximum(peak, jnp.max(scores, -1, keepdims=True))
        weights = jnp.exp2(scores - new_peak)
        acc = acc * jnp.exp2(peak - new_peak) + dot_nn(weights.astype(BF16), ones_v)
        return (new_peak, acc)

    carry = step(True, block, (jnp.full((rows, 1), NEG, F32), jnp.zeros((rows, LANES), F32)))
    carry = lax.fori_loop(lowest, inner, functools.partial(step, True), carry)
    twice = (block - inner) // 2
    carry = lax.fori_loop(0, twice, two_steps, carry)
    peak, acc = lax.fori_loop(inner + 2 * twice, block, functools.partial(step, False), carry)
    result = acc / flip(acc)
    count = rows // 2
    small_low = lane_index(count) < HEAD_DIM
    o_ref[0] = jnp.where(small_low, flip(result[:count]), result[count:]).astype(BF16)
    lse = jnp.where(low, peak + jnp.log2(acc), 0.0)
    lse_ref[0] = jnp.transpose(lse)[0:1, :]


def attend(info, starts, mine, other):
    blocks, depth, _ = mine.shape
    rows = depth * 2 // 3
    return pl.pallas_call(
        attend_kernel,
        grid_spec=pltpu.PrefetchScalarGridSpec(
            num_scalar_prefetch=2,
            grid=(blocks,),
            in_specs=[
                pl.BlockSpec(mine.shape, lambda i, *_: (0, 0, 0)),
                pl.BlockSpec(other.shape, lambda i, *_: (0, 0, 0)),
            ],
            out_specs=[
                pl.BlockSpec((1, rows // 2, LANES), lambda i, *_: (i, 0, 0)),
                pl.BlockSpec((1, 1, rows), lambda i, *_: (i, 0, 0)),
            ],
        ),
        out_shape=[
            jax.ShapeDtypeStruct((blocks, rows // 2, LANES), BF16),
            jax.ShapeDtypeStruct((blocks, 1, rows), F32),
        ],
        compiler_params=params(1),
        cost_estimate=pl.CostEstimate(
            flops=16 * 10**9, bytes_accessed=10**7, transcendentals=10**7
        ),
        name="attend",
    )(info, starts, mine, other)


def attend_grad_kernel(
    info, starts, mine, other, do_ref, o_ref, lse_ref, dm_ref, dp_ref, acc_mine, acc_other
):
    block = pl.program_id(0)
    core = info[0]
    lowest, inner = info[1 + 2 * block], info[2 + 2 * block]
    rows = mine.shape[1] * 2 // 3
    count = rows // 2

    @pl.when(block == 0)
    def _():
        acc_mine[...] = jnp.zeros_like(acc_mine)
        acc_other[...] = jnp.zeros_like(acc_other)

    queries = unpack_one(mine[block, rows:, :], True)
    grad_out = unpack_one(do_ref[0], False)
    both = jnp.concatenate([queries, grad_out], 0)
    product = jnp.transpose(do_ref[0].astype(F32) * o_ref[0].astype(F32))
    delta = jnp.concatenate(
        [
            jnp.sum(product[:HEAD_DIM], 0, keepdims=True),
            jnp.sum(product[HEAD_DIM:], 0, keepdims=True),
        ],
        1,
    )
    lse = lse_ref[0]
    row_pos = (2 * block + core) * rows + lax.broadcasted_iota(jnp.int32, (1, rows), 1)
    begins = row_begins(starts, row_pos)
    line = lax.broadcasted_iota(jnp.int32, (2 * rows, 1), 0)
    offsets = jnp.where(line < rows, line + core * rows, line - core * rows)

    def step(masked, index, grad_q):
        kv = jnp.concatenate([mine[index, :rows, :], other[index, :rows, :]], 0)
        scores = dot_nt(kv, queries)
        weights = jnp.exp2(scores - lse)
        if masked:
            key_pos = offsets + index * (2 * rows)
            weights = jnp.where((key_pos >= begins) & (key_pos <= row_pos), weights, 0.0)
        grad_weights = dot_nt(kv, grad_out)
        grad_scores = (weights * (grad_weights - delta)).astype(BF16)
        grad_kv = dot_nn(jnp.concatenate([grad_scores, weights.astype(BF16)], 1), both)
        acc_mine[index] += grad_kv[:rows]
        acc_other[index] += grad_kv[rows:]
        return grad_q + dot_tn(grad_scores, kv)

    grad_q = step(True, block, jnp.zeros((rows, LANES), F32))
    grad_q = lax.fori_loop(lowest, inner, functools.partial(step, True), grad_q)
    twice = (block - inner) // 2

    def two_steps(index, grad_q):
        grad_q = step(False, inner + 2 * index, grad_q)
        return step(False, inner + 2 * index + 1, grad_q)

    grad_q = lax.fori_loop(0, twice, two_steps, grad_q)
    grad_q = lax.fori_loop(inner + 2 * twice, block, functools.partial(step, False), grad_q)
    grad_q = grad_q * HEAD_DIM**-0.5
    small_low = lane_index(count) < HEAD_DIM
    dm_ref[block, rows:, :] = jnp.where(small_low, grad_q[:count], flip(grad_q[count:])).astype(
        BF16
    )

    @pl.when(block == pl.num_programs(0) - 1)
    def _():
        scale = jnp.where(lane_index(rows) < HEAD_DIM, LN2, 1.0)

        def flush(index, _):
            dm_ref[index, :rows, :] = (acc_mine[index] * scale).astype(BF16)
            dp_ref[index] = (acc_other[index] * scale).astype(BF16)
            return 0

        lax.fori_loop(0, mine.shape[0], flush, 0)


def attend_grad(info, starts, mine, other, grad_out, spot, out, lse):
    blocks, depth, _ = mine.shape
    rows = depth * 2 // 3
    whole = pl.BlockSpec(mine.shape, lambda i, *_: (0, 0, 0))
    small = pl.BlockSpec((1, rows // 2, LANES), lambda i, *_: (i, 0, 0))
    return pl.pallas_call(
        attend_grad_kernel,
        grid_spec=pltpu.PrefetchScalarGridSpec(
            num_scalar_prefetch=2,
            grid=(blocks,),
            in_specs=[
                whole,
                whole,
                pl.BlockSpec((1, rows // 2, LANES), lambda i, *_: (i, spot, 0)),
                small,
                pl.BlockSpec((1, 1, rows), lambda i, *_: (i, 0, 0)),
            ],
            out_specs=[whole, pl.BlockSpec((blocks, rows, LANES), lambda i, *_: (0, 0, 0))],
            scratch_shapes=[
                pltpu.VMEM((blocks, rows, LANES), F32),
                pltpu.VMEM((blocks, rows, LANES), F32),
            ],
        ),
        out_shape=[
            jax.ShapeDtypeStruct(mine.shape, BF16),
            jax.ShapeDtypeStruct((blocks, rows, LANES), BF16),
        ],
        compiler_params=params(1),
        cost_estimate=pl.CostEstimate(
            flops=32 * 10**9, bytes_accessed=10**7, transcendentals=10**7
        ),
        name="attend_grad",
    )(info, starts, mine, other, grad_out, out, lse)


def merge_kernel(own_ref, back_ref, out):
    rows = back_ref.shape[1]
    out[:, :rows, :] = (own_ref[:, :rows, :].astype(F32) + back_ref[...].astype(F32)).astype(BF16)
    out[:, rows:, :] = own_ref[:, rows:, :]


def merge(own, back):
    blocks, depth, _ = own.shape
    step = blocks // 4
    spec = pl.BlockSpec((step, depth, LANES), lambda i: (i, 0, 0))
    return pl.pallas_call(
        merge_kernel,
        grid=(4,),
        in_specs=[spec, pl.BlockSpec((step, back.shape[1], LANES), lambda i: (i, 0, 0))],
        out_specs=spec,
        out_shape=jax.ShapeDtypeStruct(own.shape, BF16),
        compiler_params=params(1),
        cost_estimate=pl.CostEstimate(flops=0, bytes_accessed=4 * 10**6, transcendentals=0),
        name="merge",
    )(own, back)


def collect_kernel(counts, *refs):
    ins, out = refs[:-1], refs[-1]
    length = out.shape[0] // 2
    pieces = [(array, first) for array in ins for first in range(0, array.shape[2], length)]
    pair = 0
    for (array, first), count in zip(pieces, counts):
        cut = slice(first, first + length)
        for spot in range(0, count, 2):
            tiles = [array[spot + side, 0, cut, :].astype(F32) for side in range(2)]
            out[:, pair * LANES : (pair + 1) * LANES] = unpack_pair(*tiles).astype(BF16)
            pair += 1


def collect(counts, micros, arrays):
    units = arrays[0].shape[0]
    length = sum(array.shape[2] for array in arrays) // len(counts)
    width = sum(counts) * HEAD_DIM
    return pl.pallas_call(
        functools.partial(collect_kernel, counts),
        grid=(micros, 2),
        in_specs=[
            pl.BlockSpec((units // micros, 1, array.shape[2], LANES), lambda m, i: (m, i, 0, 0))
            for array in arrays
        ],
        out_specs=pl.BlockSpec((2 * length, width), lambda m, i: (2 * m + i, 0)),
        out_shape=jax.ShapeDtypeStruct((micros * 4 * length, width), BF16),
        compiler_params=params(2),
        cost_estimate=pl.CostEstimate(flops=0, bytes_accessed=4 * 10**6, transcendentals=0),
        name="collect",
    )(*arrays)


def spread_kernel(counts, x_ref, *outs):
    length = x_ref.shape[0] // 2
    pieces = [(out, first) for out in outs for first in range(0, out.shape[2], length)]
    pair = 0
    for (out, first), count in zip(pieces, counts):
        cut = slice(first, first + length)
        for spot in range(0, count, 2):
            tile = x_ref[:, pair * LANES : (pair + 1) * LANES].astype(F32)
            packed = pack_pair(tile)
            for side in range(2):
                out[spot + side, 0, cut, :] = packed[side].astype(BF16)
            pair += 1
        for spot in range(count, out.shape[0]):
            out[spot, 0, cut, :] = jnp.zeros((length, LANES), BF16)


def spread(span, counts, micros, rows_array):
    rows, width = rows_array.shape
    half = rows // (2 * micros)
    lengths = [half // 2] + ([half // 2 * (len(counts) - 1)] if len(counts) > 1 else [])
    return pl.pallas_call(
        functools.partial(spread_kernel, counts),
        grid=(micros, 2),
        in_specs=[pl.BlockSpec((half, width), lambda m, i: (2 * m + i, 0))],
        out_specs=[
            pl.BlockSpec((span, 1, length, LANES), lambda m, i: (m, i, 0, 0)) for length in lengths
        ],
        out_shape=[
            jax.ShapeDtypeStruct((micros * span, 2, length, LANES), BF16) for length in lengths
        ],
        compiler_params=params(2),
        cost_estimate=pl.CostEstimate(flops=0, bytes_accessed=4 * 10**6, transcendentals=0),
        name="spread",
    )(rows_array)


def turn_back(tile, cos_table, sine_table):
    near = (lane_index(tile.shape[0]) % HEAD_DIM) < HEAD_DIM // 2
    scaled = tile * sine_table
    moved = jnp.where(
        near,
        pltpu.roll(scaled, LANES - HEAD_DIM // 2, 1),
        pltpu.roll(scaled, HEAD_DIM // 2, 1),
    )
    return tile * cos_table + moved


def collect_grad_kernel(count, c_ref, s_ref, in_ref, out):
    cos_table, sine_table = c_ref[...], s_ref[...]
    rows = cos_table.shape[0]
    span = count * HEAD_DIM
    low = lane_index(rows) < HEAD_DIM
    for pair in range(count // 2):
        kvs = [in_ref[2 * pair + side, 0, :rows, :].astype(F32) for side in range(2)]
        packed = [in_ref[2 * pair + side, 0, rows:, :].astype(F32) for side in range(2)]
        grad_k = jnp.where(low, kvs[0], flip(kvs[1]))
        grad_v = jnp.where(low, flip(kvs[0]), kvs[1])
        grad_q = turn_back(unpack_pair(*packed), cos_table, sine_table)
        grad_k = turn_back(grad_k, cos_table, sine_table)
        for part, value in enumerate((grad_q, grad_k, grad_v)):
            first = part * span + pair * LANES
            out[:, first : first + LANES] = value.astype(BF16)


def collect_grad(count, micros, array, cos_table, sine_table):
    units, _, depth, _ = array.shape
    half = depth * 2 // 3
    width = 3 * count * HEAD_DIM
    table = pl.BlockSpec((half, LANES), lambda m, i: (2 * m + i, 0))
    return pl.pallas_call(
        functools.partial(collect_grad_kernel, count),
        grid=(micros, 2),
        in_specs=[
            table,
            table,
            pl.BlockSpec((units // micros, 1, depth, LANES), lambda m, i: (m, i, 0, 0)),
        ],
        out_specs=pl.BlockSpec((half, width), lambda m, i: (2 * m + i, 0)),
        out_shape=jax.ShapeDtypeStruct((micros * 2 * half, width), BF16),
        compiler_params=params(2),
        cost_estimate=pl.CostEstimate(flops=0, bytes_accessed=6 * 10**6, transcendentals=0),
        name="collect_grad",
    )(cos_table, sine_table, array)


SUM_STEPS = 6
PLANE_Z, PLANE_Y, FAR_Z, TWIN = 4, 2, 8, 1


def add_rows(out, left, right):
    def step(index, _):
        cut = pl.ds(pl.multiple_of(index * 16, 16), 16)
        out[cut, :] = (left[cut, :].astype(F32) + right[cut, :].astype(F32)).astype(BF16)
        return 0

    lax.fori_loop(0, out.shape[0] // 16, step, 0)


def ctx_sum_kernel(count, *refs):
    ins, outs = refs[:count], refs[count : 2 * count]
    halves, quarters, sums, fars = (refs[(2 + k) * count : (3 + k) * count] for k in range(4))
    send_sems, recv_sems = refs[6 * count :]
    place = lax.axis_index("ctx")
    side = lax.axis_index("fsdp")

    def bit(weight):
        return place // weight % 2

    def partner(weight):
        return (place + weight * (1 - 2 * bit(weight)), side)

    barrier = pltpu.get_barrier_semaphore()
    for weight in (PLANE_Z, PLANE_Y, FAR_Z, TWIN):
        pl.semaphore_signal(
            barrier, inc=1, device_id=partner(weight), device_id_type=pl.DeviceIdType.MESH
        )
    pl.semaphore_wait(barrier, 4)

    def send(index, step, source, target, weight):
        copy = pltpu.make_async_remote_copy(
            src_ref=source,
            dst_ref=target,
            send_sem=send_sems.at[index, step],
            recv_sem=recv_sems.at[index, step],
            device_id=partner(weight),
            device_id_type=pl.DeviceIdType.MESH,
        )
        copy.start()
        return copy

    axes = [(PLANE_Z, PLANE_Y) if index % 4 == 2 else (PLANE_Y, PLANE_Z) for index in range(count)]
    core = bit(TWIN)
    started, copies = {}, []

    def stage(index, step):
        first, second = axes[index]
        if step:
            started[index].wait_recv()
        if step == 0:
            leave = ins[index].at[pl.ds(2 * (1 - bit(first)), 2)]
            target, weight = halves[index], first
        elif step == 1:
            for part in range(2):
                half = halves[index].at[part]
                add_rows(half, ins[index].at[2 * bit(first) + part], half)
            leave, target, weight = halves[index].at[1 - bit(second)], quarters[index], second
        elif step == 2:
            add_rows(sums[index], halves[index].at[bit(second)], quarters[index])
            leave, target, weight = sums[index], fars[index], FAR_Z
        elif step == 3:
            leave = target = outs[index].at[core, 2 * bit(first) + bit(second)]
            weight = second
            add_rows(leave, sums[index], fars[index])
        elif step == 4:
            leave = target = outs[index].at[core, pl.ds(2 * bit(first), 2)]
            weight = first
        elif step == 5:
            leave = target = outs[index].at[core]
            weight = TWIN
        if step < SUM_STEPS:
            started[index] = send(index, step, leave, target, weight)
            copies.append(started[index])

    for time in range(count + SUM_STEPS + 1):
        if time < count:
            stage(time, 0)
        for step in reversed(range(1, SUM_STEPS + 1)):
            if 0 <= time - step - 1 < count:
                stage(time - step - 1, step)
    for copy in copies:
        copy.wait_send()


def ctx_sum(parts):
    count = len(parts)
    shapes = [(part.shape[0] // 4, part.shape[1]) for part in parts]
    sent = sum(6 * part.size for part in parts)
    vmem = pl.BlockSpec(memory_space=pltpu.VMEM)
    totals = pl.pallas_call(
        functools.partial(ctx_sum_kernel, count),
        in_specs=[vmem] * count,
        out_specs=[vmem] * count,
        out_shape=[jax.ShapeDtypeStruct((2, 4) + shape, BF16) for shape in shapes],
        scratch_shapes=[pltpu.VMEM((2,) + shape, BF16) for shape in shapes]
        + [pltpu.VMEM(shape, BF16) for shape in shapes] * 3
        + [pltpu.SemaphoreType.DMA((count, SUM_STEPS))] * 2,
        compiler_params=pltpu.CompilerParams(
            collective_id=0, has_side_effects=True, vmem_limit_bytes=60 * 1024 * 1024
        ),
        cost_estimate=pl.CostEstimate(flops=0, bytes_accessed=4 * sent, transcendentals=0),
        name="ctx_sum",
    )(*[part.reshape((4,) + shape) for part, shape in zip(parts, shapes)])
    return [total.reshape((2,) + part.shape) for total, part in zip(totals, parts)]


def matmul(left, right):
    return jnp.dot(left, right, preferred_element_type=F32)


def norm_backward(grad_out, values, recip_rows, gain):
    scaled = grad_out * gain
    grad_in = recip_rows * scaled - values * (recip_rows * recip_rows * recip_rows) * jnp.mean(
        scaled * values, -1, keepdims=True
    )
    return (grad_in, jnp.sum(grad_out * values * recip_rows, 0))


def mlp_kernel(
    n_ref, nt_ref, cot_ref, mid_ref, wg_ref, wu_ref, wd_ref, out, gn_out, gwg_out, gwu_out, gwd_out, acc
):
    index = pl.program_id(0)

    @pl.when(index == 0)
    def _():
        acc[...] = mid_ref[...]
        gn_out[...] = jnp.zeros_like(gn_out)

    gate_pre = dot_nn(n_ref[...], wg_ref[...])
    up_pre = dot_nn(n_ref[...], wu_ref[...])
    grad_hidden = dot_nt(cot_ref[...], wd_ref[...])
    gate_sigmoid = 1.0 / (1.0 + jnp.exp(-gate_pre))
    silu_value = gate_pre * gate_sigmoid
    hidden_low = (silu_value * up_pre).astype(BF16)
    grad_gate = (
        grad_hidden * up_pre * gate_sigmoid * (1.0 + gate_pre * (1.0 - gate_sigmoid))
    ).astype(BF16)
    grad_up = (grad_hidden * silu_value).astype(BF16)
    acc[...] += dot_nn(hidden_low, wd_ref[...])
    gn_out[...] += dot_nt(grad_gate, wg_ref[...]) + dot_nt(grad_up, wu_ref[...])
    gwg_out[...] = dot_nn(nt_ref[...], grad_gate).astype(BF16)
    gwu_out[...] = dot_nn(nt_ref[...], grad_up).astype(BF16)
    gwd_out[...] = dot_tn(hidden_low, cot_ref[...]).astype(BF16)

    @pl.when(index == pl.num_programs(0) - 1)
    def _():
        out[...] = acc[...].astype(BF16)


def mlp(normed, cotangent, middle, w_gate, w_up, w_down):
    rows, width = normed.shape
    units = w_gate.shape[1]
    wide = 256
    across = pl.BlockSpec((width, wide), lambda j: (0, j))
    down = pl.BlockSpec((wide, width), lambda j: (j, 0))
    whole = full_block((rows, width))
    return pl.pallas_call(
        mlp_kernel,
        grid=(units // wide,),
        in_specs=[whole, full_block((width, rows)), whole, whole, across, across, down],
        out_specs=[whole, whole, across, across, down],
        out_shape=[
            jax.ShapeDtypeStruct((rows, width), BF16),
            jax.ShapeDtypeStruct((rows, width), F32),
            jax.ShapeDtypeStruct((width, units), BF16),
            jax.ShapeDtypeStruct((width, units), BF16),
            jax.ShapeDtypeStruct((units, width), BF16),
        ],
        scratch_shapes=[pltpu.VMEM((rows, width), F32)],
        compiler_params=params(1),
        cost_estimate=pl.CostEstimate(
            flops=18 * rows * width * units, bytes_accessed=12 * width * units, transcendentals=0
        ),
        name="mlp",
    )(normed, normed.T, cotangent, middle, w_gate, w_up, w_down)


def feed_forward(tokens, cotangent, attended, w_out, gain_mlp, w_gate, w_up, w_down):
    inputs = tokens.astype(F32)
    gain = gain_mlp.astype(F32)
    middle = inputs + matmul(attended, w_out)
    recip = lax.rsqrt(jnp.mean(middle * middle, -1, keepdims=True) + EPS)
    mlp_low = (middle * recip * gain).astype(BF16)
    result, grad_normed, *grads = mlp(mlp_low, cotangent, middle, w_gate, w_up, w_down)
    grad_mid, grad_gain = norm_backward(grad_normed, middle, recip, gain)
    grad_middle = cotangent.astype(F32) + grad_mid
    grad_branch = grad_middle.astype(BF16)
    grad_att = jnp.einsum("te,de->td", grad_branch, w_out, preferred_element_type=F32).astype(BF16)
    return result, grad_middle, grad_att, grad_gain, [outer(attended, grad_branch), *grads]


def widen_kernel(mids, *refs):
    ins, outs = refs[: len(refs) - mids - 3], refs[len(refs) - mids - 3 :]
    for source, out in zip(ins[:mids], outs[:mids]):
        out[...] = source[0, : out.shape[0], :].astype(F32)
    first = 0
    for source in ins[mids:]:
        wide = source.shape[2] // 3
        for which in range(3):
            out = outs[mids + which]
            piece = source[0, : out.shape[0], which * wide : (which + 1) * wide]
            out[:, first : first + wide] = piece.astype(F32)
        first += wide


def widen(mid_totals, round_totals, counts, width):
    totals = [*mid_totals, *round_totals]
    shapes = [(count, total.shape[2]) for count, total in zip(counts, mid_totals)]
    shapes += [(counts[-1], width)] * 3
    return pl.pallas_call(
        functools.partial(widen_kernel, len(mid_totals)),
        grid=(2,),
        in_specs=[pl.BlockSpec((1,) + total.shape[1:], lambda i: (i, 0, 0)) for total in totals],
        out_specs=[pl.BlockSpec(shape, lambda i: (i, 0)) for shape in shapes],
        out_shape=[jax.ShapeDtypeStruct((2 * rows, wide), F32) for rows, wide in shapes],
        compiler_params=params(1),
        cost_estimate=pl.CostEstimate(flops=0, bytes_accessed=2 * 10**7, transcendentals=0),
        name="widen",
    )(*totals)


def outer(left, right):
    return jnp.einsum("td,te->de", left, right, preferred_element_type=F32).astype(BF16)


def after(value, *others):
    return lax.optimization_barrier((value,) + others)[0]


def body(
    tokens, cotangent, doc_lengths, gain_attn, w_query, w_key, w_value, w_out, gain_mlp, w_gate, w_up, w_down
):
    micros, _, rows, width = tokens.shape
    heads = width // HEAD_DIM
    devices = lax.axis_size("ctx")
    shards = lax.axis_size("fsdp")
    place = lax.axis_index("ctx")
    side = lax.axis_index("fsdp")
    chips = devices // 2
    core = place % 2
    half = rows // 2
    depth = half + half // 2
    span = chips // micros
    rounds = -(-heads // span)
    counts = tuple(min(span, heads - index * span) for index in range(rounds))
    swap = [(i, i ^ 1) for i in range(devices)]
    cross = [(0, 1), (1, 0)]

    def pick(array, index, axis):
        return lax.dynamic_index_in_dim(array, index, axis, keepdims=False)

    def gathered(shard):
        return lax.all_gather(shard, "fsdp", axis=0, tiled=True)

    def fetched(pieces):
        if shards != 2:
            return [([gathered(piece)], 0) for piece in pieces]
        nears = []
        for piece in pieces:
            wide = piece.shape[1] // 2
            nears.append(lax.dynamic_slice_in_dim(piece, core * wide, wide, 1))
        near = nears[0] if len(nears) == 1 else jnp.concatenate(nears, 1)
        near = lax.ppermute(near, "fsdp", cross)
        far = lax.ppermute(near, "ctx", swap)
        return [([piece, near, far], index) for index, piece in enumerate(pieces)]

    def fetched_lines(lines):
        if shards != 2:
            return [gathered(line) for line in lines]
        lines = jnp.stack(lines)
        away = lax.ppermute(lines, "fsdp", cross)
        return jnp.where(
            side == 0, jnp.concatenate([lines, away], 1), jnp.concatenate([away, lines], 1)
        )

    def columns(index):
        cut = slice(index * span * HEAD_DIM, (index * span + counts[index]) * HEAD_DIM)
        return jnp.concatenate([w_query[:, cut], w_key[:, cut], w_value[:, cut]], 1)

    gain_attn, gain_mlp = fetched_lines([gain_attn, gain_mlp])
    weight_parts = fetched([columns(0)])
    if rounds > 1:
        weight_parts += fetched([columns(index) for index in range(1, rounds)])
    spot = jnp.stack([side, core]).astype(jnp.int32)
    if shards == 2:
        first_half, near, far = fetched([after(w_out, weight_parts[-1][0][-1])])[0][0]
        away = jnp.where(
            core == 0, jnp.concatenate([near, far], 1), jnp.concatenate([far, near], 1)
        )
        w_out = jnp.where(
            side == 0, jnp.concatenate([first_half, away]), jnp.concatenate([away, first_half])
        )
    else:
        w_out = gathered(w_out)
    w_gate, w_up, w_down = (
        gathered(after(shard, weight_parts[-1][0][-1])) for shard in (w_gate, w_up, w_down)
    )
    lengths = doc_lengths[:, 0]
    doc_ends = jnp.cumsum(lengths, -1)
    starts = (doc_ends - lengths).astype(jnp.int32)

    def begins_of(micro_starts, positions):
        reached = positions[:, None] >= micro_starts[None, :]
        return jnp.max(jnp.where(reached, micro_starts[None, :], 0), -1)

    lane = jnp.arange(LANES)
    inverse = jnp.power(10000.0, -(lane % (HEAD_DIM // 2)).astype(F32) / (HEAD_DIM // 2))
    sign = jnp.where((lane % HEAD_DIM) < HEAD_DIM // 2, -1.0, 1.0)
    positions = place * rows + jnp.arange(rows, dtype=jnp.int32)
    offsets = jnp.concatenate(
        [positions - begins_of(starts[micro], positions) for micro in range(micros)]
    ).astype(F32)
    angles = offsets[:, None] * inverse[None, :]
    cos_table, sine_table = jnp.cos(angles), jnp.sin(angles) * sign

    def exchange(buffer):
        return lax.all_to_all(buffer, "ctx", split_axis=0, concat_axis=0, tiled=True)

    tokens = tokens.reshape(micros * rows, width)
    cotangent = cotangent.reshape(micros * rows, width)
    inputs = tokens.astype(F32)
    recip = lax.rsqrt(jnp.mean(inputs * inputs, -1, keepdims=True) + EPS)
    normed = (inputs * recip * gain_attn.astype(F32)).astype(BF16)

    block = jnp.arange(devices, dtype=jnp.int32)
    block_first = block * rows + core * half
    chosen = pick(starts, place // 2 // span, 0)
    lowest = begins_of(chosen, block_first) // rows
    inner = jnp.minimum(-(-begins_of(chosen, block_first + half - 1) // rows), block)

    received, infos, others, attended_back, kept, in_weights = [], [], [], [], [], []
    buffers = []
    for index in range(rounds):
        buffer, weight = project(
            span, counts[index], micros, spot, normed, cos_table, sine_table, *weight_parts[index]
        )
        in_weights.append(weight)
        buffers.append(buffer.reshape(devices, depth, LANES))
    for index in range(rounds):
        live = index * span + place // 2 % span < heads
        bounds = jnp.stack([jnp.where(live, lowest, block), jnp.where(live, inner, block)], 1)
        infos.append(jnp.concatenate([core[None], bounds.reshape(-1)]).astype(jnp.int32))
        buffer = buffers[index]
        if index >= 2:
            buffer = after(buffer, kept[index - 2][1])
        received.append(exchange(buffer))
        whole = received[index]
        whole = after(whole, kept[index - 1][1]) if index else after(whole, *buffers[1:])
        others.append(lax.ppermute(whole, "ctx", swap))
        out, lse = attend(infos[index], chosen, received[index], others[index])
        kept.append((out, lse))
    def came_back(pieces):
        joined = pieces[0] if len(pieces) == 1 else jnp.concatenate(pieces, 1)
        joined = exchange(joined)
        return joined.reshape((chips, 2) + joined.shape[1:])

    early = [after(out, received[-1]) for out, _ in kept[:-1]]
    attended_back = ([came_back(early)] if early else []) + [came_back([kept[-1][0]])]

    attended = collect(counts, micros, attended_back)
    result, grad_middle, grad_att, grad_gain_mlp, mid_grads = feed_forward(
        tokens, cotangent, attended, w_out, gain_mlp, w_gate, w_up, w_down
    )
    grads_in = [
        exchange(buffer.reshape((devices,) + buffer.shape[2:]))
        for buffer in spread(span, counts, micros, grad_att)
    ]

    def paired(stay, leave, axis, routes):
        return (stay.astype(F32) + lax.ppermute(leave, axis, routes).astype(F32)).astype(BF16)

    def chip_summed(full, gain=None):
        count, wide = full.shape[0] // (2 * shards), full.shape[1]
        parts = full.reshape(shards, 2, count, wide)
        if gain is not None:
            line = gain.astype(BF16).reshape(shards, 2, 1, -1)
            line = jnp.pad(line, ((0, 0), (0, 0), (0, 63), (0, wide - line.shape[-1])))
            parts = jnp.concatenate([parts, line], 2)
        return paired(pick(parts, core, 1), pick(parts, 1 - core, 1), "ctx", swap)

    def owned(parts):
        if shards == 2:
            return paired(pick(parts, side, 0), pick(parts, 1 - side, 0), "fsdp", cross)
        return lax.psum_scatter(parts, "fsdp", scatter_dimension=0, tiled=False)

    def spaced(part):
        return jnp.where((core == jnp.arange(2))[:, None, None], part[None], 0)

    def totals_of(parts):
        if devices == 16:
            return ctx_sum(parts)
        return list(lax.psum(tuple(spaced(part) for part in parts), "ctx"))

    def gain_of(total):
        count = total.shape[1] - 64
        return total[:, count, : width // (2 * shards)].reshape(-1).astype(F32)

    grad_out, grad_gate, grad_up, grad_down = mid_grads
    chip_down, chip_gate, chip_up = (chip_summed(grad) for grad in (grad_down, grad_gate, grad_up))
    chip_out = chip_summed(grad_out, grad_gain_mlp)
    mid_parts = [owned(chip) for chip in (chip_out, chip_down, chip_gate, chip_up)]

    grad_back, sent_back = [], []
    waits = {0: (chip_out, chip_down, chip_gate, chip_up), 2: tuple(mid_parts)}
    for index in range(rounds):
        own, away = attend_grad(
            infos[index],
            chosen,
            received[index],
            others[index],
            after(
                grads_in[min(index, 1)], *waits.get(index, ()), *sent_back[-1:], *grad_back[-2:-1]
            ),
            max(index - 1, 0),
            *kept[index],
        )
        back = lax.ppermute(away, "ctx", swap)
        buffer = merge(own, back)
        sent_back.append(buffer)
        grad_back.append(exchange(buffer).reshape(chips, 2, depth, LANES))

    grad_back[:-1] = [after(back, sent_back[-1]) for back in grad_back[:-1]]
    grad_normed, parts = 0.0, []
    for index in range(rounds):
        grad_qkv = collect_grad(counts[index], micros, grad_back[index], cos_table, sine_table)
        grad_normed = grad_normed + jnp.einsum(
            "te,de->td", grad_qkv, in_weights[index], preferred_element_type=F32
        )
        final = index == rounds - 1
        if final:
            grad_in, grad_gain = norm_backward(grad_normed, inputs, recip, gain_attn.astype(F32))
        parts.append(owned(chip_summed(outer(normed, grad_qkv), grad_gain if final else None)))
    totals = totals_of(mid_parts + parts)
    mid_totals, last_totals = totals[: len(mid_parts)], totals[len(mid_parts) :]
    grad_inputs = (grad_middle + grad_in).astype(BF16)
    share = width // (2 * shards)
    grad_gain_mlp, grad_gain_attn = gain_of(mid_totals[0]), gain_of(last_totals[-1])
    grad_w_out, grad_w_down, grad_w_gate, grad_w_up, grad_w_query, grad_w_key, grad_w_value = widen(
        mid_totals, last_totals, (share, mid_totals[1].shape[1], share, share, share), width
    )
    shape = (micros, 1, rows, width)
    return (
        result.reshape(shape),
        grad_inputs.reshape(shape),
        grad_gain_attn,
        grad_w_query,
        grad_w_key,
        grad_w_value,
        grad_w_out,
        grad_gain_mlp,
        grad_w_gate,
        grad_w_up,
        grad_w_down,
    )


def solution(mesh):
    weight, gain = P("fsdp", None), P("fsdp")
    rows = P(None, "fsdp", "ctx", None)
    weights = (gain, weight, weight, weight, weight, gain, weight, weight, weight)
    return jax.shard_map(
        body,
        mesh=mesh,
        in_specs=(rows, rows, P(None, "fsdp", None)) + weights,
        out_specs=(rows, rows) + weights,
        check_vma=False,
    )
```

```python
import functools
import math

import jax
import jax.numpy as jnp
from jax import lax
from jax.experimental import pallas as pl
from jax.experimental.pallas import tpu as pltpu
from jax.sharding import PartitionSpec as P

HEAD_DIM = 64
LANES = 128
EPS = 1e-05
NEG = -1e30
LOG2E = math.log2(math.e)
LN2 = math.log(2.0)
F32 = jnp.float32
BF16 = jnp.bfloat16


def dot_nt(left, right):
    return lax.dot_general(left, right, (((1,), (1,)), ((), ())), preferred_element_type=F32)


def dot_nn(left, right):
    return lax.dot_general(left, right, (((1,), (0,)), ((), ())), preferred_element_type=F32)


def dot_tn(left, right):
    return lax.dot_general(left, right, (((0,), (0,)), ((), ())), preferred_element_type=F32)


def lane_index(rows):
    return lax.broadcasted_iota(jnp.int32, (rows, LANES), 1)


def flip(tile):
    return pltpu.roll(tile, HEAD_DIM, 1)


def params(count):
    return pltpu.CompilerParams(
        dimension_semantics=("arbitrary",) * count, vmem_limit_bytes=60 * 1024 * 1024
    )


def full_block(shape):
    zeros = (0,) * len(shape)
    return pl.BlockSpec(shape, lambda *_: zeros)


def pack_pair(tile):
    count = tile.shape[0] // 2
    low = lane_index(count) < HEAD_DIM
    top, bottom = tile[:count], tile[count:]
    return (jnp.where(low, top, flip(bottom)), jnp.where(low, flip(top), bottom))


def unpack_pair(first, second):
    low = lane_index(first.shape[0]) < HEAD_DIM
    top = jnp.where(low, first, flip(second))
    bottom = jnp.where(low, flip(first), second)
    return jnp.concatenate([top, bottom], 0)


def turn(tile):
    near = (lane_index(tile.shape[0]) % HEAD_DIM) < HEAD_DIM // 2
    return jnp.where(
        near, pltpu.roll(tile, LANES - HEAD_DIM // 2, 1), pltpu.roll(tile, HEAD_DIM // 2, 1)
    )


def project_kernel(count, info, n_ref, c_ref, s_ref, *refs):
    *parts, out, w_ref = refs

    @pl.when((pl.program_id(0) == 0) & (pl.program_id(1) == 0))
    def _():
        if len(parts) == 1:
            w_ref[...] = parts[0][...]
            return
        own, near, far = parts
        deep, wide = near.shape
        side, core = info[0], info[1]
        mine = pl.ds(pl.multiple_of(side * deep, deep), deep)
        away = pl.ds(pl.multiple_of((1 - side) * deep, deep), deep)
        w_ref[mine, :] = own[...]
        w_ref[away, pl.ds(pl.multiple_of(core * wide, wide), wide)] = near[...]
        w_ref[away, pl.ds(pl.multiple_of((1 - core) * wide, wide), wide)] = far[...]

    joined = dot_nn(n_ref[...], w_ref[...])
    cos_table, sine_table = c_ref[...], s_ref[...]
    rows = n_ref.shape[0]
    span = count * HEAD_DIM
    low = lane_index(rows) < HEAD_DIM
    for pair in range(count // 2):
        first = pair * LANES
        q2, k2, v2 = (joined[:, part * span + first : part * span + first + LANES] for part in range(3))
        q2 = (q2 * cos_table + turn(q2) * sine_table) * (LOG2E * HEAD_DIM**-0.5)
        k2 = k2 * cos_table + turn(k2) * sine_table
        packed = pack_pair(q2)
        kv = (jnp.where(low, k2, flip(v2)), jnp.where(low, flip(k2), v2))
        for side in range(2):
            out[2 * pair + side, 0, :rows, :] = kv[side].astype(BF16)
            out[2 * pair + side, 0, rows:, :] = packed[side].astype(BF16)
    if count < out.shape[0]:
        out[count:] = jnp.zeros((out.shape[0] - count,) + out.shape[1:], BF16)


def project(span, count, micros, info, normed, cos_table, sine_table, parts, column):
    rows, width = normed.shape
    half = rows // (2 * micros)
    depth = half + half // 2
    wide = parts[0].shape[1]
    return pl.pallas_call(
        functools.partial(project_kernel, count),
        grid_spec=pltpu.PrefetchScalarGridSpec(
            num_scalar_prefetch=1,
            grid=(micros, 2),
            in_specs=[
                pl.BlockSpec((half, width), lambda m, i, *_: (2 * m + i, 0)),
                pl.BlockSpec((half, LANES), lambda m, i, *_: (2 * m + i, 0)),
                pl.BlockSpec((half, LANES), lambda m, i, *_: (2 * m + i, 0)),
            ]
            + [full_block(part.shape) for part in parts[:1]]
            + [
                pl.BlockSpec((part.shape[0], wide // 2), lambda m, i, *_: (0, column))
                for part in parts[1:]
            ],
            out_specs=[
                pl.BlockSpec((span, 1, depth, LANES), lambda m, i, *_: (m, i, 0, 0)),
                full_block((width, wide)),
            ],
        ),
        out_shape=[
            jax.ShapeDtypeStruct((micros * span, 2, depth, LANES), BF16),
            jax.ShapeDtypeStruct((width, wide), BF16),
        ],
        compiler_params=params(2),
        cost_estimate=pl.CostEstimate(
            flops=2 * rows * width * wide, bytes_accessed=4 * rows * width, transcendentals=0
        ),
        name="project",
    )(info, normed, cos_table, sine_table, *parts)


def row_begins(starts_ref, positions):
    begins = jnp.zeros_like(positions)
    for index in range(starts_ref.shape[0]):
        start = starts_ref[index]
        begins = jnp.maximum(begins, jnp.where(positions >= start, start, 0))
    return begins


def unpack_one(packed, lanes_low):
    wide = packed.astype(F32)
    low = lane_index(wide.shape[0]) < HEAD_DIM
    keep = low if lanes_low else jnp.logical_not(low)
    turned = flip(wide)
    first, second = (wide, turned) if lanes_low else (turned, wide)
    return jnp.concatenate(
        [jnp.where(keep, first, 0.0), jnp.where(keep, second, 0.0)], 0
    ).astype(BF16)


def attend_kernel(info, starts, mine, other, o_ref, lse_ref):
    block = pl.program_id(0)
    core = info[0]
    lowest, inner = info[1 + 2 * block], info[2 + 2 * block]
    rows = mine.shape[1] * 2 // 3
    low = lane_index(rows) < HEAD_DIM
    queries = unpack_one(mine[block, rows:, :], True)
    row_pos = (2 * block + core) * rows + lax.broadcasted_iota(jnp.int32, (rows, 1), 0)
    begins = row_begins(starts, row_pos)
    lane_low = lane_index(2 * rows) < HEAD_DIM
    column = lax.broadcasted_iota(jnp.int32, (1, 2 * rows), 1)
    offsets = jnp.where(column < rows, column + core * rows, column - core * rows)

    def keys(index):
        kv = jnp.concatenate([mine[index, :rows, :], other[index, :rows, :]], 0)
        return kv, jnp.where(lane_low, jnp.ones_like(kv), kv)

    def two_steps(index, carry):
        peak, acc = carry
        first, first_v = keys(inner + 2 * index)
        second, second_v = keys(inner + 2 * index + 1)
        scores, more = dot_nt(queries, first), dot_nt(queries, second)
        new_peak = jnp.maximum(peak, jnp.max(jnp.maximum(scores, more), -1, keepdims=True))
        weights, more = jnp.exp2(scores - new_peak), jnp.exp2(more - new_peak)
        acc = acc * jnp.exp2(peak - new_peak) + (
            dot_nn(weights.astype(BF16), first_v) + dot_nn(more.astype(BF16), second_v)
        )
        return (new_peak, acc)

    def step(masked, index, carry):
        peak, acc = carry
        kv, ones_v = keys(index)
        scores = dot_nt(queries, kv)
        if masked:
            key_pos = offsets + index * (2 * rows)
            scores = jnp.where((key_pos >= begins) & (key_pos <= row_pos), scores, NEG)
        new_peak = jnp.maximum(peak, jnp.max(scores, -1, keepdims=True))
        weights = jnp.exp2(scores - new_peak)
        acc = acc * jnp.exp2(peak - new_peak) + dot_nn(weights.astype(BF16), ones_v)
        return (new_peak, acc)

    carry = step(True, block, (jnp.full((rows, 1), NEG, F32), jnp.zeros((rows, LANES), F32)))
    carry = lax.fori_loop(lowest, inner, functools.partial(step, True), carry)
    twice = (block - inner) // 2
    carry = lax.fori_loop(0, twice, two_steps, carry)
    peak, acc = lax.fori_loop(inner + 2 * twice, block, functools.partial(step, False), carry)
    result = acc / flip(acc)
    count = rows // 2
    small_low = lane_index(count) < HEAD_DIM
    o_ref[0] = jnp.where(small_low, flip(result[:count]), result[count:]).astype(BF16)
    lse = jnp.where(low, peak + jnp.log2(acc), 0.0)
    lse_ref[0] = jnp.transpose(lse)[0:1, :]


def attend(info, starts, mine, other):
    blocks, depth, _ = mine.shape
    rows = depth * 2 // 3
    return pl.pallas_call(
        attend_kernel,
        grid_spec=pltpu.PrefetchScalarGridSpec(
            num_scalar_prefetch=2,
            grid=(blocks,),
            in_specs=[
                pl.BlockSpec(mine.shape, lambda i, *_: (0, 0, 0)),
                pl.BlockSpec(other.shape, lambda i, *_: (0, 0, 0)),
            ],
            out_specs=[
                pl.BlockSpec((1, rows // 2, LANES), lambda i, *_: (i, 0, 0)),
                pl.BlockSpec((1, 1, rows), lambda i, *_: (i, 0, 0)),
            ],
        ),
        out_shape=[
            jax.ShapeDtypeStruct((blocks, rows // 2, LANES), BF16),
            jax.ShapeDtypeStruct((blocks, 1, rows), F32),
        ],
        compiler_params=params(1),
        cost_estimate=pl.CostEstimate(
            flops=16 * 10**9, bytes_accessed=10**7, transcendentals=10**7
        ),
        name="attend",
    )(info, starts, mine, other)


def attend_grad_kernel(
    info, starts, mine, other, do_ref, o_ref, lse_ref, dm_ref, dp_ref, acc_mine, acc_other
):
    block = pl.program_id(0)
    core = info[0]
    lowest, inner = info[1 + 2 * block], info[2 + 2 * block]
    rows = mine.shape[1] * 2 // 3
    count = rows // 2

    @pl.when(block == 0)
    def _():
        acc_mine[...] = jnp.zeros_like(acc_mine)
        acc_other[...] = jnp.zeros_like(acc_other)

    queries = unpack_one(mine[block, rows:, :], True)
    grad_out = unpack_one(do_ref[0], False)
    both = jnp.concatenate([queries, grad_out], 0)
    product = jnp.transpose(do_ref[0].astype(F32) * o_ref[0].astype(F32))
    delta = jnp.concatenate(
        [
            jnp.sum(product[:HEAD_DIM], 0, keepdims=True),
            jnp.sum(product[HEAD_DIM:], 0, keepdims=True),
        ],
        1,
    )
    lse = lse_ref[0]
    row_pos = (2 * block + core) * rows + lax.broadcasted_iota(jnp.int32, (1, rows), 1)
    begins = row_begins(starts, row_pos)
    line = lax.broadcasted_iota(jnp.int32, (2 * rows, 1), 0)
    offsets = jnp.where(line < rows, line + core * rows, line - core * rows)

    def step(masked, index, grad_q):
        kv = jnp.concatenate([mine[index, :rows, :], other[index, :rows, :]], 0)
        scores = dot_nt(kv, queries)
        weights = jnp.exp2(scores - lse)
        if masked:
            key_pos = offsets + index * (2 * rows)
            weights = jnp.where((key_pos >= begins) & (key_pos <= row_pos), weights, 0.0)
        grad_weights = dot_nt(kv, grad_out)
        grad_scores = (weights * (grad_weights - delta)).astype(BF16)
        grad_kv = dot_nn(jnp.concatenate([grad_scores, weights.astype(BF16)], 1), both)
        acc_mine[index] += grad_kv[:rows]
        acc_other[index] += grad_kv[rows:]
        return grad_q + dot_tn(grad_scores, kv)

    grad_q = step(True, block, jnp.zeros((rows, LANES), F32))
    grad_q = lax.fori_loop(lowest, inner, functools.partial(step, True), grad_q)
    twice = (block - inner) // 2

    def two_steps(index, grad_q):
        grad_q = step(False, inner + 2 * index, grad_q)
        return step(False, inner + 2 * index + 1, grad_q)

    grad_q = lax.fori_loop(0, twice, two_steps, grad_q)
    grad_q = lax.fori_loop(inner + 2 * twice, block, functools.partial(step, False), grad_q)
    grad_q = grad_q * HEAD_DIM**-0.5
    small_low = lane_index(count) < HEAD_DIM
    dm_ref[block, rows:, :] = jnp.where(small_low, grad_q[:count], flip(grad_q[count:])).astype(
        BF16
    )

    @pl.when(block == pl.num_programs(0) - 1)
    def _():
        scale = jnp.where(lane_index(rows) < HEAD_DIM, LN2, 1.0)

        def flush(index, _):
            dm_ref[index, :rows, :] = (acc_mine[index] * scale).astype(BF16)
            dp_ref[index] = (acc_other[index] * scale).astype(BF16)
            return 0

        lax.fori_loop(0, mine.shape[0], flush, 0)


def attend_grad(info, starts, mine, other, grad_out, spot, out, lse):
    blocks, depth, _ = mine.shape
    rows = depth * 2 // 3
    whole = pl.BlockSpec(mine.shape, lambda i, *_: (0, 0, 0))
    small = pl.BlockSpec((1, rows // 2, LANES), lambda i, *_: (i, 0, 0))
    return pl.pallas_call(
        attend_grad_kernel,
        grid_spec=pltpu.PrefetchScalarGridSpec(
            num_scalar_prefetch=2,
            grid=(blocks,),
            in_specs=[
                whole,
                whole,
                pl.BlockSpec((1, rows // 2, LANES), lambda i, *_: (i, spot, 0)),
                small,
                pl.BlockSpec((1, 1, rows), lambda i, *_: (i, 0, 0)),
            ],
            out_specs=[whole, pl.BlockSpec((blocks, rows, LANES), lambda i, *_: (0, 0, 0))],
            scratch_shapes=[
                pltpu.VMEM((blocks, rows, LANES), F32),
                pltpu.VMEM((blocks, rows, LANES), F32),
            ],
        ),
        out_shape=[
            jax.ShapeDtypeStruct(mine.shape, BF16),
            jax.ShapeDtypeStruct((blocks, rows, LANES), BF16),
        ],
        compiler_params=params(1),
        cost_estimate=pl.CostEstimate(
            flops=32 * 10**9, bytes_accessed=10**7, transcendentals=10**7
        ),
        name="attend_grad",
    )(info, starts, mine, other, grad_out, out, lse)


def merge_kernel(own_ref, back_ref, out):
    rows = back_ref.shape[1]
    out[:, :rows, :] = (own_ref[:, :rows, :].astype(F32) + back_ref[...].astype(F32)).astype(BF16)
    out[:, rows:, :] = own_ref[:, rows:, :]


def merge(own, back):
    blocks, depth, _ = own.shape
    step = blocks // 4
    spec = pl.BlockSpec((step, depth, LANES), lambda i: (i, 0, 0))
    return pl.pallas_call(
        merge_kernel,
        grid=(4,),
        in_specs=[spec, pl.BlockSpec((step, back.shape[1], LANES), lambda i: (i, 0, 0))],
        out_specs=spec,
        out_shape=jax.ShapeDtypeStruct(own.shape, BF16),
        compiler_params=params(1),
        cost_estimate=pl.CostEstimate(flops=0, bytes_accessed=4 * 10**6, transcendentals=0),
        name="merge",
    )(own, back)


def collect_kernel(counts, *refs):
    ins, out = refs[:-1], refs[-1]
    length = out.shape[0] // 2
    pieces = [(array, first) for array in ins for first in range(0, array.shape[2], length)]
    pair = 0
    for (array, first), count in zip(pieces, counts):
        cut = slice(first, first + length)
        for spot in range(0, count, 2):
            tiles = [array[spot + side, 0, cut, :].astype(F32) for side in range(2)]
            out[:, pair * LANES : (pair + 1) * LANES] = unpack_pair(*tiles).astype(BF16)
            pair += 1


def collect(counts, micros, arrays):
    units = arrays[0].shape[0]
    length = sum(array.shape[2] for array in arrays) // len(counts)
    width = sum(counts) * HEAD_DIM
    return pl.pallas_call(
        functools.partial(collect_kernel, counts),
        grid=(micros, 2),
        in_specs=[
            pl.BlockSpec((units // micros, 1, array.shape[2], LANES), lambda m, i: (m, i, 0, 0))
            for array in arrays
        ],
        out_specs=pl.BlockSpec((2 * length, width), lambda m, i: (2 * m + i, 0)),
        out_shape=jax.ShapeDtypeStruct((micros * 4 * length, width), BF16),
        compiler_params=params(2),
        cost_estimate=pl.CostEstimate(flops=0, bytes_accessed=4 * 10**6, transcendentals=0),
        name="collect",
    )(*arrays)


def spread_kernel(counts, x_ref, *outs):
    length = x_ref.shape[0] // 2
    pieces = [(out, first) for out in outs for first in range(0, out.shape[2], length)]
    pair = 0
    for (out, first), count in zip(pieces, counts):
        cut = slice(first, first + length)
        for spot in range(0, count, 2):
            tile = x_ref[:, pair * LANES : (pair + 1) * LANES].astype(F32)
            packed = pack_pair(tile)
            for side in range(2):
                out[spot + side, 0, cut, :] = packed[side].astype(BF16)
            pair += 1
        for spot in range(count, out.shape[0]):
            out[spot, 0, cut, :] = jnp.zeros((length, LANES), BF16)


def spread(span, counts, micros, rows_array):
    rows, width = rows_array.shape
    half = rows // (2 * micros)
    lengths = [half // 2] + ([half // 2 * (len(counts) - 1)] if len(counts) > 1 else [])
    return pl.pallas_call(
        functools.partial(spread_kernel, counts),
        grid=(micros, 2),
        in_specs=[pl.BlockSpec((half, width), lambda m, i: (2 * m + i, 0))],
        out_specs=[
            pl.BlockSpec((span, 1, length, LANES), lambda m, i: (m, i, 0, 0)) for length in lengths
        ],
        out_shape=[
            jax.ShapeDtypeStruct((micros * span, 2, length, LANES), BF16) for length in lengths
        ],
        compiler_params=params(2),
        cost_estimate=pl.CostEstimate(flops=0, bytes_accessed=4 * 10**6, transcendentals=0),
        name="spread",
    )(rows_array)


def turn_back(tile, cos_table, sine_table):
    near = (lane_index(tile.shape[0]) % HEAD_DIM) < HEAD_DIM // 2
    scaled = tile * sine_table
    moved = jnp.where(
        near,
        pltpu.roll(scaled, LANES - HEAD_DIM // 2, 1),
        pltpu.roll(scaled, HEAD_DIM // 2, 1),
    )
    return tile * cos_table + moved


def collect_grad_kernel(count, c_ref, s_ref, in_ref, out):
    cos_table, sine_table = c_ref[...], s_ref[...]
    rows = cos_table.shape[0]
    span = count * HEAD_DIM
    low = lane_index(rows) < HEAD_DIM
    for pair in range(count // 2):
        kvs = [in_ref[2 * pair + side, 0, :rows, :].astype(F32) for side in range(2)]
        packed = [in_ref[2 * pair + side, 0, rows:, :].astype(F32) for side in range(2)]
        grad_k = jnp.where(low, kvs[0], flip(kvs[1]))
        grad_v = jnp.where(low, flip(kvs[0]), kvs[1])
        grad_q = turn_back(unpack_pair(*packed), cos_table, sine_table)
        grad_k = turn_back(grad_k, cos_table, sine_table)
        for part, value in enumerate((grad_q, grad_k, grad_v)):
            first = part * span + pair * LANES
            out[:, first : first + LANES] = value.astype(BF16)


def collect_grad(count, micros, array, cos_table, sine_table):
    units, _, depth, _ = array.shape
    half = depth * 2 // 3
    width = 3 * count * HEAD_DIM
    table = pl.BlockSpec((half, LANES), lambda m, i: (2 * m + i, 0))
    return pl.pallas_call(
        functools.partial(collect_grad_kernel, count),
        grid=(micros, 2),
        in_specs=[
            table,
            table,
            pl.BlockSpec((units // micros, 1, depth, LANES), lambda m, i: (m, i, 0, 0)),
        ],
        out_specs=pl.BlockSpec((half, width), lambda m, i: (2 * m + i, 0)),
        out_shape=jax.ShapeDtypeStruct((micros * 2 * half, width), BF16),
        compiler_params=params(2),
        cost_estimate=pl.CostEstimate(flops=0, bytes_accessed=6 * 10**6, transcendentals=0),
        name="collect_grad",
    )(cos_table, sine_table, array)


SUM_STEPS = 6
PLANE_Z, PLANE_Y, FAR_Z, TWIN = 4, 2, 8, 1


def add_rows(out, left, right):
    def step(index, _):
        cut = pl.ds(pl.multiple_of(index * 16, 16), 16)
        out[cut, :] = (left[cut, :].astype(F32) + right[cut, :].astype(F32)).astype(BF16)
        return 0

    lax.fori_loop(0, out.shape[0] // 16, step, 0)


def ctx_sum_kernel(count, *refs):
    ins, outs = refs[:count], refs[count : 2 * count]
    halves, quarters, sums, fars = (refs[(2 + k) * count : (3 + k) * count] for k in range(4))
    send_sems, recv_sems = refs[6 * count :]
    place = lax.axis_index("ctx")
    side = lax.axis_index("fsdp")

    def bit(weight):
        return place // weight % 2

    def partner(weight):
        return (place + weight * (1 - 2 * bit(weight)), side)

    barrier = pltpu.get_barrier_semaphore()
    for weight in (PLANE_Z, PLANE_Y, FAR_Z, TWIN):
        pl.semaphore_signal(
            barrier, inc=1, device_id=partner(weight), device_id_type=pl.DeviceIdType.MESH
        )
    pl.semaphore_wait(barrier, 4)

    def send(index, step, source, target, weight):
        copy = pltpu.make_async_remote_copy(
            src_ref=source,
            dst_ref=target,
            send_sem=send_sems.at[index, step],
            recv_sem=recv_sems.at[index, step],
            device_id=partner(weight),
            device_id_type=pl.DeviceIdType.MESH,
        )
        copy.start()
        return copy

    axes = [(PLANE_Z, PLANE_Y) if index % 4 == 2 else (PLANE_Y, PLANE_Z) for index in range(count)]
    core = bit(TWIN)
    started, copies = {}, []

    def stage(index, step):
        first, second = axes[index]
        if step:
            started[index].wait_recv()
        if step == 0:
            leave = ins[index].at[pl.ds(2 * (1 - bit(first)), 2)]
            target, weight = halves[index], first
        elif step == 1:
            for part in range(2):
                half = halves[index].at[part]
                add_rows(half, ins[index].at[2 * bit(first) + part], half)
            leave, target, weight = halves[index].at[1 - bit(second)], quarters[index], second
        elif step == 2:
            add_rows(sums[index], halves[index].at[bit(second)], quarters[index])
            leave, target, weight = sums[index], fars[index], FAR_Z
        elif step == 3:
            leave = target = outs[index].at[core, 2 * bit(first) + bit(second)]
            weight = second
            add_rows(leave, sums[index], fars[index])
        elif step == 4:
            leave = target = outs[index].at[core, pl.ds(2 * bit(first), 2)]
            weight = first
        elif step == 5:
            leave = target = outs[index].at[core]
            weight = TWIN
        if step < SUM_STEPS:
            started[index] = send(index, step, leave, target, weight)
            copies.append(started[index])

    for time in range(count + SUM_STEPS + 1):
        if time < count:
            stage(time, 0)
        for step in reversed(range(1, SUM_STEPS + 1)):
            if 0 <= time - step - 1 < count:
                stage(time - step - 1, step)
    for copy in copies:
        copy.wait_send()


def ctx_sum(parts):
    count = len(parts)
    shapes = [(part.shape[0] // 4, part.shape[1]) for part in parts]
    sent = sum(6 * part.size for part in parts)
    vmem = pl.BlockSpec(memory_space=pltpu.VMEM)
    totals = pl.pallas_call(
        functools.partial(ctx_sum_kernel, count),
        in_specs=[vmem] * count,
        out_specs=[vmem] * count,
        out_shape=[jax.ShapeDtypeStruct((2, 4) + shape, BF16) for shape in shapes],
        scratch_shapes=[pltpu.VMEM((2,) + shape, BF16) for shape in shapes]
        + [pltpu.VMEM(shape, BF16) for shape in shapes] * 3
        + [pltpu.SemaphoreType.DMA((count, SUM_STEPS))] * 2,
        compiler_params=pltpu.CompilerParams(
            collective_id=0, has_side_effects=True, vmem_limit_bytes=60 * 1024 * 1024
        ),
        cost_estimate=pl.CostEstimate(flops=0, bytes_accessed=4 * sent, transcendentals=0),
        name="ctx_sum",
    )(*[part.reshape((4,) + shape) for part, shape in zip(parts, shapes)])
    return [total.reshape((2,) + part.shape) for total, part in zip(totals, parts)]


def matmul(left, right):
    return jnp.dot(left, right, preferred_element_type=F32)


def norm_backward(grad_out, values, recip_rows, gain):
    scaled = grad_out * gain
    grad_in = recip_rows * scaled - values * (recip_rows * recip_rows * recip_rows) * jnp.mean(
        scaled * values, -1, keepdims=True
    )
    return (grad_in, jnp.sum(grad_out * values * recip_rows, 0))


def mlp_kernel(
    n_ref, nt_ref, cot_ref, mid_ref, wg_ref, wu_ref, wd_ref, out, gn_out, gwg_out, gwu_out, gwd_out, acc
):
    index = pl.program_id(0)

    @pl.when(index == 0)
    def _():
        acc[...] = mid_ref[...]
        gn_out[...] = jnp.zeros_like(gn_out)

    gate_pre = dot_nn(n_ref[...], wg_ref[...])
    up_pre = dot_nn(n_ref[...], wu_ref[...])
    grad_hidden = dot_nt(cot_ref[...], wd_ref[...])
    gate_sigmoid = 1.0 / (1.0 + jnp.exp(-gate_pre))
    silu_value = gate_pre * gate_sigmoid
    hidden_low = (silu_value * up_pre).astype(BF16)
    grad_gate = (
        grad_hidden * up_pre * gate_sigmoid * (1.0 + gate_pre * (1.0 - gate_sigmoid))
    ).astype(BF16)
    grad_up = (grad_hidden * silu_value).astype(BF16)
    acc[...] += dot_nn(hidden_low, wd_ref[...])
    gn_out[...] += dot_nt(grad_gate, wg_ref[...]) + dot_nt(grad_up, wu_ref[...])
    gwg_out[...] = dot_nn(nt_ref[...], grad_gate).astype(BF16)
    gwu_out[...] = dot_nn(nt_ref[...], grad_up).astype(BF16)
    gwd_out[...] = dot_tn(hidden_low, cot_ref[...]).astype(BF16)

    @pl.when(index == pl.num_programs(0) - 1)
    def _():
        out[...] = acc[...].astype(BF16)


def mlp(normed, cotangent, middle, w_gate, w_up, w_down):
    rows, width = normed.shape
    units = w_gate.shape[1]
    wide = 256
    across = pl.BlockSpec((width, wide), lambda j: (0, j))
    down = pl.BlockSpec((wide, width), lambda j: (j, 0))
    whole = full_block((rows, width))
    return pl.pallas_call(
        mlp_kernel,
        grid=(units // wide,),
        in_specs=[whole, full_block((width, rows)), whole, whole, across, across, down],
        out_specs=[whole, whole, across, across, down],
        out_shape=[
            jax.ShapeDtypeStruct((rows, width), BF16),
            jax.ShapeDtypeStruct((rows, width), F32),
            jax.ShapeDtypeStruct((width, units), BF16),
            jax.ShapeDtypeStruct((width, units), BF16),
            jax.ShapeDtypeStruct((units, width), BF16),
        ],
        scratch_shapes=[pltpu.VMEM((rows, width), F32)],
        compiler_params=params(1),
        cost_estimate=pl.CostEstimate(
            flops=18 * rows * width * units, bytes_accessed=12 * width * units, transcendentals=0
        ),
        name="mlp",
    )(normed, normed.T, cotangent, middle, w_gate, w_up, w_down)


def feed_forward(tokens, cotangent, attended, w_out, gain_mlp, w_gate, w_up, w_down):
    inputs = tokens.astype(F32)
    gain = gain_mlp.astype(F32)
    middle = inputs + matmul(attended, w_out)
    recip = lax.rsqrt(jnp.mean(middle * middle, -1, keepdims=True) + EPS)
    mlp_low = (middle * recip * gain).astype(BF16)
    result, grad_normed, *grads = mlp(mlp_low, cotangent, middle, w_gate, w_up, w_down)
    grad_mid, grad_gain = norm_backward(grad_normed, middle, recip, gain)
    grad_middle = cotangent.astype(F32) + grad_mid
    grad_branch = grad_middle.astype(BF16)
    grad_att = jnp.einsum("te,de->td", grad_branch, w_out, preferred_element_type=F32).astype(BF16)
    return result, grad_middle, grad_att, grad_gain, [outer(attended, grad_branch), *grads]


def widen_kernel(mids, *refs):
    ins, outs = refs[: len(refs) - mids - 3], refs[len(refs) - mids - 3 :]
    for source, out in zip(ins[:mids], outs[:mids]):
        out[...] = source[0, : out.shape[0], :].astype(F32)
    first = 0
    for source in ins[mids:]:
        wide = source.shape[2] // 3
        for which in range(3):
            out = outs[mids + which]
            piece = source[0, : out.shape[0], which * wide : (which + 1) * wide]
            out[:, first : first + wide] = piece.astype(F32)
        first += wide


def widen(mid_totals, round_totals, counts, width):
    totals = [*mid_totals, *round_totals]
    shapes = [(count, total.shape[2]) for count, total in zip(counts, mid_totals)]
    shapes += [(counts[-1], width)] * 3
    return pl.pallas_call(
        functools.partial(widen_kernel, len(mid_totals)),
        grid=(2,),
        in_specs=[pl.BlockSpec((1,) + total.shape[1:], lambda i: (i, 0, 0)) for total in totals],
        out_specs=[pl.BlockSpec(shape, lambda i: (i, 0)) for shape in shapes],
        out_shape=[jax.ShapeDtypeStruct((2 * rows, wide), F32) for rows, wide in shapes],
        compiler_params=params(1),
        cost_estimate=pl.CostEstimate(flops=0, bytes_accessed=2 * 10**7, transcendentals=0),
        name="widen",
    )(*totals)


def outer(left, right):
    return jnp.einsum("td,te->de", left, right, preferred_element_type=F32).astype(BF16)


def after(value, *others):
    return lax.optimization_barrier((value,) + others)[0]


def body(
    tokens, cotangent, doc_lengths, gain_attn, w_query, w_key, w_value, w_out, gain_mlp, w_gate, w_up, w_down
):
    micros, _, rows, width = tokens.shape
    heads = width // HEAD_DIM
    devices = lax.axis_size("ctx")
    shards = lax.axis_size("fsdp")
    place = lax.axis_index("ctx")
    side = lax.axis_index("fsdp")
    chips = devices // 2
    core = place % 2
    half = rows // 2
    depth = half + half // 2
    span = chips // micros
    rounds = -(-heads // span)
    counts = tuple(min(span, heads - index * span) for index in range(rounds))
    swap = [(i, i ^ 1) for i in range(devices)]
    cross = [(0, 1), (1, 0)]

    def pick(array, index, axis):
        return lax.dynamic_index_in_dim(array, index, axis, keepdims=False)

    def gathered(shard):
        return lax.all_gather(shard, "fsdp", axis=0, tiled=True)

    def fetched(pieces):
        if shards != 2:
            return [([gathered(piece)], 0) for piece in pieces]
        nears = []
        for piece in pieces:
            wide = piece.shape[1] // 2
            nears.append(lax.dynamic_slice_in_dim(piece, core * wide, wide, 1))
        near = nears[0] if len(nears) == 1 else jnp.concatenate(nears, 1)
        near = lax.ppermute(near, "fsdp", cross)
        far = lax.ppermute(near, "ctx", swap)
        return [([piece, near, far], index) for index, piece in enumerate(pieces)]

    def fetched_lines(lines):
        if shards != 2:
            return [gathered(line) for line in lines]
        lines = jnp.stack(lines)
        away = lax.ppermute(lines, "fsdp", cross)
        return jnp.where(
            side == 0, jnp.concatenate([lines, away], 1), jnp.concatenate([away, lines], 1)
        )

    def columns(index):
        cut = slice(index * span * HEAD_DIM, (index * span + counts[index]) * HEAD_DIM)
        return jnp.concatenate([w_query[:, cut], w_key[:, cut], w_value[:, cut]], 1)

    gain_attn, gain_mlp = fetched_lines([gain_attn, gain_mlp])
    weight_parts = fetched([columns(0)])
    if rounds > 1:
        weight_parts += fetched([columns(index) for index in range(1, rounds)])
    spot = jnp.stack([side, core]).astype(jnp.int32)
    far = weight_parts[-1][0][-1]
    if shards == 2:
        far = lax.ppermute(after(w_out, far), "fsdp", cross)
        w_out = jnp.where(
            side == 0, jnp.concatenate([w_out, far]), jnp.concatenate([far, w_out])
        )
    else:
        w_out = gathered(w_out)
    w_gate, w_up, w_down = (
        gathered(after(shard, weight_parts[-1][0][-1])) for shard in (w_gate, w_up, w_down)
    )
    lengths = doc_lengths[:, 0]
    doc_ends = jnp.cumsum(lengths, -1)
    starts = (doc_ends - lengths).astype(jnp.int32)

    def begins_of(micro_starts, positions):
        reached = positions[:, None] >= micro_starts[None, :]
        return jnp.max(jnp.where(reached, micro_starts[None, :], 0), -1)

    lane = jnp.arange(LANES)
    inverse = jnp.power(10000.0, -(lane % (HEAD_DIM // 2)).astype(F32) / (HEAD_DIM // 2))
    sign = jnp.where((lane % HEAD_DIM) < HEAD_DIM // 2, -1.0, 1.0)
    positions = place * rows + jnp.arange(rows, dtype=jnp.int32)
    offsets = jnp.concatenate(
        [positions - begins_of(starts[micro], positions) for micro in range(micros)]
    ).astype(F32)
    angles = offsets[:, None] * inverse[None, :]
    cos_table, sine_table = jnp.cos(angles), jnp.sin(angles) * sign

    def exchange(buffer):
        return lax.all_to_all(buffer, "ctx", split_axis=0, concat_axis=0, tiled=True)

    tokens = tokens.reshape(micros * rows, width)
    cotangent = cotangent.reshape(micros * rows, width)
    inputs = tokens.astype(F32)
    recip = lax.rsqrt(jnp.mean(inputs * inputs, -1, keepdims=True) + EPS)
    normed = (inputs * recip * gain_attn.astype(F32)).astype(BF16)

    block = jnp.arange(devices, dtype=jnp.int32)
    block_first = block * rows + core * half
    chosen = pick(starts, place // 2 // span, 0)
    lowest = begins_of(chosen, block_first) // rows
    inner = jnp.minimum(-(-begins_of(chosen, block_first + half - 1) // rows), block)

    received, infos, others, attended_back, kept, in_weights = [], [], [], [], [], []
    buffers = []
    for index in range(rounds):
        buffer, weight = project(
            span, counts[index], micros, spot, normed, cos_table, sine_table, *weight_parts[index]
        )
        in_weights.append(weight)
        buffers.append(buffer.reshape(devices, depth, LANES))
    for index in range(rounds):
        live = index * span + place // 2 % span < heads
        bounds = jnp.stack([jnp.where(live, lowest, block), jnp.where(live, inner, block)], 1)
        infos.append(jnp.concatenate([core[None], bounds.reshape(-1)]).astype(jnp.int32))
        buffer = buffers[index]
        if index >= 2:
            buffer = after(buffer, kept[index - 2][1])
        received.append(exchange(buffer))
        whole = received[index]
        whole = after(whole, kept[index - 1][1], far) if index else after(whole, *buffers[1:])
        others.append(lax.ppermute(whole, "ctx", swap))
        out, lse = attend(infos[index], chosen, received[index], others[index])
        kept.append((out, lse))
    def came_back(pieces):
        joined = pieces[0] if len(pieces) == 1 else jnp.concatenate(pieces, 1)
        joined = exchange(joined)
        return joined.reshape((chips, 2) + joined.shape[1:])

    early = [after(out, received[-1]) for out, _ in kept[:-1]]
    attended_back = ([came_back(early)] if early else []) + [came_back([kept[-1][0]])]

    attended = collect(counts, micros, attended_back)
    result, grad_middle, grad_att, grad_gain_mlp, mid_grads = feed_forward(
        tokens, cotangent, attended, w_out, gain_mlp, w_gate, w_up, w_down
    )
    grads_in = [
        exchange(buffer.reshape((devices,) + buffer.shape[2:]))
        for buffer in spread(span, counts, micros, grad_att)
    ]

    def paired(stay, leave, axis, routes):
        return (stay.astype(F32) + lax.ppermute(leave, axis, routes).astype(F32)).astype(BF16)

    def chip_summed(full, gain=None):
        count, wide = full.shape[0] // (2 * shards), full.shape[1]
        parts = full.reshape(shards, 2, count, wide)
        if gain is not None:
            line = gain.astype(BF16).reshape(shards, 2, 1, -1)
            line = jnp.pad(line, ((0, 0), (0, 0), (0, 63), (0, wide - line.shape[-1])))
            parts = jnp.concatenate([parts, line], 2)
        return paired(pick(parts, core, 1), pick(parts, 1 - core, 1), "ctx", swap)

    def owned(parts):
        if shards == 2:
            return paired(pick(parts, side, 0), pick(parts, 1 - side, 0), "fsdp", cross)
        return lax.psum_scatter(parts, "fsdp", scatter_dimension=0, tiled=False)

    def spaced(part):
        return jnp.where((core == jnp.arange(2))[:, None, None], part[None], 0)

    def totals_of(parts):
        if devices == 16:
            return ctx_sum(parts)
        return list(lax.psum(tuple(spaced(part) for part in parts), "ctx"))

    def gain_of(total):
        count = total.shape[1] - 64
        return total[:, count, : width // (2 * shards)].reshape(-1).astype(F32)

    grad_out, grad_gate, grad_up, grad_down = mid_grads
    chip_down, chip_gate, chip_up = (chip_summed(grad) for grad in (grad_down, grad_gate, grad_up))
    chip_out = chip_summed(grad_out, grad_gain_mlp)
    mid_parts = [owned(chip) for chip in (chip_out, chip_down, chip_gate, chip_up)]

    grad_back, sent_back = [], []
    waits = {0: (chip_out, chip_down, chip_gate, chip_up), 2: tuple(mid_parts)}
    for index in range(rounds):
        own, away = attend_grad(
            infos[index],
            chosen,
            received[index],
            others[index],
            after(
                grads_in[min(index, 1)], *waits.get(index, ()), *sent_back[-1:], *grad_back[-2:-1]
            ),
            max(index - 1, 0),
            *kept[index],
        )
        back = lax.ppermute(away, "ctx", swap)
        buffer = merge(own, back)
        sent_back.append(buffer)
        grad_back.append(exchange(buffer).reshape(chips, 2, depth, LANES))

    grad_back[:-1] = [after(back, sent_back[-1]) for back in grad_back[:-1]]
    grad_normed, parts = 0.0, []
    for index in range(rounds):
        grad_qkv = collect_grad(counts[index], micros, grad_back[index], cos_table, sine_table)
        grad_normed = grad_normed + jnp.einsum(
            "te,de->td", grad_qkv, in_weights[index], preferred_element_type=F32
        )
        final = index == rounds - 1
        if final:
            grad_in, grad_gain = norm_backward(grad_normed, inputs, recip, gain_attn.astype(F32))
        parts.append(owned(chip_summed(outer(normed, grad_qkv), grad_gain if final else None)))
    totals = totals_of(mid_parts + parts)
    mid_totals, last_totals = totals[: len(mid_parts)], totals[len(mid_parts) :]
    grad_inputs = (grad_middle + grad_in).astype(BF16)
    share = width // (2 * shards)
    grad_gain_mlp, grad_gain_attn = gain_of(mid_totals[0]), gain_of(last_totals[-1])
    grad_w_out, grad_w_down, grad_w_gate, grad_w_up, grad_w_query, grad_w_key, grad_w_value = widen(
        mid_totals, last_totals, (share, mid_totals[1].shape[1], share, share, share), width
    )
    shape = (micros, 1, rows, width)
    return (
        result.reshape(shape),
        grad_inputs.reshape(shape),
        grad_gain_attn,
        grad_w_query,
        grad_w_key,
        grad_w_value,
        grad_w_out,
        grad_gain_mlp,
        grad_w_gate,
        grad_w_up,
        grad_w_down,
    )


def solution(mesh):
    weight, gain = P("fsdp", None), P("fsdp")
    rows = P(None, "fsdp", "ctx", None)
    weights = (gain, weight, weight, weight, weight, gain, weight, weight, weight)
    return jax.shard_map(
        body,
        mesh=mesh,
        in_specs=(rows, rows, P(None, "fsdp", None)) + weights,
        out_specs=(rows, rows) + weights,
        check_vma=False,
    )
```
